128 devices in a mesh: src: 32 (over x, z, core), tgt: 4 (over y).
Axes of the slice: x: 4, y: 4, z: 4, core: 2. Of those that a mesh axis runs over, the one named last changes fastest.
Arguments:
- features: bfloat16 [65536, 1024], P('src', 'tgt'), may hold values from -6 to 6
- cites_tiles: bfloat16 [6144, 128, 128], P('src'), may hold values from -0.0546875 to 0.0546875
- cites_targets: int32 [6144], P('src'), may hold values from 0 to 31
- cites_sources: int32 [6144], P('src'), may hold values from 0 to 15
- cites_counts: int32 [32], P('src'), may hold values from 1 to 192, 3072 in all
- writes_tiles: bfloat16 [3072, 128, 128], P('src'), may hold values from -0.078125 to 0.078125
- writes_targets: int32 [3072], P('src'), may hold values from 0 to 31
- writes_sources: int32 [3072], P('src'), may hold values from 0 to 15
- writes_counts: int32 [32], P('src'), may hold values from 1 to 96, 1536 in all
- topic_tiles: bfloat16 [1536, 128, 128], P('src'), may hold values from -0.109375 to 0.109375
- topic_targets: int32 [1536], P('src'), may hold values from 0 to 31
- topic_sources: int32 [1536], P('src'), may hold values from 0 to 15
- topic_counts: int32 [32], P('src'), may hold values from 1 to 48, 768 in all
- owner_map: int32 [32], replicated, may hold values from 0 to 31, each once
- weights: bfloat16 [3, 1024, 1024], P(None, 'tgt'), may hold values from -0.1875 to 0.1875
- bias_row: bfloat16 [1024], P('tgt'), may hold values from -3 to 3
- cotangent: bfloat16 [4096, 1024], P('src', 'tgt'), may hold values from -6 to 6
Outputs:
- mixed_out: bfloat16 [4096, 1024], P('src', 'tgt')
- grad_weight: float32 [3, 1024, 1024], P(None, 'tgt', 'src')
- grad_source: bfloat16 [65536, 1024], P('src', 'tgt')
The draws below stay inside these ranges and needn't reach their ends.
Inputs may be any that keep to these rules, and one draw needn't show every extreme that they name: `cites_targets`: target block of a slot; only live slots are read. `cites_sources`: source block within the slot's own partition. `cites_counts`: live slots come first in each partition's 192 slots; they sum to 3072. `writes_targets`: target block of a slot; only live slots are read. `writes_sources`: source block within the slot's own partition. `writes_counts`: live slots come first in each partition's 96 slots; they sum to 1536. `topic_targets`: target block of a slot; only live slots are read. `topic_sources`: source block within the slot's own partition. `topic_counts`: live slots come first in each partition's 48 slots; they sum to 768. `owner_map`: A permutation of the target blocks.
All inputs are finite; a program needn't handle non-finite values.
Results may differ from the reference program's by a relative error of at most 0.015.
Values may be sent and summed in bfloat16 or wider, within the bound.
No kernel may reach another device: no remote copies, remote signals or barrier semaphores. Data moves between devices by JAX's collectives and lax.ppermute only.
A program may use at most 128 MiB of HBM per device.

```python
import math
import jax
import jax.numpy as jnp
import numpy as np
from jax import lax

D = 1024
TILE = 128
K_CITES = 96
K_WRITES = 48
K_TOPIC = 24
SB_DEV = 16
BLOCKS = 32
CAP_CITES = 192
CAP_WRITES = 96
CAP_TOPIC = 48
CITES_SLOTS = 6144
WRITES_SLOTS = 3072
TOPIC_SLOTS = 1536
TARGETS = 4096
SOURCES = 65536


def with_ends(values, rng, smallest, high):
    spot = [jax.random.randint(jax.random.fold_in(rng, axis), (), 0, length) for axis, length in enumerate(values.shape)]
    main_axis = values.shape.index(max(values.shape))
    beside = spot[:main_axis] + [(spot[main_axis] + 1) % values.shape[main_axis]] + spot[main_axis + 1:]
    return values.at[tuple(spot)].set(smallest).at[tuple(beside)].set(high)


def shard_levels(key, shape, cuts, least, largest):
    level = 1.0
    for position, parts in cuts:
        draws = jax.random.uniform(jax.random.fold_in(jax.random.fold_in(key, 6), position), (parts,), jnp.float32, least / len(cuts), largest / len(cuts))
        level = level * jnp.repeat(jnp.exp(draws), shape[position] // parts).reshape((-1,) + (1,) * (len(shape) - 1 - position))
    return level


def split_up(amount, total, reach, skew):
    loads = [(1 << 20) // math.isqrt(rank ** skew) + 1 for rank in range(2, amount + 1)]
    spare, given = total - reach - (amount - 1), [1] * (amount - 1)
    while spare > 0:
        candidates = [i for i in range(amount - 1) if given[i] < reach]
        mass, budget = sum([loads[i] for i in candidates]), spare
        for i in candidates:
            more = min(reach - given[i], max(1, budget * loads[i] // mass), spare)
            given[i] = given[i] + more
            spare = spare - more
    return np.array([reach] + given)


def ragged_sizes(stream_key, count, total, limit, lean):
    if count == 2:
        one = jax.random.randint(stream_key, (), max(1, total - limit), min(limit, total - 1) + 1)
        return jnp.stack([one, total - one])
    sizes = jnp.asarray(split_up(count, total, limit, lean), jnp.int32)
    twos = (count - 1) // 2
    donor, sink = sizes[1:1 + 2 * twos:2], sizes[2:2 + 2 * twos:2]
    margin = jnp.minimum(donor - 1, limit - sink)
    moved = jax.random.randint(jax.random.fold_in(stream_key, 1), (twos,), 0, 1 << 20) % (margin + 1)
    sizes = sizes.at[1:1 + 2 * twos:2].set(donor - moved).at[2:2 + 2 * twos:2].set(sink + moved)
    return sizes[jax.random.permutation(jax.random.fold_in(stream_key, 2), count)]


def bell_draw(stream_key, dims, width, bound, shards=(), held_as=jnp.bfloat16):
    factor_of = shard_levels(stream_key, dims, shards, -0.22, 0.18) if shards else 1.0
    drawn = jax.random.normal(stream_key, dims, jnp.float32) * width * factor_of
    return jnp.minimum(jnp.maximum(drawn, -bound), bound).astype(held_as)


def setup_inputs(seed: int = 0) -> dict:
    arg_keys = jax.random.split(jax.random.key(seed), 18)
    features = bell_draw(arg_keys[0], (SOURCES, D), 1.0, 6.0, ((0, 32), (1, 4)))
    cites_tiles = bell_draw(arg_keys[1], (CITES_SLOTS, TILE, TILE), (K_CITES * TILE) ** -0.5, 0.0546875, ((0, 32),))
    cites_targets = with_ends(jax.random.randint(arg_keys[2], (CITES_SLOTS,), 0, BLOCKS), jax.random.fold_in(arg_keys[2], 1), 0, BLOCKS - 1).astype(jnp.int32)
    cites_sources = with_ends(jax.random.randint(arg_keys[3], (CITES_SLOTS,), 0, SB_DEV), jax.random.fold_in(arg_keys[3], 1), 0, SB_DEV - 1).astype(jnp.int32)
    cites_counts = ragged_sizes(arg_keys[4], BLOCKS, BLOCKS * K_CITES, CAP_CITES, 2).astype(jnp.int32)
    writes_tiles = bell_draw(arg_keys[5], (WRITES_SLOTS, TILE, TILE), (K_WRITES * TILE) ** -0.5, 0.078125, ((0, 32),))
    writes_targets = with_ends(jax.random.randint(arg_keys[6], (WRITES_SLOTS,), 0, BLOCKS), jax.random.fold_in(arg_keys[6], 1), 0, BLOCKS - 1).astype(jnp.int32)
    writes_sources = with_ends(jax.random.randint(arg_keys[7], (WRITES_SLOTS,), 0, SB_DEV), jax.random.fold_in(arg_keys[7], 1), 0, SB_DEV - 1).astype(jnp.int32)
    writes_counts = ragged_sizes(arg_keys[8], BLOCKS, BLOCKS * K_WRITES, CAP_WRITES, 2).astype(jnp.int32)
    topic_tiles = bell_draw(arg_keys[9], (TOPIC_SLOTS, TILE, TILE), (K_TOPIC * TILE) ** -0.5, 0.109375, ((0, 32),))
    topic_targets = with_ends(jax.random.randint(arg_keys[10], (TOPIC_SLOTS,), 0, BLOCKS), jax.random.fold_in(arg_keys[10], 1), 0, BLOCKS - 1).astype(jnp.int32)
    topic_sources = with_ends(jax.random.randint(arg_keys[11], (TOPIC_SLOTS,), 0, SB_DEV), jax.random.fold_in(arg_keys[11], 1), 0, SB_DEV - 1).astype(jnp.int32)
    topic_counts = ragged_sizes(arg_keys[12], BLOCKS, BLOCKS * K_TOPIC, CAP_TOPIC, 2).astype(jnp.int32)
    owner_map = jax.random.permutation(arg_keys[13], BLOCKS).astype(jnp.int32)
    weights = bell_draw(arg_keys[14], (3, D, D), D ** -0.5, 0.1875, ((1, 4),))
    bias_row = bell_draw(arg_keys[15], (D,), 0.5, 3.0, ((0, 4),))
    cotangent = bell_draw(arg_keys[16], (TARGETS, D), 1.0, 6.0, ((0, 32), (1, 4)))
    return dict(features=features, cites_tiles=cites_tiles, cites_targets=cites_targets, cites_sources=cites_sources, cites_counts=cites_counts, writes_tiles=writes_tiles, writes_targets=writes_targets, writes_sources=writes_sources, writes_counts=writes_counts, topic_tiles=topic_tiles, topic_targets=topic_targets, topic_sources=topic_sources, topic_counts=topic_counts, owner_map=owner_map, weights=weights, bias_row=bias_row, cotangent=cotangent)


def gelu_tanh(values):
    return jax.nn.gelu(values, approximate=True)

def prepare(tile_values, tile_targets, tile_sources, tile_counts, owner_map):
    capacity = tile_values.shape[0] // BLOCKS
    columns = jnp.arange(BLOCKS, dtype=jnp.int32)
    slots = lax.optimization_barrier(jnp.sum(jnp.where(tile_targets[:, None] == owner_map[None, :], columns[None, :], 0), axis=1)).astype(jnp.int32)
    living = jnp.arange(capacity, dtype=jnp.int32)[None, :] < tile_counts[:, None]
    return (tile_values.reshape(BLOCKS, capacity, TILE, TILE), slots.reshape(BLOCKS, capacity), tile_sources.reshape(BLOCKS, capacity), living)

def reference(features, cites_tiles, cites_targets, cites_sources, cites_counts, writes_tiles, writes_targets, writes_sources, writes_counts, topic_tiles, topic_targets, topic_sources, topic_counts, owner_map, weights, bias_row, cotangent):
    source_blocks = features.reshape(BLOCKS, SB_DEV, TILE, D)
    prepared = [prepare(cites_tiles, cites_targets, cites_sources, cites_counts, owner_map), prepare(writes_tiles, writes_targets, writes_sources, writes_counts, owner_map), prepare(topic_tiles, topic_targets, topic_sources, topic_counts, owner_map)]

    def forward_part(totals, partition):
        results = []
        for number in range(3):
            values_all, slots_all, sources_all, living_all = prepared[number]
            picked = jnp.take(source_blocks[partition], sources_all[partition], axis=0).astype(jnp.float32)
            product = jnp.einsum('ctk,ckd->ctd', values_all[partition].astype(jnp.float32), picked, precision=lax.Precision.HIGHEST)
            product = product * living_all[partition].astype(jnp.float32)[:, None, None]
            results.append(totals[number] + jax.ops.segment_sum(product, slots_all[partition], num_segments=BLOCKS))
        return (tuple(results), None)
    start_sums = tuple((jnp.zeros((BLOCKS, TILE, D), jnp.float32) for number in range(3)))
    totals = lax.scan(forward_part, start_sums, jnp.arange(BLOCKS, dtype=jnp.int32))[0]
    rounded = [totals[number].reshape(BLOCKS * TILE, D).astype(jnp.bfloat16) for number in range(3)]
    hidden = jnp.dot(rounded[0], weights[0], preferred_element_type=jnp.float32)
    for number in range(1, 3):
        hidden = hidden + jnp.dot(rounded[number], weights[number], preferred_element_type=jnp.float32)
    hidden = hidden + bias_row.astype(jnp.float32)[None, :]
    mixed_out, pullback = jax.vjp(gelu_tanh, hidden)
    grad_hidden = pullback(cotangent.astype(jnp.float32))[0].astype(jnp.bfloat16)
    grad_weight = jnp.stack([jnp.dot(rounded[number].T, grad_hidden, preferred_element_type=jnp.float32) for number in range(3)])
    messages = [jnp.dot(grad_hidden, weights[number].T, preferred_element_type=jnp.float32).astype(jnp.bfloat16).reshape(BLOCKS, TILE, D) for number in range(3)]

    def backward_part(carry_unused, partition):
        grad_part = jnp.zeros((SB_DEV, TILE, D), jnp.float32)
        for number in range(3):
            values_all, slots_all, sources_all, living_all = prepared[number]
            picked = jnp.take(messages[number], slots_all[partition], axis=0).astype(jnp.float32)
            product = jnp.einsum('ctk,ctd->ckd', values_all[partition].astype(jnp.float32), picked, precision=lax.Precision.HIGHEST)
            product = product * living_all[partition].astype(jnp.float32)[:, None, None]
            grad_part = grad_part + jax.ops.segment_sum(product, sources_all[partition], num_segments=SB_DEV)
        return (carry_unused, grad_part.astype(jnp.bfloat16))
    grad_source = lax.scan(backward_part, jnp.zeros((), jnp.float32), jnp.arange(BLOCKS, dtype=jnp.int32))[1]
    return (mixed_out.astype(jnp.bfloat16), grad_weight, grad_source.reshape(BLOCKS * SB_DEV * TILE, D))
```

```python
import functools

import jax
import jax.numpy as jnp
from jax import lax
from jax.experimental import pallas as pl
from jax.experimental.pallas import tpu as pltpu
from jax.sharding import PartitionSpec as P

TILE = 128
SIDE = 4
GROUP = 8
BF16 = jnp.bfloat16
F32 = jnp.float32
VMEM_LIMIT = 60 * 1024 * 1024


def spec(space):
    return pl.BlockSpec(memory_space=space)


ANY, SMEM, VMEM = pl.ANY, pltpu.SMEM, pltpu.VMEM


def place_of(slot, place_ref):
    x, z, c = slot // 8, (slot // 2) % 4, slot % 2
    dx = (x - place_ref[0] + SIDE) % SIDE
    dz = (z - place_ref[1] + SIDE) % SIDE
    first = jnp.where(c == 0, dx, dz)
    second = jnp.where(c == 0, dz, dx)
    away = jnp.where(c == place_ref[2], 0, 16)
    return first, second, away


def start_tiles(tiles, counts, buffer, sems, bases):
    for number in range(3):
        def start(group, carry, number=number):
            offset = group * GROUP
            pltpu.make_async_copy(
                tiles[number].at[pl.ds(offset, GROUP)],
                buffer.at[pl.ds(bases[number] + offset, GROUP)],
                sems.at[bases[number] // GROUP + group],
            ).start()
            return carry

        lax.fori_loop(0, (counts[number][0] + GROUP - 1) // GROUP, start, 0)


def wait_tiles(tiles, buffer, sems, base, number, group):
    offset = group * GROUP
    pltpu.make_async_copy(
        tiles[number].at[pl.ds(offset, GROUP)],
        buffer.at[pl.ds(base + offset, GROUP)],
        sems.at[base // GROUP + group],
    ).wait()


def gather_kernel(
    place, owner_map,
    targets0, targets1, targets2, sources0, sources1, sources2, counts0, counts1, counts2,
    features, tiles0, tiles1, tiles2,
    keep, send,
    buffer, total, staged, table, tile_sems, out_sems,
):
    targets, sources = (targets0, targets1, targets2), (sources0, sources1, sources2)
    counts, tiles = (counts0, counts1, counts2), (tiles0, tiles1, tiles2)
    capacities = [t.shape[0] for t in tiles]
    bases = [0, capacities[0], capacities[0] + capacities[1]]
    start_tiles(tiles, counts, buffer, tile_sems, bases)

    def fill(slot, carry):
        first, second, away = place_of(slot, place)
        table[owner_map[slot]] = (away + first * SIDE + second) * 3
        return carry

    lax.fori_loop(0, 32, fill, 0)

    def clear(block, carry):
        total[block] = jnp.zeros(total.shape[1:], F32)
        return carry

    lax.fori_loop(0, 96, clear, 0)

    for number in range(3):
        def add_group(group, carry, number=number):
            wait_tiles(tiles, buffer, tile_sems, bases[number], number, group)
            products = []
            for lane in range(GROUP):
                j = group * GROUP + lane
                tile = buffer[bases[number] + j]
                block = features[sources[number][j]]
                products.append(jnp.dot(tile, block, preferred_element_type=F32))
            for lane in range(GROUP):
                j = group * GROUP + lane
                spot = jnp.where(j < counts[number][0], table[targets[number][j]] + number, 96)
                total[spot] += products[lane]
            return carry

        lax.fori_loop(0, (counts[number][0] + GROUP - 1) // GROUP, add_group, 0)

    def out_copy(where, spot):
        target = keep if where == 0 else send
        return pltpu.make_async_copy(
            staged.at[where * 16 + spot], target.at[spot], out_sems.at[where * 16 + spot]
        )

    for where in (1, 0):
        def emit(spot, carry, where=where):
            for number in range(3):
                staged[where * 16 + spot, pl.ds(number * TILE, TILE), :] = total[
                    (where * 16 + spot) * 3 + number
                ].astype(BF16)
            out_copy(where, spot).start()
            return carry

        lax.fori_loop(0, 16, emit, 0)
    for where in (1, 0):
        def finish(spot, carry, where=where):
            out_copy(where, spot).wait()
            return carry

        lax.fori_loop(0, 16, finish, 0)


def gather_sums(place, owner_map, relations, features):
    width = features.shape[-1]
    slots = sum(relation[0].shape[0] for relation in relations)
    blocks = jax.ShapeDtypeStruct((16, 3 * TILE, width), BF16)
    return pl.pallas_call(
        gather_kernel,
        out_shape=(blocks, blocks),
        in_specs=[spec(SMEM)] * 11 + [spec(VMEM)] + [spec(ANY)] * 3,
        out_specs=(spec(ANY), spec(ANY)),
        scratch_shapes=[
            pltpu.VMEM((slots, TILE, TILE), BF16),
            pltpu.VMEM((97, TILE, width), F32),
            pltpu.VMEM((32, 3 * TILE, width), BF16),
            pltpu.SMEM((32,), jnp.int32),
            pltpu.SemaphoreType.DMA((slots // GROUP,)),
            pltpu.SemaphoreType.DMA((32,)),
        ],
        compiler_params=pltpu.CompilerParams(vmem_limit_bytes=VMEM_LIMIT),
        name="gather_sums",
    )(
        place, owner_map,
        *[relation[1] for relation in relations],
        *[relation[2] for relation in relations],
        *[relation[3] for relation in relations],
        features.reshape(-1, TILE, width),
        *[relation[0] for relation in relations],
    )


def spread_kernel(
    place, owner_map,
    targets0, targets1, targets2, sources0, sources1, sources2, counts0, counts1, counts2,
    tiles0, tiles1, tiles2,
    own0, own3, own1, own2a, own2b, sib0, sib3, sib1, sib2a, sib2b,
    out,
    buffer, messages, total, table, tile_sems, in_sems,
):
    targets, sources = (targets0, targets1, targets2), (sources0, sources1, sources2)
    counts, tiles = (counts0, counts1, counts2), (tiles0, tiles1, tiles2)
    capacities = [t.shape[0] for t in tiles]
    bases = [0, capacities[0], capacities[0] + capacities[1]]
    pieces = [
        (own0, 0), (own3, 12), (own1, 4), (own2a, 8), (own2b, 10),
        (sib0, 16), (sib3, 28), (sib1, 20), (sib2a, 24), (sib2b, 26),
    ]
    copies = [
        pltpu.make_async_copy(
            piece, messages.at[pl.ds(at, piece.shape[0])], in_sems.at[number]
        )
        for number, (piece, at) in enumerate(pieces)
    ]
    for copy in copies:
        copy.start()
    start_tiles(tiles, counts, buffer, tile_sems, bases)

    def fill(slot, carry):
        first, second, away = place_of(slot, place)
        table[owner_map[slot]] = away + second * SIDE + first
        return carry

    lax.fori_loop(0, 32, fill, 0)

    def clear(block, carry):
        total[block] = jnp.zeros(total.shape[1:], F32)
        return carry

    lax.fori_loop(0, 16, clear, 0)
    for copy in copies:
        copy.wait()

    width = total.shape[1]
    for number in range(3):
        def add_group(group, carry, number=number):
            wait_tiles(tiles, buffer, tile_sems, bases[number], number, group)
            products = []
            for lane in range(GROUP):
                j = group * GROUP + lane
                tile = buffer[bases[number] + j]
                block = messages[table[targets[number][j]], pl.ds(number * width, width), :]
                products.append(jnp.dot(block, tile, preferred_element_type=F32))
            for lane in range(GROUP):
                j = group * GROUP + lane
                spot = jnp.where(j < counts[number][0], sources[number][j], 16)
                total[spot] += products[lane]
            return carry

        lax.fori_loop(0, (counts[number][0] + GROUP - 1) // GROUP, add_group, 0)

    def emit(block, carry):
        out[block] = total[block].T.astype(BF16)
        return carry

    lax.fori_loop(0, 16, emit, 0)


def spread_sums(place, owner_map, relations, pieces, width):
    slots = sum(relation[0].shape[0] for relation in relations)
    return pl.pallas_call(
        spread_kernel,
        out_shape=jax.ShapeDtypeStruct((16, TILE, width), BF16),
        in_specs=[spec(SMEM)] * 11 + [spec(ANY)] * 13,
        out_specs=spec(VMEM),
        scratch_shapes=[
            pltpu.VMEM((slots, TILE, TILE), BF16),
            pltpu.VMEM((32, 3 * width, TILE), BF16),
            pltpu.VMEM((17, width, TILE), F32),
            pltpu.SMEM((32,), jnp.int32),
            pltpu.SemaphoreType.DMA((slots // GROUP,)),
            pltpu.SemaphoreType.DMA((10,)),
        ],
        compiler_params=pltpu.CompilerParams(vmem_limit_bytes=VMEM_LIMIT),
        name="spread_sums",
    )(
        place, owner_map,
        *[relation[1] for relation in relations],
        *[relation[2] for relation in relations],
        *[relation[3] for relation in relations],
        *[relation[0] for relation in relations],
        *pieces,
    )


def columns_at(place, step, width):
    column = (place[3] + step) % SIDE
    return pl.ds(pl.multiple_of(column * width, width), width)


def hidden_kernel(place, part0, part1, part2, weights, rounded, terms0, terms1, terms2, terms3):
    width = part0.shape[1]
    whole = (part0[...].astype(F32) + part1[...].astype(F32) + part2[...].astype(F32)).astype(BF16)
    rounded[...] = whole
    for step, terms in enumerate((terms0, terms1, terms2, terms3)):
        value = jnp.zeros(terms.shape, F32)
        for number in range(3):
            value += jnp.dot(
                whole[number * TILE:(number + 1) * TILE],
                weights[number, :, columns_at(place, step, width)],
                preferred_element_type=F32,
            )
        terms[...] = value.astype(terms.dtype)


def hidden_terms(place, parts, weights):
    width = parts[0].shape[1]
    return pl.pallas_call(
        hidden_kernel,
        out_shape=(
            jax.ShapeDtypeStruct((3 * TILE, width), BF16),
            jax.ShapeDtypeStruct((TILE, width), F32),
            jax.ShapeDtypeStruct((TILE, width), BF16),
            jax.ShapeDtypeStruct((TILE, width), BF16),
            jax.ShapeDtypeStruct((TILE, width), BF16),
        ),
        in_specs=[spec(SMEM)] + [spec(VMEM)] * 4,
        out_specs=tuple([spec(VMEM)] * 5),
        name="hidden_terms",
    )(place, *parts, weights)


def message_kernel(place, grad0, grad1, grad2, grad3, weights, messages):
    width = grad0.shape[1]
    for number in range(3):
        value = jnp.zeros((width, TILE), F32)
        for step, grad in enumerate((grad0, grad1, grad2, grad3)):
            value += lax.dot_general(
                weights[number, :, columns_at(place, step, width)],
                grad[...],
                (((1,), (1,)), ((), ())),
                preferred_element_type=F32,
            )
        messages[pl.ds(number * width, width), :] = value.astype(BF16)


def form_messages(place, grads, weights):
    width = grads[0].shape[1]
    return pl.pallas_call(
        message_kernel,
        out_shape=jax.ShapeDtypeStruct((3 * width, TILE), BF16),
        in_specs=[spec(SMEM)] + [spec(VMEM)] * 5,
        out_specs=spec(VMEM),
        name="form_messages",
    )(place, *grads, weights)


def weight_kernel(place, grad0, grad1, grad2, grad3, rounded, keep, send):
    width = grad0.shape[1]
    for step, grad in enumerate((grad0, grad1, grad2, grad3)):
        block = (place[3] + step) % SIDE
        for number in range(3):
            value = lax.dot_general(
                grad[...],
                rounded[number * TILE:(number + 1) * TILE, :],
                (((0,), (0,)), ((), ())),
                preferred_element_type=F32,
            ).astype(BF16)
            columns = pl.ds(number * width, width)
            for part in range(8):
                first, second, away = place_of(block * 8 + part, place)
                spot = first * SIDE + second
                piece = value[part * 32:(part + 1) * 32]

                @pl.when(away == 0)
                def _():
                    keep[spot, :, columns] = piece

                @pl.when(away != 0)
                def _():
                    send[spot, :, columns] = piece


def weight_terms(place, grads, rounded):
    width = grads[0].shape[1]
    blocks = jax.ShapeDtypeStruct((16, 32, 3 * width), BF16)
    return pl.pallas_call(
        weight_kernel,
        out_shape=(blocks, blocks),
        in_specs=[spec(SMEM)] + [spec(VMEM)] * 5,
        out_specs=(spec(VMEM), spec(VMEM)),
        name="weight_terms",
    )(place, *grads, rounded)


def shift_pairs(step, second):
    pairs = []
    for s in range(32):
        x, z, c = s // 8, (s // 2) % 4, s % 2
        if (c == 0) != second:
            x = (x + step) % SIDE
        else:
            z = (z + step) % SIDE
        pairs.append((s, (x * SIDE + z) * 2 + c))
    return pairs


def shift(value, step, second=False):
    return lax.ppermute(value, "src", shift_pairs(step, second))


def swap(value):
    return lax.ppermute(value, "src", [(s, s ^ 1) for s in range(32)])


def add(*values):
    total = values[0].astype(F32)
    for value in values[1:]:
        total = total + value.astype(F32)
    return total.astype(BF16)


def ring_sum(keep, send):
    rows = keep.shape[1]
    got = swap(send)
    forth = shift(add(keep[8:10], got[8:10]), 1)
    back = shift(add(keep[10:12], got[10:12]), -1)
    one = jnp.concatenate([add(keep[4:6], got[4:6], forth), add(keep[6:8], got[6:8])])
    three = jnp.concatenate([add(keep[12:14], got[12:14]), add(keep[14:16], got[14:16], back)])
    forth, back = shift(one, 1), shift(three, -1)
    line = [add(keep[k], got[k], forth[k], back[k]) for k in range(4)]
    half = rows // 2
    forth = shift(line[2][:half], 1, True)
    back = shift(line[2][half:], -1, True)
    one = jnp.concatenate([add(line[1][:half], forth), line[1][half:]])
    three = jnp.concatenate([line[3][:half], add(line[3][half:], back)])
    return line[0], shift(one, 1, True), shift(three, -1, True)


def ring_gather(own):
    half = own.shape[0] // 2
    three, one = shift(own, 1), shift(own, -1)
    two = jnp.concatenate([shift(three[:half], 1), shift(one[half:], -1)])
    line = jnp.stack([own, one, two, three])
    three, one = shift(line, 1, True), shift(line, -1, True)
    return [line, three, one, shift(three[:2], 1, True), shift(one[2:], -1, True)]


def turn(value, step):
    return lax.ppermute(value, "tgt", [(t, (t + step) % SIDE) for t in range(SIDE)])


def shards(
    features,
    cites_tiles,
    cites_targets,
    cites_sources,
    cites_counts,
    writes_tiles,
    writes_targets,
    writes_sources,
    writes_counts,
    topic_tiles,
    topic_targets,
    topic_sources,
    topic_counts,
    owner_map,
    weights,
    bias_row,
    cotangent,
):
    width = features.shape[1]
    relations = (
        (cites_tiles, cites_targets, cites_sources, cites_counts),
        (writes_tiles, writes_targets, writes_sources, writes_counts),
        (topic_tiles, topic_targets, topic_sources, topic_counts),
    )
    s = lax.axis_index("src")
    place = jnp.stack([s // 8, (s // 2) % 4, s % 2, lax.axis_index("tgt")]).astype(jnp.int32)

    keep, send = gather_sums(place, owner_map, relations, features)
    parts = ring_sum(keep, send)

    rounded, terms0, terms1, terms2, terms3 = hidden_terms(place, parts, weights)
    hidden = (
        terms0
        + turn(terms1, 1).astype(F32)
        + turn(terms2, 2).astype(F32)
        + turn(terms3, 3).astype(F32)
        + bias_row.astype(F32)[None, :]
    )
    mixed_out, pullback = jax.vjp(functools.partial(jax.nn.gelu, approximate=True), hidden)
    grad_hidden = pullback(cotangent.astype(F32))[0].astype(BF16)
    grads = [grad_hidden, turn(grad_hidden, -1), turn(grad_hidden, -2), turn(grad_hidden, -3)]

    own = ring_gather(form_messages(place, grads, weights))
    sibling = [swap(piece) for piece in own]
    grad_source = spread_sums(place, owner_map, relations, own + sibling, width)

    weight_parts = ring_sum(*weight_terms(place, grads, rounded))
    weight_sum = sum(part.astype(F32) for part in weight_parts)
    grad_weight = weight_sum.reshape(32, 3, width).transpose(1, 2, 0)
    return (mixed_out.astype(BF16), grad_weight, grad_source.reshape(-1, width))


def solution(mesh):
    in_specs = (
        P("src", "tgt"),
        P("src", None, None),
        P("src"),
        P("src"),
        P("src"),
        P("src", None, None),
        P("src"),
        P("src"),
        P("src"),
        P("src", None, None),
        P("src"),
        P("src"),
        P("src"),
        P(),
        P(None, "tgt", None),
        P("tgt"),
        P("src", "tgt"),
    )
    out_specs = (P("src", "tgt"), P(None, "tgt", "src"), P("src", "tgt"))
    return jax.shard_map(shards, mesh=mesh, in_specs=in_specs, out_specs=out_specs, check_vma=False)
```

```python
import functools

import jax
import jax.numpy as jnp
from jax import lax
from jax.experimental import pallas as pl
from jax.experimental.pallas import tpu as pltpu
from jax.sharding import PartitionSpec as P

TILE = 128
SIDE = 4
GROUP = 8
BF16 = jnp.bfloat16
F32 = jnp.float32
MIB = 1024 * 1024
LOAD = 24
QUAD = 4
barrier = lax.optimization_barrier


def spec(space):
    return pl.BlockSpec(memory_space=space)


ANY, SMEM, VMEM = pl.ANY, pltpu.SMEM, pltpu.VMEM


def here():
    s = lax.axis_index("src")
    return s // 8, (s // 2) % SIDE, s % 2


def place_of(slot, mine):
    x, z, c = slot // 8, (slot // 2) % SIDE, slot % 2
    dx = (x - mine[0] + SIDE) % SIDE
    dz = (z - mine[1] + SIDE) % SIDE
    first = jnp.where(c == 0, dx, dz)
    second = jnp.where(c == 0, dz, dx)
    away = jnp.where(c == mine[2], 0, 16)
    return first, second, away


def each_load(tiles, counts, buffer, sems, bases, act):
    for number in range(3):
        def step(part, carry, number=number):
            offset = part * LOAD
            act(
                pltpu.make_async_copy(
                    tiles[number].at[pl.ds(offset, LOAD)],
                    buffer.at[pl.ds(bases[number] + offset, LOAD)],
                    sems.at[bases[number] // LOAD + part],
                )
            )
            return carry

        lax.fori_loop(0, (counts[number][0] + LOAD - 1) // LOAD, step, 0)


def gather_kernel(
    owner_map,
    targets0, targets1, targets2, sources0, sources1, sources2, counts0, counts1, counts2,
    features, tiles0, tiles1, tiles2,
    keep, send,
    buffer, total, staged, table, pending, pair_a, pair_b, pair_spot, tile_sems, out_sems,
):
    targets, sources = (targets0, targets1, targets2), (sources0, sources1, sources2)
    counts, tiles = (counts0, counts1, counts2), (tiles0, tiles1, tiles2)
    capacities = [t.shape[0] for t in tiles]
    bases = [0, capacities[0], capacities[0] + capacities[1]]
    blank = sum(capacities)
    each_load(tiles, counts, buffer, tile_sems, bases, lambda copy: copy.start())
    mine = here()
    buffer[blank] = jnp.zeros((TILE, TILE), BF16)

    def fill(slot, carry):
        first, second, away = place_of(slot, mine)
        table[owner_map[slot]] = (away + first * SIDE + second) * 3
        for number in range(3):
            pending[slot * 3 + number] = -1
            total[slot * 3 + number] = jnp.zeros(total.shape[1:], F32)
        return carry

    lax.fori_loop(0, 32, fill, 0)

    found = jnp.int32(0)
    for number in range(3):
        def match(group, found, number=number):
            for lane in range(GROUP):
                j = group * GROUP + lane
                live = j < counts[number][0]
                spot = table[targets[number][j]] + number
                code = (bases[number] + j) + sources[number][j] * 1024
                waiting = pending[spot]
                pair_a[found] = waiting
                pair_b[found] = code
                pair_spot[found] = spot
                hit = waiting >= 0
                pending[spot] = jnp.where(live, jnp.where(hit, -1, code), waiting)
                found = found + jnp.where(live & hit, 1, 0)
            return found

        found = lax.fori_loop(0, (counts[number][0] + GROUP - 1) // GROUP, match, found)

    def flush(group, found):
        for lane in range(GROUP):
            spot = group * GROUP + lane
            waiting = pending[spot]
            pair_a[found] = waiting
            pair_b[found] = blank
            pair_spot[found] = spot
            found = found + jnp.where(waiting >= 0, 1, 0)
        return found

    found = lax.fori_loop(0, 96 // GROUP, flush, found)
    for lane in range(GROUP):
        pair_a[found + lane] = blank
        pair_b[found + lane] = blank
        pair_spot[found + lane] = 96
    each_load(tiles, counts, buffer, tile_sems, bases, lambda copy: copy.wait())

    def add_group(group, carry):
        products = []
        for lane in range(GROUP):
            a, b = pair_a[group * GROUP + lane], pair_b[group * GROUP + lane]
            tile = jnp.concatenate([buffer[a & 1023], buffer[b & 1023]], axis=1)
            block = jnp.concatenate([features[a >> 10], features[b >> 10]], axis=0)
            products.append(jnp.dot(tile, block, preferred_element_type=F32))
        for lane in range(GROUP):
            total[pair_spot[group * GROUP + lane]] += products[lane]
        return carry

    lax.fori_loop(0, (found + GROUP - 1) // GROUP, add_group, 0)

    def out_copy(where, spot):
        target = keep if where == 0 else send
        return pltpu.make_async_copy(
            staged.at[where * 16 + spot], target.at[spot], out_sems.at[where * 16 + spot]
        )

    for where in (1, 0):
        def emit(spot, carry, where=where):
            for number in range(3):
                staged[where * 16 + spot, pl.ds(number * TILE, TILE), :] = total[
                    (where * 16 + spot) * 3 + number
                ].astype(BF16)
            out_copy(where, spot).start()
            return carry

        lax.fori_loop(0, 16, emit, 0)
    for where in (1, 0):
        def finish(spot, carry, where=where):
            out_copy(where, spot).wait()
            return carry

        lax.fori_loop(0, 16, finish, 0)


def flat_args(relations):
    return (
        *[relation[1] for relation in relations],
        *[relation[2] for relation in relations],
        *[relation[3] for relation in relations],
    )


def gather_sums(owner_map, relations, features):
    width = features.shape[-1]
    slots = sum(relation[0].shape[0] for relation in relations)
    blocks = jax.ShapeDtypeStruct((16, 3 * TILE, width), BF16)
    pairs = slots // 2 + 48 + 2 * GROUP
    return pl.pallas_call(
        gather_kernel,
        out_shape=(blocks, blocks),
        in_specs=[spec(SMEM)] * 10 + [spec(VMEM)] + [spec(ANY)] * 3,
        out_specs=(spec(ANY), spec(ANY)),
        scratch_shapes=[
            pltpu.VMEM((slots + 1, TILE, TILE), BF16),
            pltpu.VMEM((97, TILE, width), F32),
            pltpu.VMEM((32, 3 * TILE, width), BF16),
            pltpu.SMEM((32,), jnp.int32),
            pltpu.SMEM((96,), jnp.int32),
            pltpu.SMEM((pairs,), jnp.int32),
            pltpu.SMEM((pairs,), jnp.int32),
            pltpu.SMEM((pairs,), jnp.int32),
            pltpu.SemaphoreType.DMA((slots // LOAD,)),
            pltpu.SemaphoreType.DMA((32,)),
        ],
        compiler_params=pltpu.CompilerParams(vmem_limit_bytes=36 * MIB),
        cost_estimate=pl.CostEstimate(
            flops=3 * 10**9, bytes_accessed=18 * 10**6, transcendentals=0
        ),
        name="gather_sums",
    )(
        owner_map,
        *flat_args(relations),
        features.reshape(-1, TILE, width),
        *[relation[0] for relation in relations],
    )


def plan_kernel(
    owner_map,
    targets0, targets1, targets2, sources0, sources1, sources2, counts0, counts1, counts2,
    capacities,
    codes, starts, spots, amount,
    table, filled,
):
    targets, sources = (targets0, targets1, targets2), (sources0, sources1, sources2)
    counts = (counts0, counts1, counts2)
    bases = [0, capacities[0], capacities[0] + capacities[1]]
    blank = sum(capacities)
    room = blank + 16
    mine = here()

    def fill(slot, carry):
        first, second, away = place_of(slot, mine)
        table[owner_map[slot]] = (away + second * SIDE + first) * 3
        return carry

    lax.fori_loop(0, 32, fill, 0)
    for source in range(17):
        filled[source] = 0
    for number in range(3):
        def sort(group, carry, number=number):
            for lane in range(GROUP):
                j = group * GROUP + lane
                source = jnp.where(j < counts[number][0], sources[number][j], 16)
                at = filled[source]
                codes[source * room + at] = (
                    bases[number] + j + (table[targets[number][j]] + number) * 1024
                )
                filled[source] = at + 1
            return carry

        lax.fori_loop(0, (counts[number][0] + GROUP - 1) // GROUP, sort, 0)
    found = jnp.int32(0)
    for source in range(16):
        for lane in range(QUAD):
            codes[source * room + filled[source] + lane] = blank
        quads = (filled[source] + QUAD - 1) // QUAD

        def emit(quad, found, source=source):
            starts[found] = source * room + quad * QUAD
            spots[found] = source
            return found + 1

        found = lax.fori_loop(0, quads, emit, found)
    for lane in range(QUAD):
        codes[17 * room + lane] = blank
        starts[found + lane] = 17 * room
        spots[found + lane] = 16
    amount[0] = found


def plan_spread(owner_map, relations):
    capacities = [relation[0].shape[0] for relation in relations]
    slots = sum(capacities)
    quads = slots // QUAD + 16 + 2 * QUAD
    return pl.pallas_call(
        lambda *refs: plan_kernel(*refs[:10], capacities, *refs[10:]),
        out_shape=(
            jax.ShapeDtypeStruct((17 * (slots + 16) + QUAD,), jnp.int32),
            jax.ShapeDtypeStruct((quads,), jnp.int32),
            jax.ShapeDtypeStruct((quads,), jnp.int32),
            jax.ShapeDtypeStruct((1,), jnp.int32),
        ),
        in_specs=[spec(SMEM)] * 10,
        out_specs=tuple([spec(SMEM)] * 4),
        scratch_shapes=[pltpu.SMEM((32,), jnp.int32), pltpu.SMEM((17,), jnp.int32)],
        compiler_params=pltpu.CompilerParams(vmem_limit_bytes=MIB),
        cost_estimate=pl.CostEstimate(flops=10**9, bytes_accessed=10**6, transcendentals=0),
        name="plan_spread",
    )(owner_map, *flat_args(relations))


def spread_kernel(
    codes, starts, spots, amount, counts0, counts1, counts2,
    tiles0, tiles1, tiles2,
    own0, own2, own3, own1, sib0, sib2, sib3, sib1,
    out,
    buffer, messages, total, tile_sems, in_sems,
):
    counts, tiles = (counts0, counts1, counts2), (tiles0, tiles1, tiles2)
    capacities = [t.shape[0] for t in tiles]
    bases = [0, capacities[0], capacities[0] + capacities[1]]
    blank = sum(capacities)
    pieces = [
        (own0, 0), (own2, 8), (own3, 12), (own1, 4),
        (sib0, 16), (sib2, 24), (sib3, 28), (sib1, 20),
    ]
    copies = [
        pltpu.make_async_copy(piece, messages.at[pl.ds(at * 3, 12)], in_sems.at[number])
        for number, (piece, at) in enumerate(pieces)
    ]
    for copy in copies:
        copy.start()
    each_load(tiles, counts, buffer, tile_sems, bases, lambda copy: copy.start())
    buffer[blank] = jnp.zeros((TILE, TILE), BF16)

    def clear(block, carry):
        total[block] = jnp.zeros(total.shape[1:], F32)
        return carry

    lax.fori_loop(0, 16, clear, 0)
    for copy in copies:
        copy.wait()
    each_load(tiles, counts, buffer, tile_sems, bases, lambda copy: copy.wait())

    def add_group(group, carry):
        products = []
        for lane in range(QUAD):
            start = starts[group * QUAD + lane]
            marks = [codes[start + k] for k in range(QUAD)]
            block = jnp.concatenate([messages[mark >> 10] for mark in marks], axis=1)
            tile = jnp.concatenate([buffer[mark & 1023] for mark in marks], axis=0)
            products.append(jnp.dot(block, tile, preferred_element_type=F32))
        for lane in range(QUAD):
            total[spots[group * QUAD + lane]] += products[lane]
        return carry

    lax.fori_loop(0, (amount[0] + QUAD - 1) // QUAD, add_group, 0)

    def emit(block, carry):
        out[block] = total[block].T.astype(BF16)
        return carry

    lax.fori_loop(0, 16, emit, 0)


def spread_sums(plan, relations, pieces, width):
    slots = sum(relation[0].shape[0] for relation in relations)
    return pl.pallas_call(
        spread_kernel,
        out_shape=jax.ShapeDtypeStruct((16, TILE, width), BF16),
        in_specs=[spec(SMEM)] * 7 + [spec(ANY)] * 11,
        out_specs=spec(VMEM),
        scratch_shapes=[
            pltpu.VMEM((slots + 1, TILE, TILE), BF16),
            pltpu.VMEM((96, width, TILE), BF16),
            pltpu.VMEM((17, width, TILE), F32),
            pltpu.SemaphoreType.DMA((slots // LOAD,)),
            pltpu.SemaphoreType.DMA((8,)),
        ],
        compiler_params=pltpu.CompilerParams(vmem_limit_bytes=26 * MIB),
        cost_estimate=pl.CostEstimate(
            flops=3 * 10**9, bytes_accessed=18 * 10**6, transcendentals=0
        ),
        name="spread_sums",
    )(
        *plan,
        *[relation[3] for relation in relations],
        *[relation[0] for relation in relations],
        *pieces,
    )


def columns_at(step, width):
    column = (lax.axis_index("tgt") + step) % SIDE
    return pl.ds(pl.multiple_of(column * width, width), width)


def hidden_kernel(part0, part1, part2, part3, weights, rounded, terms0, terms1, terms2, terms3):
    width = part0.shape[1]
    whole = part0[...].astype(F32)
    for part in (part1, part2, part3):
        whole = whole + part[...].astype(F32)
    whole = whole.astype(BF16)
    rounded[...] = whole
    for step, terms in ((2, terms2), (1, terms1), (3, terms3), (0, terms0)):
        value = jnp.zeros(terms.shape, F32)
        for number in range(3):
            value += jnp.dot(
                whole[number * TILE:(number + 1) * TILE],
                weights[number, :, columns_at(step, width)],
                preferred_element_type=F32,
            )
        terms[...] = value.astype(terms.dtype)


def hidden_terms(parts, weights):
    width = parts[0].shape[1]
    return pl.pallas_call(
        hidden_kernel,
        out_shape=(
            jax.ShapeDtypeStruct((3 * TILE, width), BF16),
            jax.ShapeDtypeStruct((TILE, width), F32),
            jax.ShapeDtypeStruct((TILE, width), BF16),
            jax.ShapeDtypeStruct((TILE, width), BF16),
            jax.ShapeDtypeStruct((TILE, width), BF16),
        ),
        in_specs=[spec(VMEM)] * 5,
        out_specs=tuple([spec(VMEM)] * 5),
        compiler_params=pltpu.CompilerParams(vmem_limit_bytes=8 * MIB),
        name="hidden_terms",
    )(*parts, weights)


def message_kernel(grad0, grad1, grad2, grad3, weights, messages):
    width = grad0.shape[1]
    for number in range(3):
        value = jnp.zeros((width, TILE), F32)
        for step, grad in enumerate((grad0, grad1, grad2, grad3)):
            value += lax.dot_general(
                weights[number, :, columns_at(step, width)],
                grad[...],
                (((1,), (1,)), ((), ())),
                preferred_element_type=F32,
            )
        messages[number] = value.astype(BF16)


def form_messages(grads, weights):
    width = grads[0].shape[1]
    return pl.pallas_call(
        message_kernel,
        out_shape=jax.ShapeDtypeStruct((3, width, TILE), BF16),
        in_specs=[spec(VMEM)] * 5,
        out_specs=spec(VMEM),
        compiler_params=pltpu.CompilerParams(vmem_limit_bytes=8 * MIB),
        name="form_messages",
    )(*grads, weights)


def weight_kernel(grad0, grad1, grad2, grad3, rounded, keep, send, staged, sems):
    mine = here()
    block0 = lax.axis_index("tgt")
    values = jnp.concatenate(
        [rounded[number * TILE:(number + 1) * TILE, :] for number in range(3)], axis=1
    )
    for step, grad in enumerate((grad0, grad1, grad2, grad3)):
        turned = grad[...].astype(F32).T.astype(BF16)
        block = (block0 + step) % SIDE
        for part in range(8):
            first, second, away = place_of(block * 8 + part, mine)
            spot = away + second * SIDE + first
            value = jnp.dot(
                turned[part * 32:(part + 1) * 32], values, preferred_element_type=F32
            ).astype(BF16)
            for column in range(values.shape[1] // TILE):
                staged[spot, pl.ds(column * 32, 32), :] = value[
                    :, column * TILE:(column + 1) * TILE
                ]
    copies = [
        pltpu.make_async_copy(staged.at[pl.ds(16, 16)], send, sems.at[0]),
        pltpu.make_async_copy(staged.at[pl.ds(0, 16)], keep, sems.at[1]),
    ]
    for copy in copies:
        copy.start()
    for copy in copies:
        copy.wait()


def weight_terms(grads, rounded):
    width = grads[0].shape[1]
    rows = 32 * 3 * width // TILE
    blocks = jax.ShapeDtypeStruct((16, rows, TILE), BF16)
    return pl.pallas_call(
        weight_kernel,
        out_shape=(blocks, blocks),
        in_specs=[spec(VMEM)] * 5,
        out_specs=(spec(ANY), spec(ANY)),
        scratch_shapes=[
            pltpu.VMEM((32, rows, TILE), BF16),
            pltpu.SemaphoreType.DMA((2,)),
        ],
        compiler_params=pltpu.CompilerParams(vmem_limit_bytes=8 * MIB),
        cost_estimate=pl.CostEstimate(flops=10**9, bytes_accessed=3 * 10**6, transcendentals=0),
        name="weight_terms",
    )(*grads, rounded)


def shift_pairs(step, second):
    pairs = []
    for s in range(32):
        x, z, c = s // 8, (s // 2) % 4, s % 2
        if (c == 0) != second:
            x = (x + step) % SIDE
        else:
            z = (z + step) % SIDE
        pairs.append((s, (x * SIDE + z) * 2 + c))
    return pairs


def shift(value, step, second=False):
    return lax.ppermute(value, "src", shift_pairs(step, second))


def swap(value):
    return lax.ppermute(value, "src", [(s, s ^ 1) for s in range(32)])


def add(*values):
    total = values[0].astype(F32)
    for value in values[1:]:
        total = total + value.astype(F32)
    return total.astype(BF16)


def three_ways(values, second=False):
    return barrier(
        tuple(shift(values[k], k if k < 3 else -1, second) for k in (2, 1, 3))
    )


def turn(value, step):
    return lax.ppermute(value, "tgt", [(t, (t + step) % SIDE) for t in range(SIDE)])


def shards(
    features,
    cites_tiles,
    cites_targets,
    cites_sources,
    cites_counts,
    writes_tiles,
    writes_targets,
    writes_sources,
    writes_counts,
    topic_tiles,
    topic_targets,
    topic_sources,
    topic_counts,
    owner_map,
    weights,
    bias_row,
    cotangent,
):
    width = features.shape[1]
    relations = (
        (cites_tiles, cites_targets, cites_sources, cites_counts),
        (writes_tiles, writes_targets, writes_sources, writes_counts),
        (topic_tiles, topic_targets, topic_sources, topic_counts),
    )
    keep, send = gather_sums(owner_map, relations, features)
    got = swap(send)
    quarters = [add(keep[4 * k:4 * k + 4], got[4 * k:4 * k + 4]) for k in range(4)]
    arrived = three_ways(quarters)
    line = [add(quarters[0][k], *[part[k] for part in arrived]) for k in range(4)]
    owner_map, *line = barrier((owner_map, *line))
    plan = plan_spread(owner_map, relations)
    parts = (line[0], *three_ways(line, True))

    rounded, terms0, terms1, terms2, terms3 = hidden_terms(parts, weights)
    turned = barrier((turn(terms2, 2), turn(terms1, 1), turn(terms3, 3)))
    hidden = terms0 + bias_row.astype(F32)[None, :]
    for part in turned:
        hidden = hidden + part.astype(F32)
    mixed_out, pullback = jax.vjp(functools.partial(jax.nn.gelu, approximate=True), hidden)
    grad_hidden = pullback(cotangent.astype(F32))[0].astype(BF16)
    two, one, three = barrier(
        (turn(grad_hidden, -2), turn(grad_hidden, -1), turn(grad_hidden, -3))
    )
    grads = [grad_hidden, one, two, three]

    own = form_messages(grads, weights)
    held = (own, own, own, own)
    two, three, one = three_ways(held)
    weight_keep, weight_send = weight_terms(grads, rounded)
    weight_got = swap(weight_send)
    whole = jnp.concatenate([own, one, two, three])
    whole, weight_keep, weight_got = barrier((whole, weight_keep, weight_got))
    spread_out = (shift(whole, 2, True), shift(whole, 1, True), shift(whole, -1, True))
    beside = swap(whole)
    quarters = [
        add(weight_keep[4 * k:4 * k + 4], weight_got[4 * k:4 * k + 4]) for k in range(4)
    ]
    arrived = three_ways(quarters, True)
    line = [add(quarters[0][k], *[part[k] for part in arrived]) for k in range(4)]
    *spread_out, beside, l0, l1, l2, l3 = barrier((*spread_out, beside, *line))
    siblings = [swap(piece) for piece in spread_out]
    weight_parts = three_ways((l0, l1, l2, l3))
    grad_source = spread_sums(
        plan, relations, [whole, *spread_out, beside, *siblings], width
    )
    weight_sum = l0.astype(F32)
    for part in weight_parts:
        weight_sum = weight_sum + part.astype(F32)
    grad_weight = weight_sum.reshape(3 * width // TILE, 32, TILE).transpose(0, 2, 1)
    return (
        mixed_out.astype(BF16),
        grad_weight.reshape(3, width, 32),
        grad_source.reshape(-1, width),
    )


def solution(mesh):
    in_specs = (
        P("src", "tgt"),
        P("src", None, None),
        P("src"),
        P("src"),
        P("src"),
        P("src", None, None),
        P("src"),
        P("src"),
        P("src"),
        P("src", None, None),
        P("src"),
        P("src"),
        P("src"),
        P(),
        P(None, "tgt", None),
        P("tgt"),
        P("src", "tgt"),
    )
    out_specs = (P("src", "tgt"), P(None, "tgt", "src"), P("src", "tgt"))
    return jax.shard_map(shards, mesh=mesh, in_specs=in_specs, out_specs=out_specs, check_vma=False)
```

```python
import functools

import jax
import jax.numpy as jnp
from jax import lax
from jax.experimental import pallas as pl
from jax.experimental.pallas import tpu as pltpu
from jax.sharding import PartitionSpec as P

TILE = 128
SIDE = 4
GROUP = 16
BF16 = jnp.bfloat16
F32 = jnp.float32
MIB = 1024 * 1024
GATHER_LIMIT = 60 * MIB
SPREAD_LIMIT = 60 * MIB
barrier = lax.optimization_barrier


def spec(space):
    return pl.BlockSpec(memory_space=space)


ANY, HBM, SMEM, VMEM = pl.ANY, pltpu.HBM, pltpu.SMEM, pltpu.VMEM


def here():
    s = lax.axis_index("src")
    return s // 8, (s // 2) % SIDE, s % 2


def place_of(slot, mine):
    x, z, c = slot // 8, (slot // 2) % SIDE, slot % 2
    dx = (x - mine[0] + SIDE) % SIDE
    dz = (z - mine[1] + SIDE) % SIDE
    first = jnp.where(c == 0, dx, dz)
    second = jnp.where(c == 0, dz, dx)
    away = jnp.where(c == mine[2], 0, 16)
    return first, second, away


def each_load(tiles, counts, buffer, sems, bases):
    for number in range(3):
        def step(part, carry, number=number):
            load(tiles, buffer, sems, bases, number, part).start()
            return carry

        lax.fori_loop(0, (counts[number][0] + GROUP - 1) // GROUP, step, 0)


def load(tiles, buffer, sems, bases, number, part):
    offset = part * GROUP
    return pltpu.make_async_copy(
        tiles[number].at[pl.ds(offset, GROUP)],
        buffer.at[pl.ds(bases[number] + offset, GROUP)],
        sems.at[bases[number] // GROUP + part],
    )


def gather_kernel(
    owner_map,
    targets0, targets1, targets2, sources0, sources1, sources2, counts0, counts1, counts2,
    features, tiles0, tiles1, tiles2,
    keep, send,
    buffer, total0, total1, total2, total3, staged, table, tile_sems, out_sems,
):
    targets, sources = (targets0, targets1, targets2), (sources0, sources1, sources2)
    counts, tiles = (counts0, counts1, counts2), (tiles0, tiles1, tiles2)
    totals = (total0, total1, total2, total3)
    rows = TILE // 4
    capacities = [t.shape[0] for t in tiles]
    bases = [0, capacities[0], capacities[0] + capacities[1]]
    each_load(tiles, counts, buffer, tile_sems, bases)
    mine = here()

    def fill(slot, carry):
        first, second, away = place_of(slot, mine)
        table[owner_map[slot]] = (away + first * SIDE + second) * 3
        for number in range(3):
            for total in totals:
                total[slot * 3 + number] = jnp.zeros(total.shape[1:], F32)
        return carry

    lax.fori_loop(0, 32, fill, 0)

    for number in range(3):
        def add_group(group, carry, number=number):
            load(tiles, buffer, tile_sems, bases, number, group).wait()
            products = []
            for lane in range(GROUP):
                j = group * GROUP + lane
                products.append(
                    jnp.dot(
                        buffer[bases[number] + j],
                        features[sources[number][j]],
                        preferred_element_type=F32,
                    )
                )
            for lane in range(GROUP):
                j = group * GROUP + lane
                spot = jnp.where(j < counts[number][0], table[targets[number][j]] + number, 96)
                for part, total in enumerate(totals):
                    total[spot] += products[lane][part * rows:(part + 1) * rows]
            return carry

        lax.fori_loop(0, (counts[number][0] + GROUP - 1) // GROUP, add_group, 0)

    def out_copy(where, spot):
        target = keep if where == 0 else send
        return pltpu.make_async_copy(
            staged.at[where * 16 + spot], target.at[spot], out_sems.at[where * 16 + spot]
        )

    for where in (1, 0):
        def emit(spot, carry, where=where):
            for number in range(3):
                for part, total in enumerate(totals):
                    staged[where * 16 + spot, pl.ds(number * TILE + part * rows, rows), :] = total[
                        (where * 16 + spot) * 3 + number
                    ].astype(BF16)
            out_copy(where, spot).start()
            return carry

        lax.fori_loop(0, 16, emit, 0)
    for where in (1, 0):
        def finish(spot, carry, where=where):
            out_copy(where, spot).wait()
            return carry

        lax.fori_loop(0, 16, finish, 0)


def flat_args(relations):
    return (
        *[relation[1] for relation in relations],
        *[relation[2] for relation in relations],
        *[relation[3] for relation in relations],
    )


def gather_sums(owner_map, relations, features):
    width = features.shape[-1]
    slots = sum(relation[0].shape[0] for relation in relations)
    blocks = jax.ShapeDtypeStruct((16, 3 * TILE, width), BF16)
    return pl.pallas_call(
        gather_kernel,
        out_shape=(blocks, blocks),
        in_specs=[spec(SMEM)] * 10 + [spec(VMEM)] + [spec(ANY)] * 3,
        out_specs=(spec(ANY), spec(ANY)),
        scratch_shapes=[
            pltpu.VMEM((slots, TILE, TILE), BF16),
            *[pltpu.VMEM((97, TILE // 4, width), F32)] * 4,
            pltpu.VMEM((32, 3 * TILE, width), BF16),
            pltpu.SMEM((32,), jnp.int32),
            pltpu.SemaphoreType.DMA((slots // GROUP,)),
            pltpu.SemaphoreType.DMA((32,)),
        ],
        compiler_params=pltpu.CompilerParams(vmem_limit_bytes=GATHER_LIMIT),
        cost_estimate=pl.CostEstimate(
            flops=3 * 10**9, bytes_accessed=18 * 10**6, transcendentals=0
        ),
        name="gather_sums",
    )(
        owner_map,
        *flat_args(relations),
        features.reshape(-1, TILE, width),
        *[relation[0] for relation in relations],
    )


def spread_kernel(
    owner_map,
    targets0, targets1, targets2, sources0, sources1, sources2, counts0, counts1, counts2,
    tiles0, tiles1, tiles2,
    own0, own2, own3, own1, sib0, sib2, sib3, sib1,
    out,
    buffer, messages, total0, total1, total2, total3, table, tile_sems, in_sems,
):
    targets, sources = (targets0, targets1, targets2), (sources0, sources1, sources2)
    counts, tiles = (counts0, counts1, counts2), (tiles0, tiles1, tiles2)
    totals = (total0, total1, total2, total3)
    rows = total0.shape[1]
    capacities = [t.shape[0] for t in tiles]
    bases = [0, capacities[0], capacities[0] + capacities[1]]
    each_load(tiles, counts, buffer, tile_sems, bases)
    pieces = [
        (own0, 0), (own2, 8), (own3, 12), (own1, 4),
        (sib0, 16), (sib2, 24), (sib3, 28), (sib1, 20),
    ]
    copies = [
        pltpu.make_async_copy(piece, messages.at[pl.ds(at * 3, 12)], in_sems.at[number])
        for number, (piece, at) in enumerate(pieces)
    ]
    for copy in copies:
        copy.start()
    mine = here()

    def fill(slot, carry):
        first, second, away = place_of(slot, mine)
        table[owner_map[slot]] = (away + second * SIDE + first) * 3
        return carry

    lax.fori_loop(0, 32, fill, 0)

    def clear(block, carry):
        for total in totals:
            total[block] = jnp.zeros(total.shape[1:], F32)
        return carry

    lax.fori_loop(0, 16, clear, 0)
    for copy in copies:
        copy.wait()

    for number in range(3):
        def add_group(group, carry, number=number):
            load(tiles, buffer, tile_sems, bases, number, group).wait()
            products = []
            for lane in range(GROUP):
                j = group * GROUP + lane
                products.append(
                    jnp.dot(
                        messages[table[targets[number][j]] + number],
                        buffer[bases[number] + j],
                        preferred_element_type=F32,
                    )
                )
            for lane in range(GROUP):
                j = group * GROUP + lane
                spot = jnp.where(j < counts[number][0], sources[number][j], 16)
                for part, total in enumerate(totals):
                    total[spot] += products[lane][part * rows:(part + 1) * rows]
            return carry

        lax.fori_loop(0, (counts[number][0] + GROUP - 1) // GROUP, add_group, 0)

    def emit(block, carry):
        whole = jnp.concatenate([total[block] for total in totals])
        out[block] = whole.T.astype(BF16)
        return carry

    lax.fori_loop(0, 16, emit, 0)


def spread_sums(owner_map, relations, pieces, width):
    slots = sum(relation[0].shape[0] for relation in relations)
    return pl.pallas_call(
        spread_kernel,
        out_shape=jax.ShapeDtypeStruct((16, TILE, width), BF16),
        in_specs=[spec(SMEM)] * 10 + [spec(ANY)] * 11,
        out_specs=spec(VMEM),
        scratch_shapes=[
            pltpu.VMEM((slots, TILE, TILE), BF16),
            pltpu.VMEM((96, width, TILE), BF16),
            *[pltpu.VMEM((17, width // 4, TILE), F32)] * 4,
            pltpu.SMEM((32,), jnp.int32),
            pltpu.SemaphoreType.DMA((slots // GROUP,)),
            pltpu.SemaphoreType.DMA((8,)),
        ],
        compiler_params=pltpu.CompilerParams(vmem_limit_bytes=SPREAD_LIMIT),
        cost_estimate=pl.CostEstimate(
            flops=3 * 10**9, bytes_accessed=18 * 10**6, transcendentals=0
        ),
        name="spread_sums",
    )(
        owner_map,
        *flat_args(relations),
        *[relation[0] for relation in relations],
        *pieces,
    )


def columns_at(step, width):
    column = (lax.axis_index("tgt") + step) % SIDE
    return pl.ds(pl.multiple_of(column * width, width), width)


def hidden_kernel(part0, part1, part2, part3, weights, rounded, terms0, terms1, terms2, terms3):
    width = part0.shape[1]
    whole = part0[...].astype(F32)
    for part in (part1, part2, part3):
        whole = whole + part[...].astype(F32)
    whole = whole.astype(BF16)
    rounded[...] = whole
    for step, terms in ((2, terms2), (1, terms1), (3, terms3), (0, terms0)):
        value = jnp.zeros(terms.shape, F32)
        for number in range(3):
            value += jnp.dot(
                whole[number * TILE:(number + 1) * TILE],
                weights[number, :, columns_at(step, width)],
                preferred_element_type=F32,
            )
        terms[...] = value.astype(terms.dtype)


def hidden_terms(parts, weights):
    width = parts[0].shape[1]
    return pl.pallas_call(
        hidden_kernel,
        out_shape=(
            jax.ShapeDtypeStruct((3 * TILE, width), BF16),
            jax.ShapeDtypeStruct((TILE, width), F32),
            jax.ShapeDtypeStruct((TILE, width), BF16),
            jax.ShapeDtypeStruct((TILE, width), BF16),
            jax.ShapeDtypeStruct((TILE, width), BF16),
        ),
        in_specs=[spec(VMEM)] * 5,
        out_specs=tuple([spec(VMEM)] * 5),
        compiler_params=pltpu.CompilerParams(vmem_limit_bytes=8 * MIB),
        name="hidden_terms",
    )(*parts, weights)


def message_kernel(grad0, grad1, grad2, grad3, weights, messages):
    width = grad0.shape[1]
    for number in range(3):
        value = jnp.zeros((width, TILE), F32)
        for step, grad in enumerate((grad0, grad1, grad2, grad3)):
            value += lax.dot_general(
                weights[number, :, columns_at(step, width)],
                grad[...],
                (((1,), (1,)), ((), ())),
                preferred_element_type=F32,
            )
        messages[number] = value.astype(BF16)


def form_messages(grads, weights):
    width = grads[0].shape[1]
    return pl.pallas_call(
        message_kernel,
        out_shape=jax.ShapeDtypeStruct((3, width, TILE), BF16),
        in_specs=[spec(VMEM)] * 5,
        out_specs=spec(VMEM),
        compiler_params=pltpu.CompilerParams(vmem_limit_bytes=8 * MIB),
        name="form_messages",
    )(*grads, weights)


def weight_kernel(grad0, grad1, grad2, grad3, rounded, keep, send, staged, sems):
    mine = here()
    block0 = lax.axis_index("tgt")
    values = jnp.concatenate(
        [rounded[number * TILE:(number + 1) * TILE, :] for number in range(3)], axis=1
    )
    for step, grad in enumerate((grad0, grad1, grad2, grad3)):
        turned = grad[...].astype(F32).T.astype(BF16)
        block = (block0 + step) % SIDE
        for part in range(8):
            first, second, away = place_of(block * 8 + part, mine)
            spot = away + second * SIDE + first
            value = jnp.dot(
                turned[part * 32:(part + 1) * 32], values, preferred_element_type=F32
            ).astype(BF16)
            for column in range(values.shape[1] // TILE):
                staged[spot, pl.ds(column * 32, 32), :] = value[
                    :, column * TILE:(column + 1) * TILE
                ]
    copies = [
        pltpu.make_async_copy(staged.at[pl.ds(16, 16)], send, sems.at[0]),
        pltpu.make_async_copy(staged.at[pl.ds(0, 16)], keep, sems.at[1]),
    ]
    for copy in copies:
        copy.start()
    for copy in copies:
        copy.wait()


def weight_terms(grads, rounded):
    width = grads[0].shape[1]
    rows = 32 * 3 * width // TILE
    blocks = jax.ShapeDtypeStruct((16, rows, TILE), BF16)
    return pl.pallas_call(
        weight_kernel,
        out_shape=(blocks, blocks),
        in_specs=[spec(VMEM)] * 5,
        out_specs=(spec(ANY), spec(ANY)),
        scratch_shapes=[
            pltpu.VMEM((32, rows, TILE), BF16),
            pltpu.SemaphoreType.DMA((2,)),
        ],
        compiler_params=pltpu.CompilerParams(vmem_limit_bytes=8 * MIB),
        cost_estimate=pl.CostEstimate(flops=10**9, bytes_accessed=3 * 10**6, transcendentals=0),
        name="weight_terms",
    )(*grads, rounded)


def shift_pairs(step, second):
    pairs = []
    for s in range(32):
        x, z, c = s // 8, (s // 2) % 4, s % 2
        if (c == 0) != second:
            x = (x + step) % SIDE
        else:
            z = (z + step) % SIDE
        pairs.append((s, (x * SIDE + z) * 2 + c))
    return pairs


def shift(value, step, second=False):
    return lax.ppermute(value, "src", shift_pairs(step, second))


def swap(value):
    return lax.ppermute(value, "src", [(s, s ^ 1) for s in range(32)])


def add(*values):
    total = values[0].astype(F32)
    for value in values[1:]:
        total = total + value.astype(F32)
    return total.astype(BF16)


def three_ways(values, second=False):
    return barrier(
        tuple(shift(values[k], k if k < 3 else -1, second) for k in (2, 1, 3))
    )


def turn(value, step):
    return lax.ppermute(value, "tgt", [(t, (t + step) % SIDE) for t in range(SIDE)])


def shards(
    features,
    cites_tiles,
    cites_targets,
    cites_sources,
    cites_counts,
    writes_tiles,
    writes_targets,
    writes_sources,
    writes_counts,
    topic_tiles,
    topic_targets,
    topic_sources,
    topic_counts,
    owner_map,
    weights,
    bias_row,
    cotangent,
):
    width = features.shape[1]
    relations = (
        (cites_tiles, cites_targets, cites_sources, cites_counts),
        (writes_tiles, writes_targets, writes_sources, writes_counts),
        (topic_tiles, topic_targets, topic_sources, topic_counts),
    )
    keep, send = gather_sums(owner_map, relations, features)
    got = swap(send)
    quarters = [add(keep[4 * k:4 * k + 4], got[4 * k:4 * k + 4]) for k in range(4)]
    arrived = three_ways(quarters)
    line = [add(quarters[0][k], *[part[k] for part in arrived]) for k in range(4)]
    parts = (line[0], *three_ways(line, True))

    rounded, terms0, terms1, terms2, terms3 = hidden_terms(parts, weights)
    turned = barrier((turn(terms2, 2), turn(terms1, 1), turn(terms3, 3)))
    hidden = terms0 + bias_row.astype(F32)[None, :]
    for part in turned:
        hidden = hidden + part.astype(F32)
    mixed_out, pullback = jax.vjp(functools.partial(jax.nn.gelu, approximate=True), hidden)
    grad_hidden = pullback(cotangent.astype(F32))[0].astype(BF16)
    two, one, three = barrier(
        (turn(grad_hidden, -2), turn(grad_hidden, -1), turn(grad_hidden, -3))
    )
    grads = [grad_hidden, one, two, three]

    own = form_messages(grads, weights)
    held = (own, own, own, own)
    two, three, one = three_ways(held)
    weight_keep, weight_send = weight_terms(grads, rounded)
    weight_got = swap(weight_send)
    whole = jnp.concatenate([own, one, two, three])
    whole, weight_keep, weight_got = barrier((whole, weight_keep, weight_got))
    spread_out = (shift(whole, 2, True), shift(whole, 1, True), shift(whole, -1, True))
    beside = swap(whole)
    quarters = [
        add(weight_keep[4 * k:4 * k + 4], weight_got[4 * k:4 * k + 4]) for k in range(4)
    ]
    arrived = three_ways(quarters, True)
    line = [add(quarters[0][k], *[part[k] for part in arrived]) for k in range(4)]
    *spread_out, beside, l0, l1, l2, l3 = barrier((*spread_out, beside, *line))
    siblings = [swap(piece) for piece in spread_out]
    weight_parts = three_ways((l0, l1, l2, l3))
    grad_source = spread_sums(
        owner_map, relations, [whole, *spread_out, beside, *siblings], width
    )
    weight_sum = l0.astype(F32)
    for part in weight_parts:
        weight_sum = weight_sum + part.astype(F32)
    grad_weight = weight_sum.reshape(3 * width // TILE, 32, TILE).transpose(0, 2, 1)
    return (
        mixed_out.astype(BF16),
        grad_weight.reshape(3, width, 32),
        grad_source.reshape(-1, width),
    )


def solution(mesh):
    in_specs = (
        P("src", "tgt"),
        P("src", None, None),
        P("src"),
        P("src"),
        P("src"),
        P("src", None, None),
        P("src"),
        P("src"),
        P("src"),
        P("src", None, None),
        P("src"),
        P("src"),
        P("src"),
        P(),
        P(None, "tgt", None),
        P("tgt"),
        P("src", "tgt"),
    )
    out_specs = (P("src", "tgt"), P(None, "tgt", "src"), P("src", "tgt"))
    return jax.shard_map(shards, mesh=mesh, in_specs=in_specs, out_specs=out_specs, check_vma=False)
```

```python
import functools

import jax
import jax.numpy as jnp
from jax import lax
from jax.experimental import pallas as pl
from jax.experimental.pallas import tpu as pltpu
from jax.sharding import PartitionSpec as P

TILE = 128
SIDE = 4
GROUP = 16
PAIRS = 16
BF16 = jnp.bfloat16
F32 = jnp.float32
MIB = 1024 * 1024
GATHER_LIMIT = 60 * MIB
SPREAD_LIMIT = 60 * MIB
barrier = lax.optimization_barrier


def spec(space):
    return pl.BlockSpec(memory_space=space)


ANY, HBM, SMEM, VMEM = pl.ANY, pltpu.HBM, pltpu.SMEM, pltpu.VMEM


def here():
    s = lax.axis_index("src")
    return s >> 3, (s >> 1) & 3, s & 1


def place_of(slot, mine):
    c = slot & 1
    dx = ((slot >> 3) - mine[0]) & 3
    dz = ((slot >> 1) - mine[1]) & 3
    first = jnp.where(c == 0, dx, dz)
    second = jnp.where(c == 0, dz, dx)
    return first, second, c ^ mine[2]


def live_parts(counts):
    parts = [(count[0] + GROUP - 1) // GROUP for count in counts]
    return parts, [0, parts[0], parts[0] + parts[1], parts[0] + parts[1] + parts[2]]


def start_tiles(tiles, counts, buffer, sems):
    parts, begins = live_parts(counts)
    for number in range(3):
        def step(part, carry, number=number):
            at = begins[number] + part
            pltpu.make_async_copy(
                tiles[number].at[pl.ds(part * GROUP, GROUP)],
                buffer.at[pl.ds(at * GROUP, GROUP)],
                sems.at[at],
            ).start()
            return carry

        lax.fori_loop(0, parts[number], step, 0)
    return begins


def wait_tiles(tile, buffer, sems, waited, needed):
    def step(at, carry):
        pltpu.make_async_copy(
            tile.at[pl.ds(0, GROUP)], buffer.at[pl.ds(at * GROUP, GROUP)], sems.at[at]
        ).wait()
        return carry

    lax.fori_loop(waited, needed, step, 0)
    return jnp.maximum(waited, needed)


def clear(total, amount):
    def step(block, carry):
        total[block] = jnp.zeros(total.shape[1:], F32)
        return carry

    lax.fori_loop(0, amount, step, 0)


def gather_kernel(
    owner_map,
    targets0, targets1, targets2, sources0, sources1, sources2, counts0, counts1, counts2,
    features, tiles0, tiles1, tiles2,
    keep, send,
    buffer, held, total, staged, table, tile_sems, out_sems, feature_sem,
):
    targets, sources = (targets0, targets1, targets2), (sources0, sources1, sources2)
    counts, tiles = (counts0, counts1, counts2), (tiles0, tiles1, tiles2)
    feature_copy = pltpu.make_async_copy(features, held, feature_sem)
    feature_copy.start()
    begins = start_tiles(tiles, counts, buffer, tile_sems)
    mine = here()

    def fill(slot, carry):
        first, second, away = place_of(slot, mine)
        table[owner_map[slot]] = (away * 16 + first * SIDE + second) * 3
        for number in range(3):
            total[slot * 3 + number] = jnp.zeros(total.shape[1:], F32)
        return carry

    lax.fori_loop(0, 32, fill, 0)
    feature_copy.wait()

    for number in range(3):
        def add_group(group, carry, number=number):
            at = begins[number] + group
            wait_tiles(tiles[0], buffer, tile_sems, at, at + 1)
            products = []
            for lane in range(GROUP):
                source = sources[number][group * GROUP + lane]
                products.append(
                    jnp.dot(
                        buffer[at * GROUP + lane], held[source], preferred_element_type=F32
                    )
                )
            for lane in range(GROUP):
                j = group * GROUP + lane
                spot = jnp.where(j < counts[number][0], table[targets[number][j]] + number, 96)
                total[spot] += products[lane]
            return carry

        lax.fori_loop(0, (counts[number][0] + GROUP - 1) // GROUP, add_group, 0)

    def out_copy(where, spot):
        target = keep if where == 0 else send
        return pltpu.make_async_copy(
            staged.at[where * 16 + spot], target.at[spot], out_sems.at[where * 16 + spot]
        )

    for where in (1, 0):
        def emit(spot, carry, where=where):
            block = where * 16 + spot
            for number in range(3):
                staged[block, pl.ds(number * TILE, TILE), :] = total[block * 3 + number].astype(
                    BF16
                )
            out_copy(where, spot).start()
            return carry

        lax.fori_loop(0, 16, emit, 0)
    for where in (1, 0):
        def finish(spot, carry, where=where):
            out_copy(where, spot).wait()
            return carry

        lax.fori_loop(0, 16, finish, 0)


def flat_args(relations):
    return (
        *[relation[1] for relation in relations],
        *[relation[2] for relation in relations],
        *[relation[3] for relation in relations],
    )


def gather_sums(owner_map, relations, features):
    width = features.shape[-1]
    slots = sum(relation[0].shape[0] for relation in relations)
    blocks = jax.ShapeDtypeStruct((16, 3 * TILE, width), BF16)
    features = features.reshape(-1, TILE, width)
    return pl.pallas_call(
        gather_kernel,
        out_shape=(blocks, blocks),
        in_specs=[spec(SMEM)] * 10 + [spec(ANY)] * 4,
        out_specs=(spec(ANY), spec(ANY)),
        scratch_shapes=[
            pltpu.VMEM((slots, TILE, TILE), BF16),
            pltpu.VMEM(features.shape, BF16),
            pltpu.VMEM((97, TILE, width), F32),
            pltpu.VMEM((32, 3 * TILE, width), BF16),
            pltpu.SMEM((32,), jnp.int32),
            pltpu.SemaphoreType.DMA((slots // GROUP,)),
            pltpu.SemaphoreType.DMA((32,)),
            pltpu.SemaphoreType.DMA(()),
        ],
        compiler_params=pltpu.CompilerParams(vmem_limit_bytes=GATHER_LIMIT),
        cost_estimate=pl.CostEstimate(
            flops=3 * 10**9, bytes_accessed=18 * 10**6, transcendentals=0
        ),
        name="gather_sums",
    )(owner_map, *flat_args(relations), features, *[relation[0] for relation in relations])


def plan_kernel(
    owner_map,
    targets0, targets1, targets2, sources0, sources1, sources2, counts0, counts1, counts2,
    pair_a, pair_b, pair_spot, amount,
    table, pending,
    *, blank,
):
    targets, sources = (targets0, targets1, targets2), (sources0, sources1, sources2)
    counts = (counts0, counts1, counts2)
    begins = live_parts(counts)[1]
    mine = here()

    def fill(slot, carry):
        first, second, away = place_of(slot, mine)
        table[owner_map[slot]] = (away * 16 + second * SIDE + first) * 3
        return carry

    lax.fori_loop(0, 32, fill, 0)
    for spot in range(17):
        pending[spot] = -1

    def put(found, a, b, spot, yes):
        pair_a[found] = a
        pair_b[found] = b
        pair_spot[found] = spot
        return found + jnp.where(yes, 1, 0)

    found = jnp.int32(0)
    for number in range(3):
        def match(group, found, number=number):
            for lane in range(GROUP):
                j = group * GROUP + lane
                live = j < counts[number][0]
                code = begins[number] * GROUP + j + (table[targets[number][j]] + number) * 1024
                spot = jnp.where(live, sources[number][j], 16)
                waiting = pending[spot]
                hit = live & (waiting >= 0)
                found = put(found, waiting, code, spot, hit)
                pending[spot] = jnp.where(hit, -1, code)
            return found

        found = lax.fori_loop(0, (counts[number][0] + GROUP - 1) // GROUP, match, found)
    for spot in range(16):
        found = put(found, pending[spot], blank, spot, pending[spot] >= 0)
    for lane in range(PAIRS):
        put(found + lane, blank, blank, 16, False)
    amount[0] = found


def plan_spread(owner_map, relations):
    slots = sum(relation[0].shape[0] for relation in relations)
    pairs = jax.ShapeDtypeStruct((slots // 2 + 16 + 2 * PAIRS,), jnp.int32)
    return pl.pallas_call(
        functools.partial(plan_kernel, blank=slots),
        out_shape=(pairs, pairs, pairs, jax.ShapeDtypeStruct((1,), jnp.int32)),
        in_specs=[spec(SMEM)] * 10,
        out_specs=tuple([spec(SMEM)] * 4),
        scratch_shapes=[pltpu.SMEM((32,), jnp.int32), pltpu.SMEM((17,), jnp.int32)],
        compiler_params=pltpu.CompilerParams(vmem_limit_bytes=MIB),
        cost_estimate=pl.CostEstimate(flops=10**9, bytes_accessed=10**6, transcendentals=0),
        name="plan_spread",
    )(owner_map, *flat_args(relations))


PLACES = (0, 8, 12, 4, 16, 24, 28, 20)


def spread_kernel(pair_a, pair_b, pair_spot, amount, *refs):
    counts, tiles, pieces, refs = refs[:3], refs[3:6], refs[6:14], refs[14:]
    out, buffer, messages, total, tile_sems, in_sems = refs
    begins = start_tiles(tiles, counts, buffer, tile_sems)
    copies = [
        pltpu.make_async_copy(piece, messages.at[pl.ds(at * 3, 12)], in_sems.at[number])
        for number, (piece, at) in enumerate(zip(pieces, PLACES))
    ]
    for copy in copies:
        copy.start()
    blank = buffer.shape[0] - 1
    buffer[blank] = jnp.zeros((TILE, TILE), BF16)
    clear(total, 16)
    for copy in copies:
        copy.wait()

    def add_group(group, waited):
        at = group * PAIRS
        needed = jnp.minimum(((pair_b[at + PAIRS - 1] & 1023) >> 4) + 1, begins[3])
        waited = wait_tiles(tiles[0], buffer, tile_sems, waited, needed)
        products = []
        for lane in range(PAIRS):
            marks = (pair_a[at + lane], pair_b[at + lane])
            tile = jnp.concatenate([buffer[mark & 1023] for mark in marks], axis=0)
            block = jnp.concatenate([messages[mark >> 10] for mark in marks], axis=0)
            products.append(
                lax.dot_general(
                    tile, block, (((0,), (0,)), ((), ())), preferred_element_type=F32
                )
            )
        for lane in range(PAIRS):
            total[pair_spot[at + lane]] += products[lane]
        return waited

    waited = lax.fori_loop(0, (amount[0] + PAIRS - 1) // PAIRS, add_group, jnp.int32(0))
    wait_tiles(tiles[0], buffer, tile_sems, waited, begins[3])

    def emit(block, carry):
        out[block] = total[block].astype(out.dtype)
        return carry

    lax.fori_loop(0, 16, emit, 0)


def spread_sums(plan, relations, pieces):
    width = pieces[0].shape[-1]
    slots = sum(relation[0].shape[0] for relation in relations)
    return pl.pallas_call(
        spread_kernel,
        out_shape=jax.ShapeDtypeStruct((16, TILE, width), BF16),
        in_specs=[spec(SMEM)] * 7 + [spec(ANY)] * 11,
        out_specs=spec(VMEM),
        scratch_shapes=[
            pltpu.VMEM((slots + 1, TILE, TILE), BF16),
            pltpu.VMEM((96, TILE, width), BF16),
            pltpu.VMEM((17, TILE, width), F32),
            pltpu.SemaphoreType.DMA((slots // GROUP,)),
            pltpu.SemaphoreType.DMA((8,)),
        ],
        compiler_params=pltpu.CompilerParams(vmem_limit_bytes=SPREAD_LIMIT),
        cost_estimate=pl.CostEstimate(
            flops=3 * 10**9, bytes_accessed=18 * 10**6, transcendentals=0
        ),
        name="spread_sums",
    )(
        *plan,
        *[relation[3] for relation in relations],
        *[relation[0] for relation in relations],
        *pieces,
    )


def columns_at(step, width):
    column = (lax.axis_index("tgt") + step) % SIDE
    return pl.ds(pl.multiple_of(column * width, width), width)


def hidden_kernel(part0, part1, part2, part3, weights, rounded, terms0, terms1, terms2, terms3):
    width = part0.shape[1]
    whole = part0[...].astype(F32)
    for part in (part1, part2, part3):
        whole = whole + part[...].astype(F32)
    whole = whole.astype(BF16)
    rounded[...] = whole
    for step, terms in ((2, terms2), (1, terms1), (3, terms3), (0, terms0)):
        value = jnp.zeros(terms.shape, F32)
        for number in range(3):
            value += jnp.dot(
                whole[number * TILE:(number + 1) * TILE],
                weights[number, :, columns_at(step, width)],
                preferred_element_type=F32,
            )
        terms[...] = value.astype(terms.dtype)


def hidden_terms(parts, weights):
    width = parts[0].shape[1]
    return pl.pallas_call(
        hidden_kernel,
        out_shape=(
            jax.ShapeDtypeStruct((3 * TILE, width), BF16),
            jax.ShapeDtypeStruct((TILE, width), F32),
            jax.ShapeDtypeStruct((TILE, width), BF16),
            jax.ShapeDtypeStruct((TILE, width), BF16),
            jax.ShapeDtypeStruct((TILE, width), BF16),
        ),
        in_specs=[spec(VMEM)] * 5,
        out_specs=tuple([spec(VMEM)] * 5),
        compiler_params=pltpu.CompilerParams(vmem_limit_bytes=8 * MIB),
        name="hidden_terms",
    )(*parts, weights)


def message_kernel(grad0, grad1, grad2, grad3, weights, messages):
    width = grad0.shape[1]
    for number in range(3):
        value = jnp.zeros((TILE, width), F32)
        for step, grad in enumerate((grad0, grad1, grad2, grad3)):
            value += lax.dot_general(
                grad[...],
                weights[number, :, columns_at(step, width)],
                (((1,), (1,)), ((), ())),
                preferred_element_type=F32,
            )
        messages[number] = value.astype(BF16)


def form_messages(grads, weights):
    width = grads[0].shape[1]
    return pl.pallas_call(
        message_kernel,
        out_shape=jax.ShapeDtypeStruct((3, TILE, width), BF16),
        in_specs=[spec(VMEM)] * 5,
        out_specs=spec(VMEM),
        compiler_params=pltpu.CompilerParams(vmem_limit_bytes=8 * MIB),
        name="form_messages",
    )(*grads, weights)


def weight_kernel(grad0, grad1, grad2, grad3, rounded, keep, send, staged, sems):
    mine = here()
    block0 = lax.axis_index("tgt")
    values = jnp.concatenate(
        [rounded[number * TILE:(number + 1) * TILE, :] for number in range(3)], axis=1
    )
    for step, grad in enumerate((grad0, grad1, grad2, grad3)):
        turned = grad[...].astype(F32).T.astype(BF16)
        block = (block0 + step) % SIDE
        for part in range(8):
            first, second, away = place_of(block * 8 + part, mine)
            spot = away * 16 + second * SIDE + first
            value = jnp.dot(
                turned[part * 32:(part + 1) * 32], values, preferred_element_type=F32
            ).astype(BF16)
            for column in range(values.shape[1] // TILE):
                staged[spot, pl.ds(column * 32, 32), :] = value[
                    :, column * TILE:(column + 1) * TILE
                ]
    copies = [
        pltpu.make_async_copy(staged.at[pl.ds(16, 16)], send, sems.at[0]),
        pltpu.make_async_copy(staged.at[pl.ds(0, 16)], keep, sems.at[1]),
    ]
    for copy in copies:
        copy.start()
    for copy in copies:
        copy.wait()


def weight_terms(grads, rounded):
    width = grads[0].shape[1]
    rows = 32 * 3 * width // TILE
    blocks = jax.ShapeDtypeStruct((16, rows, TILE), BF16)
    return pl.pallas_call(
        weight_kernel,
        out_shape=(blocks, blocks),
        in_specs=[spec(VMEM)] * 5,
        out_specs=(spec(ANY), spec(ANY)),
        scratch_shapes=[
            pltpu.VMEM((32, rows, TILE), BF16),
            pltpu.SemaphoreType.DMA((2,)),
        ],
        compiler_params=pltpu.CompilerParams(vmem_limit_bytes=8 * MIB),
        cost_estimate=pl.CostEstimate(flops=10**9, bytes_accessed=3 * 10**6, transcendentals=0),
        name="weight_terms",
    )(*grads, rounded)


def shift_pairs(step, second):
    pairs = []
    for s in range(32):
        x, z, c = s // 8, (s // 2) % 4, s % 2
        if (c == 0) != second:
            x = (x + step) % SIDE
        else:
            z = (z + step) % SIDE
        pairs.append((s, (x * SIDE + z) * 2 + c))
    return pairs


def shift(value, step, second=False):
    return lax.ppermute(value, "src", shift_pairs(step, second))


def swap(value):
    return lax.ppermute(value, "src", [(s, s ^ 1) for s in range(32)])


def add(*values):
    total = values[0].astype(F32)
    for value in values[1:]:
        total = total + value.astype(F32)
    return total.astype(BF16)


def three_ways(values, second=False):
    return barrier(
        tuple(shift(values[k], k if k < 3 else -1, second) for k in (2, 1, 3))
    )


def turn(value, step):
    return lax.ppermute(value, "tgt", [(t, (t + step) % SIDE) for t in range(SIDE)])


def shards(
    features,
    cites_tiles,
    cites_targets,
    cites_sources,
    cites_counts,
    writes_tiles,
    writes_targets,
    writes_sources,
    writes_counts,
    topic_tiles,
    topic_targets,
    topic_sources,
    topic_counts,
    owner_map,
    weights,
    bias_row,
    cotangent,
):
    width = features.shape[1]
    relations = (
        (cites_tiles, cites_targets, cites_sources, cites_counts),
        (writes_tiles, writes_targets, writes_sources, writes_counts),
        (topic_tiles, topic_targets, topic_sources, topic_counts),
    )
    keep, send = gather_sums(owner_map, relations, features)
    got = swap(send)
    quarters = [add(keep[4 * k:4 * k + 4], got[4 * k:4 * k + 4]) for k in range(4)]
    owner_map, *quarters = barrier((owner_map, *quarters))
    arrived = three_ways(quarters)
    plan = plan_spread(owner_map, relations)
    *plan, a0, a1, a2 = barrier((*plan, *arrived))
    line = [add(quarters[0][k], *[part[k] for part in (a0, a1, a2)]) for k in range(4)]
    parts = (line[0], *three_ways(line, True))

    rounded, terms0, terms1, terms2, terms3 = hidden_terms(parts, weights)
    turned = barrier((turn(terms2, 2), turn(terms1, 1), turn(terms3, 3)))
    hidden = terms0 + bias_row.astype(F32)[None, :]
    for part in turned:
        hidden = hidden + part.astype(F32)
    mixed_out, pullback = jax.vjp(functools.partial(jax.nn.gelu, approximate=True), hidden)
    grad_hidden = pullback(cotangent.astype(F32))[0].astype(BF16)
    two, one, three = barrier(
        (turn(grad_hidden, -2), turn(grad_hidden, -1), turn(grad_hidden, -3))
    )
    grads = [grad_hidden, one, two, three]

    own = form_messages(grads, weights)
    own, *grads = barrier((own, *grads))
    two, three, one = three_ways((own, own, own, own))
    weight_keep, weight_send = weight_terms(grads, rounded)
    weight_got = swap(weight_send)
    whole = jnp.concatenate([own, one, two, three])
    whole, weight_keep, weight_got = barrier((whole, weight_keep, weight_got))
    spread_out = (shift(whole, 2, True), shift(whole, 1, True), shift(whole, -1, True))
    beside = swap(whole)
    quarters = [
        add(weight_keep[4 * k:4 * k + 4], weight_got[4 * k:4 * k + 4]) for k in range(4)
    ]
    arrived = three_ways(quarters, True)
    line = [add(quarters[0][k], *[part[k] for part in arrived]) for k in range(4)]
    *spread_out, beside, l0, l1, l2, l3 = barrier((*spread_out, beside, *line))
    siblings = [swap(piece) for piece in spread_out]
    weight_parts = three_ways((l0, l1, l2, l3))
    grad_source = spread_sums(plan, relations, [whole, *spread_out, beside, *siblings])
    *weight_parts, grad_source = barrier((*weight_parts, grad_source))
    weight_sum = l0.astype(F32)
    for part in weight_parts:
        weight_sum = weight_sum + part.astype(F32)
    grad_weight = weight_sum.reshape(3 * width // TILE, 32, TILE).transpose(0, 2, 1)
    return (
        mixed_out.astype(BF16),
        grad_weight.reshape(3, width, 32),
        grad_source.reshape(-1, width),
    )


def solution(mesh):
    in_specs = (
        P("src", "tgt"),
        P("src", None, None),
        P("src"),
        P("src"),
        P("src"),
        P("src", None, None),
        P("src"),
        P("src"),
        P("src"),
        P("src", None, None),
        P("src"),
        P("src"),
        P("src"),
        P(),
        P(None, "tgt", None),
        P("tgt"),
        P("src", "tgt"),
    )
    out_specs = (P("src", "tgt"), P(None, "tgt", "src"), P("src", "tgt"))
    return jax.shard_map(shards, mesh=mesh, in_specs=in_specs, out_specs=out_specs, check_vma=False)
```

```python
import functools

import jax
import jax.numpy as jnp
from jax import lax
from jax.experimental import pallas as pl
from jax.experimental.pallas import tpu as pltpu
from jax.sharding import PartitionSpec as P


TILE = 128
SIDE = 4
GROUP = 16
PAIRS = 16
BF16 = jnp.bfloat16
F32 = jnp.float32
MIB = 1024 * 1024
GATHER_LIMIT = 36 * MIB
SPREAD_LIMIT = 26 * MIB
barrier = lax.optimization_barrier


def spec(space):
    return pl.BlockSpec(memory_space=space)


ANY, SMEM, VMEM = pl.ANY, pltpu.SMEM, pltpu.VMEM


def here():
    s = lax.axis_index("src")
    return s >> 3, (s >> 1) & 3, s & 1


def place_of(slot, mine):
    c = slot & 1
    dx = ((slot >> 3) - mine[0]) & 3
    dz = ((slot >> 1) - mine[1]) & 3
    first = jnp.where(c == 0, dx, dz)
    second = jnp.where(c == 0, dz, dx)
    return first, second, c ^ mine[2]


def live_parts(counts):
    parts = [(count[0] + GROUP - 1) // GROUP for count in counts]
    return parts, [0, parts[0], parts[0] + parts[1], parts[0] + parts[1] + parts[2]]


def start_tiles(tiles, counts, buffer, sems):
    parts, begins = live_parts(counts)
    for number in range(3):
        def step(part, carry, number=number):
            at = begins[number] + part
            pltpu.make_async_copy(
                tiles[number].at[pl.ds(part * GROUP, GROUP)],
                buffer.at[pl.ds(at * GROUP, GROUP)],
                sems.at[at],
            ).start()
            return carry

        lax.fori_loop(0, parts[number], step, 0)
    return begins


def wait_tiles(tile, buffer, sems, waited, needed):
    def step(at, carry):
        pltpu.make_async_copy(
            tile.at[pl.ds(0, GROUP)], buffer.at[pl.ds(at * GROUP, GROUP)], sems.at[at]
        ).wait()
        return carry

    lax.fori_loop(waited, needed, step, 0)
    return jnp.maximum(waited, needed)


def clear(total, amount):
    def step(block, carry):
        total[block] = jnp.zeros(total.shape[1:], F32)
        return carry

    lax.fori_loop(0, amount, step, 0)


def gather_kernel(
    owner_map,
    targets0, targets1, targets2, sources0, sources1, sources2, counts0, counts1, counts2,
    features, tiles0, tiles1, tiles2,
    keep, send,
    buffer, held, total, staged, table, tile_sems, out_sems, feature_sem,
):
    targets, sources = (targets0, targets1, targets2), (sources0, sources1, sources2)
    counts, tiles = (counts0, counts1, counts2), (tiles0, tiles1, tiles2)
    feature_copy = pltpu.make_async_copy(features, held, feature_sem)
    feature_copy.start()
    begins = start_tiles(tiles, counts, buffer, tile_sems)
    mine = here()

    def fill(slot, carry):
        first, second, away = place_of(slot, mine)
        table[owner_map[slot]] = (away * 16 + first * SIDE + second) * 3
        for number in range(3):
            total[slot * 3 + number] = jnp.zeros(total.shape[1:], F32)
        return carry

    lax.fori_loop(0, 32, fill, 0)
    feature_copy.wait()

    for number in range(3):
        def add_group(group, carry, number=number):
            at = begins[number] + group
            wait_tiles(tiles[0], buffer, tile_sems, at, at + 1)
            products = []
            for lane in range(GROUP):
                source = sources[number][group * GROUP + lane]
                products.append(
                    jnp.dot(
                        buffer[at * GROUP + lane], held[source], preferred_element_type=F32
                    )
                )
            for lane in range(GROUP):
                j = group * GROUP + lane
                spot = jnp.where(j < counts[number][0], table[targets[number][j]] + number, 96)
                total[spot] += products[lane]
            return carry

        lax.fori_loop(0, (counts[number][0] + GROUP - 1) // GROUP, add_group, 0)

    def out_copy(where, spot):
        target = keep if where == 0 else send
        return pltpu.make_async_copy(
            staged.at[where * 16 + spot], target.at[spot], out_sems.at[where * 16 + spot]
        )

    for where in (1, 0):
        def emit(spot, carry, where=where):
            block = where * 16 + spot
            for number in range(3):
                staged[block, pl.ds(number * TILE, TILE), :] = total[block * 3 + number].astype(
                    BF16
                )
            out_copy(where, spot).start()
            return carry

        lax.fori_loop(0, 16, emit, 0)
    for where in (1, 0):
        def finish(spot, carry, where=where):
            out_copy(where, spot).wait()
            return carry

        lax.fori_loop(0, 16, finish, 0)


def in_hbm(value):
    return pltpu.with_memory_space_constraint(value, pltpu.HBM)


def flat_args(owner_map, relations):
    return (
        in_hbm(owner_map),
        *[in_hbm(relation[1]) for relation in relations],
        *[in_hbm(relation[2]) for relation in relations],
        *[relation[3] for relation in relations],
    )


def tile_args(relations):
    return [in_hbm(relation[0]) for relation in relations]


def gather_sums(owner_map, relations, features):
    width = features.shape[-1]
    slots = sum(relation[0].shape[0] for relation in relations)
    blocks = jax.ShapeDtypeStruct((16, 3 * TILE, width), BF16)
    features = features.reshape(-1, TILE, width)
    return pl.pallas_call(
        gather_kernel,
        out_shape=(blocks, blocks),
        in_specs=[spec(SMEM)] * 10 + [spec(ANY)] * 4,
        out_specs=(spec(ANY), spec(ANY)),
        scratch_shapes=[
            pltpu.VMEM((slots, TILE, TILE), BF16),
            pltpu.VMEM(features.shape, BF16),
            pltpu.VMEM((97, TILE, width), F32),
            pltpu.VMEM((32, 3 * TILE, width), BF16),
            pltpu.SMEM((32,), jnp.int32),
            pltpu.SemaphoreType.DMA((slots // GROUP,)),
            pltpu.SemaphoreType.DMA((32,)),
            pltpu.SemaphoreType.DMA(()),
        ],
        compiler_params=pltpu.CompilerParams(vmem_limit_bytes=GATHER_LIMIT),
        cost_estimate=pl.CostEstimate(
            flops=3 * 10**9, bytes_accessed=18 * 10**6, transcendentals=0
        ),
        name="gather_sums",
    )(*flat_args(owner_map, relations), in_hbm(features), *tile_args(relations))


def plan_kernel(
    owner_map,
    targets0, targets1, targets2, sources0, sources1, sources2, counts0, counts1, counts2,
    pair_a, pair_b, pair_spot, amount,
    table, pending,
    *, blank,
):
    targets, sources = (targets0, targets1, targets2), (sources0, sources1, sources2)
    counts = (counts0, counts1, counts2)
    begins = live_parts(counts)[1]
    mine = here()

    def fill(slot, carry):
        first, second, away = place_of(slot, mine)
        table[owner_map[slot]] = (away * 16 + second * SIDE + first) * 3
        return carry

    lax.fori_loop(0, 32, fill, 0)
    for spot in range(17):
        pending[spot] = -1

    def put(found, a, b, spot, yes):
        pair_a[found] = a
        pair_b[found] = b
        pair_spot[found] = spot
        return found + jnp.where(yes, 1, 0)

    found = jnp.int32(0)
    for number in range(3):
        def match(group, found, number=number):
            for lane in range(GROUP):
                j = group * GROUP + lane
                live = j < counts[number][0]
                code = begins[number] * GROUP + j + (table[targets[number][j]] + number) * 1024
                spot = jnp.where(live, sources[number][j], 16)
                waiting = pending[spot]
                hit = live & (waiting >= 0)
                found = put(found, waiting, code, spot, hit)
                pending[spot] = jnp.where(hit, -1, code)
            return found

        found = lax.fori_loop(0, (counts[number][0] + GROUP - 1) // GROUP, match, found)
    for spot in range(16):
        found = put(found, pending[spot], blank, spot, pending[spot] >= 0)
    for lane in range(PAIRS):
        put(found + lane, blank, blank, 16, False)
    amount[0] = found


def plan_spread(owner_map, relations):
    slots = sum(relation[0].shape[0] for relation in relations)
    pairs = jax.ShapeDtypeStruct((slots // 2 + 16 + 2 * PAIRS,), jnp.int32)
    return pl.pallas_call(
        functools.partial(plan_kernel, blank=slots),
        out_shape=(pairs, pairs, pairs, jax.ShapeDtypeStruct((1,), jnp.int32)),
        in_specs=[spec(SMEM)] * 10,
        out_specs=tuple([spec(SMEM)] * 4),
        scratch_shapes=[pltpu.SMEM((32,), jnp.int32), pltpu.SMEM((17,), jnp.int32)],
        compiler_params=pltpu.CompilerParams(vmem_limit_bytes=MIB),
        cost_estimate=pl.CostEstimate(flops=10**9, bytes_accessed=10**6, transcendentals=0),
        name="plan_spread",
    )(*flat_args(owner_map, relations))


PLACES = (0, 8, 12, 4, 16, 24, 28, 20)


def spread_kernel(pair_a, pair_b, pair_spot, amount, *refs):
    counts, tiles, pieces, refs = refs[:3], refs[3:6], refs[6:14], refs[14:]
    out, buffer, messages, total, tile_sems, in_sems = refs
    begins = start_tiles(tiles, counts, buffer, tile_sems)
    copies = [
        pltpu.make_async_copy(piece, messages.at[pl.ds(at * 3, 12)], in_sems.at[number])
        for number, (piece, at) in enumerate(zip(pieces, PLACES))
    ]
    for copy in copies:
        copy.start()
    blank = buffer.shape[0] - 1
    buffer[blank] = jnp.zeros((TILE, TILE), BF16)
    clear(total, 16)
    for copy in copies:
        copy.wait()

    def add_group(group, waited):
        at = group * PAIRS
        needed = jnp.minimum(((pair_b[at + PAIRS - 1] & 1023) >> 4) + 1, begins[3])
        waited = wait_tiles(tiles[0], buffer, tile_sems, waited, needed)
        products = []
        for lane in range(PAIRS):
            marks = (pair_a[at + lane], pair_b[at + lane])
            tile = jnp.concatenate([buffer[mark & 1023] for mark in marks], axis=0)
            block = jnp.concatenate([messages[mark >> 10] for mark in marks], axis=0)
            products.append(
                lax.dot_general(
                    tile, block, (((0,), (0,)), ((), ())), preferred_element_type=F32
                )
            )
        for lane in range(PAIRS):
            total[pair_spot[at + lane]] += products[lane]
        return waited

    waited = lax.fori_loop(0, (amount[0] + PAIRS - 1) // PAIRS, add_group, jnp.int32(0))
    wait_tiles(tiles[0], buffer, tile_sems, waited, begins[3])

    def emit(block, carry):
        out[block] = total[block].astype(out.dtype)
        return carry

    lax.fori_loop(0, 16, emit, 0)


def spread_sums(plan, relations, pieces):
    width = pieces[0].shape[-1]
    slots = sum(relation[0].shape[0] for relation in relations)
    return pl.pallas_call(
        spread_kernel,
        out_shape=jax.ShapeDtypeStruct((16, TILE, width), BF16),
        in_specs=[spec(SMEM)] * 7 + [spec(ANY)] * 11,
        out_specs=spec(VMEM),
        scratch_shapes=[
            pltpu.VMEM((slots + 1, TILE, TILE), BF16),
            pltpu.VMEM((96, TILE, width), BF16),
            pltpu.VMEM((17, TILE, width), F32),
            pltpu.SemaphoreType.DMA((slots // GROUP,)),
            pltpu.SemaphoreType.DMA((8,)),
        ],
        compiler_params=pltpu.CompilerParams(vmem_limit_bytes=SPREAD_LIMIT),
        cost_estimate=pl.CostEstimate(
            flops=3 * 10**9, bytes_accessed=18 * 10**6, transcendentals=0
        ),
        name="spread_sums",
    )(
        *plan,
        *[relation[3] for relation in relations],
        *tile_args(relations),
        *pieces,
    )


def columns_at(step, width):
    column = (lax.axis_index("tgt") + step) % SIDE
    return pl.ds(pl.multiple_of(column * width, width), width)


def hidden_kernel(part0, part1, part2, part3, weights, rounded, terms0, terms1, terms2, terms3):
    width = part0.shape[1]
    whole = part0[...].astype(F32)
    for part in (part1, part2, part3):
        whole = whole + part[...].astype(F32)
    whole = whole.astype(BF16)
    rounded[...] = whole
    for step, terms in ((2, terms2), (1, terms1), (3, terms3), (0, terms0)):
        value = jnp.zeros(terms.shape, F32)
        for number in range(3):
            value += jnp.dot(
                whole[number * TILE:(number + 1) * TILE],
                weights[number, :, columns_at(step, width)],
                preferred_element_type=F32,
            )
        terms[...] = value.astype(terms.dtype)


def hidden_terms(parts, weights):
    width = parts[0].shape[1]
    return pl.pallas_call(
        hidden_kernel,
        out_shape=(
            jax.ShapeDtypeStruct((3 * TILE, width), BF16),
            jax.ShapeDtypeStruct((TILE, width), F32),
            jax.ShapeDtypeStruct((TILE, width), BF16),
            jax.ShapeDtypeStruct((TILE, width), BF16),
            jax.ShapeDtypeStruct((TILE, width), BF16),
        ),
        in_specs=[spec(VMEM)] * 5,
        out_specs=tuple([spec(VMEM)] * 5),
        compiler_params=pltpu.CompilerParams(vmem_limit_bytes=8 * MIB),
        name="hidden_terms",
    )(*parts, weights)


def message_kernel(grad0, grad1, grad2, grad3, weights, messages):
    width = grad0.shape[1]
    for number in range(3):
        value = jnp.zeros((TILE, width), F32)
        for step, grad in enumerate((grad0, grad1, grad2, grad3)):
            value += lax.dot_general(
                grad[...],
                weights[number, :, columns_at(step, width)],
                (((1,), (1,)), ((), ())),
                preferred_element_type=F32,
            )
        messages[number] = value.astype(BF16)


def form_messages(grads, weights):
    width = grads[0].shape[1]
    return pl.pallas_call(
        message_kernel,
        out_shape=jax.ShapeDtypeStruct((3, TILE, width), BF16),
        in_specs=[spec(VMEM)] * 5,
        out_specs=spec(VMEM),
        compiler_params=pltpu.CompilerParams(vmem_limit_bytes=8 * MIB),
        name="form_messages",
    )(*grads, weights)


def weight_kernel(grad0, grad1, grad2, grad3, rounded, keep, send, staged, sems):
    mine = here()
    block0 = lax.axis_index("tgt")
    values = jnp.concatenate(
        [rounded[number * TILE:(number + 1) * TILE, :] for number in range(3)], axis=1
    )
    for step, grad in enumerate((grad0, grad1, grad2, grad3)):
        turned = grad[...].astype(F32).T.astype(BF16)
        block = (block0 + step) % SIDE
        for part in range(8):
            first, second, away = place_of(block * 8 + part, mine)
            spot = away * 16 + second * SIDE + first
            value = jnp.dot(
                turned[part * 32:(part + 1) * 32], values, preferred_element_type=F32
            ).astype(BF16)
            for column in range(values.shape[1] // TILE):
                staged[spot, pl.ds(column * 32, 32), :] = value[
                    :, column * TILE:(column + 1) * TILE
                ]
    copies = [
        pltpu.make_async_copy(staged.at[pl.ds(16, 16)], send, sems.at[0]),
        pltpu.make_async_copy(staged.at[pl.ds(0, 16)], keep, sems.at[1]),
    ]
    for copy in copies:
        copy.start()
    for copy in copies:
        copy.wait()


def weight_terms(grads, rounded):
    width = grads[0].shape[1]
    rows = 32 * 3 * width // TILE
    blocks = jax.ShapeDtypeStruct((16, rows, TILE), BF16)
    return pl.pallas_call(
        weight_kernel,
        out_shape=(blocks, blocks),
        in_specs=[spec(VMEM)] * 5,
        out_specs=(spec(ANY), spec(ANY)),
        scratch_shapes=[
            pltpu.VMEM((32, rows, TILE), BF16),
            pltpu.SemaphoreType.DMA((2,)),
        ],
        compiler_params=pltpu.CompilerParams(vmem_limit_bytes=8 * MIB),
        cost_estimate=pl.CostEstimate(flops=10**9, bytes_accessed=3 * 10**6, transcendentals=0),
        name="weight_terms",
    )(*grads, rounded)


def shift_pairs(step, second):
    pairs = []
    for s in range(32):
        x, z, c = s // 8, (s // 2) % 4, s % 2
        if (c == 0) != second:
            x = (x + step) % SIDE
        else:
            z = (z + step) % SIDE
        pairs.append((s, (x * SIDE + z) * 2 + c))
    return pairs


def shift(value, step, second=False):
    return lax.ppermute(value, "src", shift_pairs(step, second))


def swap(value):
    return lax.ppermute(value, "src", [(s, s ^ 1) for s in range(32)])


def add(*values):
    total = values[0].astype(F32)
    for value in values[1:]:
        total = total + value.astype(F32)
    return total.astype(BF16)


def three_starts(values, second=False):
    arrived = []
    for k in (2, 1, 3):
        arrived.append(shift(values[k], k if k < 3 else -1, second))
    return tuple(arrived)


def three_ways(values, second=False):
    return barrier(three_starts(values, second))


def turn(value, step):
    return lax.ppermute(value, "tgt", [(t, (t + step) % SIDE) for t in range(SIDE)])


def shards(
    features,
    cites_tiles,
    cites_targets,
    cites_sources,
    cites_counts,
    writes_tiles,
    writes_targets,
    writes_sources,
    writes_counts,
    topic_tiles,
    topic_targets,
    topic_sources,
    topic_counts,
    owner_map,
    weights,
    bias_row,
    cotangent,
):
    width = features.shape[1]
    relations = (
        (cites_tiles, cites_targets, cites_sources, cites_counts),
        (writes_tiles, writes_targets, writes_sources, writes_counts),
        (topic_tiles, topic_targets, topic_sources, topic_counts),
    )
    keep, send = gather_sums(owner_map, relations, features)
    got = swap(send)
    quarters = [add(keep[4 * k:4 * k + 4], got[4 * k:4 * k + 4]) for k in range(4)]
    owner_map, *quarters = barrier((owner_map, *quarters))
    arrived = three_ways(quarters)
    plan = plan_spread(owner_map, relations)
    *plan, a0, a1, a2 = barrier((*plan, *arrived))
    line = [add(quarters[0][k], *[part[k] for part in (a0, a1, a2)]) for k in range(4)]
    parts = (line[0], *three_ways(line, True))

    rounded, terms0, terms1, terms2, terms3 = hidden_terms(parts, weights)
    turned = barrier((turn(terms2, 2), turn(terms1, 1), turn(terms3, 3)))
    hidden = terms0 + bias_row.astype(F32)[None, :]
    for part in turned:
        hidden = hidden + part.astype(F32)
    mixed_out, pullback = jax.vjp(functools.partial(jax.nn.gelu, approximate=True), hidden)
    grad_hidden = pullback(cotangent.astype(F32))[0].astype(BF16)
    two, one, three = barrier(
        (turn(grad_hidden, -2), turn(grad_hidden, -1), turn(grad_hidden, -3))
    )
    grads = [grad_hidden, one, two, three]

    own = form_messages(grads, weights)
    own, *grads = barrier((own, *grads))
    two, three, one = barrier(three_starts((own,) * 4))
    weight_keep, weight_send = weight_terms(grads, rounded)
    weight_got = swap(weight_send)
    quarters = [
        add(weight_keep[4 * k:4 * k + 4], weight_got[4 * k:4 * k + 4]) for k in range(4)
    ]
    arrived = barrier(three_starts(quarters, True))
    whole = jnp.concatenate([own, one, two, three])
    spread_out = three_starts((whole,) * 4, True)
    beside = swap(whole)
    line = [add(quarters[0][k], *[part[k] for part in arrived]) for k in range(4)]
    weight_parts = three_ways(line)
    *spread_out, beside, l0, w0, w1, w2 = barrier((*spread_out, beside, line[0], *weight_parts))
    weight_parts = (w0, w1, w2)
    siblings = [swap(piece) for piece in spread_out]
    grad_source = spread_sums(plan, relations, [whole, *spread_out, beside, *siblings])
    weight_sum = l0.astype(F32)
    for part in weight_parts:
        weight_sum = weight_sum + part.astype(F32)
    grad_weight = weight_sum.reshape(3 * width // TILE, 32, TILE).transpose(0, 2, 1)
    return (
        mixed_out.astype(BF16),
        grad_weight.reshape(3, width, 32),
        grad_source.reshape(-1, width),
    )


def solution(mesh):
    in_specs = (
        P("src", "tgt"),
        P("src", None, None),
        P("src"),
        P("src"),
        P("src"),
        P("src", None, None),
        P("src"),
        P("src"),
        P("src"),
        P("src", None, None),
        P("src"),
        P("src"),
        P("src"),
        P(),
        P(None, "tgt", None),
        P("tgt"),
        P("src", "tgt"),
    )
    out_specs = (P("src", "tgt"), P(None, "tgt", "src"), P("src", "tgt"))

    return jax.shard_map(shards, mesh=mesh, in_specs=in_specs, out_specs=out_specs, check_vma=False)
```

```python
import functools

import jax
import jax.numpy as jnp
from jax import lax
from jax.experimental import pallas as pl
from jax.experimental.pallas import tpu as pltpu
from jax.sharding import PartitionSpec as P


TILE = 128
SIDE = 4
GROUP = 16
PAIRS = 16
BF16 = jnp.bfloat16
F32 = jnp.float32
MIB = 1024 * 1024
GATHER_LIMIT = 36 * MIB
SPREAD_LIMIT = 28 * MIB
barrier = lax.optimization_barrier


def spec(space):
    return pl.BlockSpec(memory_space=space)


ANY, SMEM, VMEM = pl.ANY, pltpu.SMEM, pltpu.VMEM


def here():
    s = lax.axis_index("src")
    return s >> 3, (s >> 1) & 3, s & 1


def place_of(slot, mine):
    c = slot & 1
    dx = ((slot >> 3) - mine[0]) & 3
    dz = ((slot >> 1) - mine[1]) & 3
    first = jnp.where(c == 0, dx, dz)
    second = jnp.where(c == 0, dz, dx)
    return first, second, c ^ mine[2]


def live_parts(counts):
    parts = [(count[0] + GROUP - 1) // GROUP for count in counts]
    return parts, [0, parts[0], parts[0] + parts[1], parts[0] + parts[1] + parts[2]]


def start_tiles(tiles, counts, buffer, sems):
    parts, begins = live_parts(counts)
    for number in range(3):
        def step(part, carry, number=number):
            at = begins[number] + part
            pltpu.make_async_copy(
                tiles[number].at[pl.ds(part * GROUP, GROUP)],
                buffer.at[pl.ds(at * GROUP, GROUP)],
                sems.at[at],
            ).start()
            return carry

        lax.fori_loop(0, parts[number], step, 0)
    return begins


def wait_tiles(tile, buffer, sems, waited, needed):
    def step(at, carry):
        pltpu.make_async_copy(
            tile.at[pl.ds(0, GROUP)], buffer.at[pl.ds(at * GROUP, GROUP)], sems.at[at]
        ).wait()
        return carry

    lax.fori_loop(waited, needed, step, 0)
    return jnp.maximum(waited, needed)


def clear(total, amount):
    def step(block, carry):
        total[block] = jnp.zeros(total.shape[1:], F32)
        return carry

    lax.fori_loop(0, amount, step, 0)


def gather_kernel(
    owner_map,
    targets0, targets1, targets2, sources0, sources1, sources2, counts0, counts1, counts2,
    features, tiles0, tiles1, tiles2,
    keep, send,
    buffer, held, total, table, tile_sems, feature_sem,
):
    targets, sources = (targets0, targets1, targets2), (sources0, sources1, sources2)
    counts, tiles = (counts0, counts1, counts2), (tiles0, tiles1, tiles2)
    feature_copy = pltpu.make_async_copy(features, held, feature_sem)
    feature_copy.start()
    begins = start_tiles(tiles, counts, buffer, tile_sems)
    mine = here()

    def fill(slot, carry):
        first, second, away = place_of(slot, mine)
        table[owner_map[slot]] = (away * 16 + first * SIDE + second) * 3
        for number in range(3):
            total[slot * 3 + number] = jnp.zeros(total.shape[1:], F32)
        return carry

    lax.fori_loop(0, 32, fill, 0)
    feature_copy.wait()

    for number in range(3):
        def add_group(group, carry, number=number):
            at = begins[number] + group
            wait_tiles(tiles[0], buffer, tile_sems, at, at + 1)
            products = []
            for lane in range(GROUP):
                source = sources[number][group * GROUP + lane]
                products.append(
                    jnp.dot(
                        buffer[at * GROUP + lane], held[source], preferred_element_type=F32
                    )
                )
            for lane in range(GROUP):
                j = group * GROUP + lane
                spot = jnp.where(j < counts[number][0], table[targets[number][j]] + number, 96)
                total[spot] += products[lane]
            return carry

        lax.fori_loop(0, (counts[number][0] + GROUP - 1) // GROUP, add_group, 0)

    for where, target in ((16, send), (0, keep)):
        def emit(spot, carry, where=where, target=target):
            for number in range(3):
                target[spot, pl.ds(number * TILE, TILE), :] = total[
                    (where + spot) * 3 + number
                ].astype(BF16)
            return carry

        lax.fori_loop(0, 16, emit, 0)


def in_hbm(value):
    return pltpu.with_memory_space_constraint(value, pltpu.HBM)


def flat_args(owner_map, relations):
    return (
        in_hbm(owner_map),
        *[in_hbm(relation[1]) for relation in relations],
        *[in_hbm(relation[2]) for relation in relations],
        *[relation[3] for relation in relations],
    )


def tile_args(relations):
    return [in_hbm(relation[0]) for relation in relations]


def gather_sums(owner_map, relations, features):
    width = features.shape[-1]
    slots = sum(relation[0].shape[0] for relation in relations)
    blocks = jax.ShapeDtypeStruct((16, 3 * TILE, width), BF16)
    features = features.reshape(-1, TILE, width)
    return pl.pallas_call(
        gather_kernel,
        out_shape=(blocks, blocks),
        in_specs=[spec(SMEM)] * 10 + [spec(ANY)] * 4,
        out_specs=(spec(VMEM), spec(VMEM)),
        scratch_shapes=[
            pltpu.VMEM((slots, TILE, TILE), BF16),
            pltpu.VMEM(features.shape, BF16),
            pltpu.VMEM((97, TILE, width), F32),
            pltpu.SMEM((32,), jnp.int32),
            pltpu.SemaphoreType.DMA((slots // GROUP,)),
            pltpu.SemaphoreType.DMA(()),
        ],
        compiler_params=pltpu.CompilerParams(vmem_limit_bytes=GATHER_LIMIT),
        cost_estimate=pl.CostEstimate(
            flops=3 * 10**9, bytes_accessed=18 * 10**6, transcendentals=0
        ),
        name="gather_sums",
    )(*flat_args(owner_map, relations), in_hbm(features), *tile_args(relations))


def plan_kernel(
    owner_map,
    targets0, targets1, targets2, sources0, sources1, sources2, counts0, counts1, counts2,
    pair_a, pair_b, pair_spot, amount,
    table, pending,
    *, blank,
):
    targets, sources = (targets0, targets1, targets2), (sources0, sources1, sources2)
    counts = (counts0, counts1, counts2)
    begins = live_parts(counts)[1]
    mine = here()

    def fill(slot, carry):
        first, second, away = place_of(slot, mine)
        table[owner_map[slot]] = (away * 16 + second * SIDE + first) * 3
        return carry

    lax.fori_loop(0, 32, fill, 0)
    for spot in range(17):
        pending[spot] = -1

    def put(found, a, b, spot, yes):
        pair_a[found] = a
        pair_b[found] = b
        pair_spot[found] = spot
        return found + jnp.where(yes, 1, 0)

    found = jnp.int32(0)
    for number in range(3):
        def match(group, found, number=number):
            for lane in range(GROUP):
                j = group * GROUP + lane
                live = j < counts[number][0]
                code = begins[number] * GROUP + j + (table[targets[number][j]] + number) * 1024
                spot = jnp.where(live, sources[number][j], 16)
                waiting = pending[spot]
                hit = live & (waiting >= 0)
                found = put(found, waiting, code, spot, hit)
                pending[spot] = jnp.where(hit, -1, code)
            return found

        found = lax.fori_loop(0, (counts[number][0] + GROUP - 1) // GROUP, match, found)
    for spot in range(16):
        found = put(found, pending[spot], blank, spot, pending[spot] >= 0)
    for lane in range(PAIRS):
        put(found + lane, blank, blank, 16, False)
    amount[0] = found


def plan_spread(owner_map, relations):
    slots = sum(relation[0].shape[0] for relation in relations)
    pairs = jax.ShapeDtypeStruct((slots // 2 + 16 + 2 * PAIRS,), jnp.int32)
    return pl.pallas_call(
        functools.partial(plan_kernel, blank=slots),
        out_shape=(pairs, pairs, pairs, jax.ShapeDtypeStruct((1,), jnp.int32)),
        in_specs=[spec(SMEM)] * 10,
        out_specs=tuple([spec(SMEM)] * 4),
        scratch_shapes=[pltpu.SMEM((32,), jnp.int32), pltpu.SMEM((17,), jnp.int32)],
        compiler_params=pltpu.CompilerParams(vmem_limit_bytes=MIB),
        cost_estimate=pl.CostEstimate(flops=10**9, bytes_accessed=10**6, transcendentals=0),
        name="plan_spread",
    )(*flat_args(owner_map, relations))


PLACES = (0, 8, 12, 4, 16, 24, 28, 20)
FAR = (3, 5, 6, 7)


def spread_kernel(pair_a, pair_b, pair_spot, amount, *refs):
    counts, tiles, pieces, refs = refs[:3], refs[3:6], refs[6:14], refs[14:]
    out, buffer, messages, total, tile_sems, piece_sems = refs
    copies = [
        pltpu.make_async_copy(
            pieces[number], messages.at[pl.ds(PLACES[number] * 3, 12)], piece_sems.at[sem]
        )
        for sem, number in enumerate(FAR)
    ]
    for copy in copies:
        copy.start()
    begins = start_tiles(tiles, counts, buffer, tile_sems)

    def place(block, carry):
        for number, (piece, at) in enumerate(zip(pieces, PLACES)):
            if number not in FAR:
                messages[at * 3 + block] = piece[block]
        return carry

    lax.fori_loop(0, 12, place, 0)
    blank = buffer.shape[0] - 1
    buffer[blank] = jnp.zeros((TILE, TILE), BF16)
    clear(total, 16)
    for copy in copies:
        copy.wait()

    def add_group(group, waited):
        at = group * PAIRS
        needed = jnp.minimum(((pair_b[at + PAIRS - 1] & 1023) >> 4) + 1, begins[3])
        waited = wait_tiles(tiles[0], buffer, tile_sems, waited, needed)
        products = []
        for lane in range(PAIRS):
            marks = (pair_a[at + lane], pair_b[at + lane])
            tile = jnp.concatenate([buffer[mark & 1023] for mark in marks], axis=0)
            block = jnp.concatenate([messages[mark >> 10] for mark in marks], axis=0)
            products.append(
                lax.dot_general(
                    tile, block, (((0,), (0,)), ((), ())), preferred_element_type=F32
                )
            )
        for lane in range(PAIRS):
            total[pair_spot[at + lane]] += products[lane]
        return waited

    waited = lax.fori_loop(0, (amount[0] + PAIRS - 1) // PAIRS, add_group, jnp.int32(0))
    wait_tiles(tiles[0], buffer, tile_sems, waited, begins[3])

    def emit(block, carry):
        out[block] = total[block].astype(out.dtype)
        return carry

    lax.fori_loop(0, 16, emit, 0)


def spread_sums(plan, relations, pieces):
    width = pieces[0].shape[-1]
    slots = sum(relation[0].shape[0] for relation in relations)
    return pl.pallas_call(
        spread_kernel,
        out_shape=jax.ShapeDtypeStruct((16, TILE, width), BF16),
        in_specs=[spec(SMEM)] * 7
        + [spec(ANY)] * 3
        + [spec(ANY if number in FAR else VMEM) for number in range(8)],
        out_specs=spec(VMEM),
        scratch_shapes=[
            pltpu.VMEM((slots + 1, TILE, TILE), BF16),
            pltpu.VMEM((96, TILE, width), BF16),
            pltpu.VMEM((17, TILE, width), F32),
            pltpu.SemaphoreType.DMA((slots // GROUP,)),
            pltpu.SemaphoreType.DMA((len(FAR),)),
        ],
        compiler_params=pltpu.CompilerParams(vmem_limit_bytes=SPREAD_LIMIT),
        cost_estimate=pl.CostEstimate(
            flops=3 * 10**9, bytes_accessed=18 * 10**6, transcendentals=0
        ),
        name="spread_sums",
    )(
        *plan,
        *[relation[3] for relation in relations],
        *tile_args(relations),
        *[in_hbm(piece) if number in FAR else piece for number, piece in enumerate(pieces)],
    )


def columns_at(step, width):
    column = (lax.axis_index("tgt") + step) % SIDE
    return pl.ds(pl.multiple_of(column * width, width), width)


def hidden_kernel(part0, part1, part2, part3, weights, rounded, terms0, terms1, terms2, terms3):
    width = part0.shape[1]
    whole = part0[...].astype(F32)
    for part in (part1, part2, part3):
        whole = whole + part[...].astype(F32)
    whole = whole.astype(BF16)
    rounded[...] = whole
    for step, terms in ((2, terms2), (1, terms1), (3, terms3), (0, terms0)):
        value = jnp.zeros(terms.shape, F32)
        for number in range(3):
            value += jnp.dot(
                whole[number * TILE:(number + 1) * TILE],
                weights[number, :, columns_at(step, width)],
                preferred_element_type=F32,
            )
        terms[...] = value.astype(terms.dtype)


def hidden_terms(parts, weights):
    width = parts[0].shape[1]
    return pl.pallas_call(
        hidden_kernel,
        out_shape=(
            jax.ShapeDtypeStruct((3 * TILE, width), BF16),
            jax.ShapeDtypeStruct((TILE, width), F32),
            jax.ShapeDtypeStruct((TILE, width), BF16),
            jax.ShapeDtypeStruct((TILE, width), BF16),
            jax.ShapeDtypeStruct((TILE, width), BF16),
        ),
        in_specs=[spec(VMEM)] * 5,
        out_specs=tuple([spec(VMEM)] * 5),
        compiler_params=pltpu.CompilerParams(vmem_limit_bytes=8 * MIB),
        name="hidden_terms",
    )(*parts, weights)


def message_kernel(grad0, grad1, grad2, grad3, weights, messages):
    width = grad0.shape[1]
    for number in range(3):
        value = jnp.zeros((TILE, width), F32)
        for step, grad in enumerate((grad0, grad1, grad2, grad3)):
            value += lax.dot_general(
                grad[...],
                weights[number, :, columns_at(step, width)],
                (((1,), (1,)), ((), ())),
                preferred_element_type=F32,
            )
        messages[number] = value.astype(BF16)


def form_messages(grads, weights):
    width = grads[0].shape[1]
    return pl.pallas_call(
        message_kernel,
        out_shape=jax.ShapeDtypeStruct((3, TILE, width), BF16),
        in_specs=[spec(VMEM)] * 5,
        out_specs=spec(VMEM),
        compiler_params=pltpu.CompilerParams(vmem_limit_bytes=8 * MIB),
        name="form_messages",
    )(*grads, weights)


def weight_kernel(grad0, grad1, grad2, grad3, rounded, keep, send, staged, sems):
    mine = here()
    block0 = lax.axis_index("tgt")
    values = jnp.concatenate(
        [rounded[number * TILE:(number + 1) * TILE, :] for number in range(3)], axis=1
    )
    for step, grad in enumerate((grad0, grad1, grad2, grad3)):
        turned = grad[...].astype(F32).T.astype(BF16)
        block = (block0 + step) % SIDE
        for part in range(8):
            first, second, away = place_of(block * 8 + part, mine)
            spot = away * 16 + second * SIDE + first
            value = jnp.dot(
                turned[part * 32:(part + 1) * 32], values, preferred_element_type=F32
            ).astype(BF16)
            for column in range(values.shape[1] // TILE):
                staged[spot, pl.ds(column * 32, 32), :] = value[
                    :, column * TILE:(column + 1) * TILE
                ]
    copies = [
        pltpu.make_async_copy(staged.at[pl.ds(16, 16)], send, sems.at[0]),
        pltpu.make_async_copy(staged.at[pl.ds(0, 16)], keep, sems.at[1]),
    ]
    for copy in copies:
        copy.start()
    for copy in copies:
        copy.wait()


def weight_terms(grads, rounded):
    width = grads[0].shape[1]
    rows = 32 * 3 * width // TILE
    blocks = jax.ShapeDtypeStruct((16, rows, TILE), BF16)
    return pl.pallas_call(
        weight_kernel,
        out_shape=(blocks, blocks),
        in_specs=[spec(VMEM)] * 5,
        out_specs=(spec(ANY), spec(ANY)),
        scratch_shapes=[
            pltpu.VMEM((32, rows, TILE), BF16),
            pltpu.SemaphoreType.DMA((2,)),
        ],
        compiler_params=pltpu.CompilerParams(vmem_limit_bytes=8 * MIB),
        cost_estimate=pl.CostEstimate(flops=10**9, bytes_accessed=3 * 10**6, transcendentals=0),
        name="weight_terms",
    )(*grads, rounded)


def shift_pairs(step, second):
    pairs = []
    for s in range(32):
        x, z, c = s // 8, (s // 2) % 4, s % 2
        if (c == 0) != second:
            x = (x + step) % SIDE
        else:
            z = (z + step) % SIDE
        pairs.append((s, (x * SIDE + z) * 2 + c))
    return pairs


def shift(value, step, second=False):
    return lax.ppermute(value, "src", shift_pairs(step, second))


def swap(value):
    return lax.ppermute(value, "src", [(s, s ^ 1) for s in range(32)])


def add(*values):
    total = values[0].astype(F32)
    for value in values[1:]:
        total = total + value.astype(F32)
    return total.astype(BF16)


def three_starts(values, second=False):
    arrived = []
    for k in (2, 1, 3):
        arrived.append(shift(values[k], k if k < 3 else -1, second))
    return tuple(arrived)


def three_ways(values, second=False):
    return barrier(three_starts(values, second))


def turn(value, step):
    return lax.ppermute(value, "tgt", [(t, (t + step) % SIDE) for t in range(SIDE)])


def shards(
    features,
    cites_tiles,
    cites_targets,
    cites_sources,
    cites_counts,
    writes_tiles,
    writes_targets,
    writes_sources,
    writes_counts,
    topic_tiles,
    topic_targets,
    topic_sources,
    topic_counts,
    owner_map,
    weights,
    bias_row,
    cotangent,
):
    width = features.shape[1]
    relations = (
        (cites_tiles, cites_targets, cites_sources, cites_counts),
        (writes_tiles, writes_targets, writes_sources, writes_counts),
        (topic_tiles, topic_targets, topic_sources, topic_counts),
    )
    keep, send = gather_sums(owner_map, relations, features)
    got = swap(send)
    quarters = [add(keep[4 * k:4 * k + 4], got[4 * k:4 * k + 4]) for k in range(4)]
    owner_map, *quarters = barrier((owner_map, *quarters))
    arrived = three_ways(quarters)
    plan = plan_spread(owner_map, relations)
    *plan, a0, a1, a2 = barrier((*plan, *arrived))
    line = [add(quarters[0][k], *[part[k] for part in (a0, a1, a2)]) for k in range(4)]
    parts = (line[0], *three_ways(line, True))

    rounded, terms0, terms1, terms2, terms3 = hidden_terms(parts, weights)
    turned = barrier((turn(terms2, 2), turn(terms1, 1), turn(terms3, 3)))
    hidden = terms0 + bias_row.astype(F32)[None, :]
    for part in turned:
        hidden = hidden + part.astype(F32)
    mixed_out, pullback = jax.vjp(functools.partial(jax.nn.gelu, approximate=True), hidden)
    grad_hidden = pullback(cotangent.astype(F32))[0].astype(BF16)
    two, one, three = barrier(
        (turn(grad_hidden, -2), turn(grad_hidden, -1), turn(grad_hidden, -3))
    )
    grads = [grad_hidden, one, two, three]

    own = form_messages(grads, weights)
    own, *grads = barrier((own, *grads))
    two, three, one = barrier(three_starts((own,) * 4))
    weight_keep, weight_send = weight_terms(grads, rounded)
    weight_got = swap(weight_send)
    quarters = [
        add(weight_keep[4 * k:4 * k + 4], weight_got[4 * k:4 * k + 4]) for k in range(4)
    ]
    arrived = barrier(three_starts(quarters, True))
    whole = jnp.concatenate([own, one, two, three])
    spread_out = three_starts((whole,) * 4, True)
    beside = swap(whole)
    line = [add(quarters[0][k], *[part[k] for part in arrived]) for k in range(4)]
    weight_parts = three_ways(line)
    *spread_out, beside, l0, w0, w1, w2 = barrier((*spread_out, beside, line[0], *weight_parts))
    weight_parts = (w0, w1, w2)
    siblings = [swap(piece) for piece in spread_out]
    grad_source = spread_sums(plan, relations, [whole, *spread_out, beside, *siblings])
    weight_sum = l0.astype(F32)
    for part in weight_parts:
        weight_sum = weight_sum + part.astype(F32)
    grad_weight = weight_sum.reshape(3 * width // TILE, 32, TILE).transpose(0, 2, 1)
    return (
        mixed_out.astype(BF16),
        grad_weight.reshape(3, width, 32),
        grad_source.reshape(-1, width),
    )


def solution(mesh):
    in_specs = (
        P("src", "tgt"),
        P("src", None, None),
        P("src"),
        P("src"),
        P("src"),
        P("src", None, None),
        P("src"),
        P("src"),
        P("src"),
        P("src", None, None),
        P("src"),
        P("src"),
        P("src"),
        P(),
        P(None, "tgt", None),
        P("tgt"),
        P("src", "tgt"),
    )
    out_specs = (P("src", "tgt"), P(None, "tgt", "src"), P("src", "tgt"))

    return jax.shard_map(shards, mesh=mesh, in_specs=in_specs, out_specs=out_specs, check_vma=False)
```

```python
import functools

import jax
import jax.numpy as jnp
from jax import lax
from jax.experimental import pallas as pl
from jax.experimental.pallas import tpu as pltpu
from jax.sharding import PartitionSpec as P


TILE = 128
SIDE = 4
GROUP = 16
PAIRS = 16
BF16 = jnp.bfloat16
F32 = jnp.float32
MIB = 1024 * 1024
GATHER_LIMIT = 36 * MIB
SPREAD_LIMIT = 28 * MIB
barrier = lax.optimization_barrier


def spec(space):
    return pl.BlockSpec(memory_space=space)


ANY, SMEM, VMEM = pl.ANY, pltpu.SMEM, pltpu.VMEM


def here():
    s = lax.axis_index("src")
    return s >> 3, (s >> 1) & 3, s & 1


def place_of(slot, mine):
    c = slot & 1
    dx = ((slot >> 3) - mine[0]) & 3
    dz = ((slot >> 1) - mine[1]) & 3
    first = jnp.where(c == 0, dx, dz)
    second = jnp.where(c == 0, dz, dx)
    return first, second, c ^ mine[2]


def live_parts(counts):
    parts = [(count[0] + GROUP - 1) // GROUP for count in counts]
    return parts, [0, parts[0], parts[0] + parts[1], parts[0] + parts[1] + parts[2]]


def start_tiles(tiles, counts, buffer, sems):
    parts, begins = live_parts(counts)
    for number in range(3):
        def step(part, carry, number=number):
            at = begins[number] + part
            pltpu.make_async_copy(
                tiles[number].at[pl.ds(part * GROUP, GROUP)],
                buffer.at[pl.ds(at * GROUP, GROUP)],
                sems.at[at],
            ).start()
            return carry

        lax.fori_loop(0, parts[number], step, 0)
    return begins


def wait_tiles(tile, buffer, sems, waited, needed):
    def step(at, carry):
        pltpu.make_async_copy(
            tile.at[pl.ds(0, GROUP)], buffer.at[pl.ds(at * GROUP, GROUP)], sems.at[at]
        ).wait()
        return carry

    lax.fori_loop(waited, needed, step, 0)
    return jnp.maximum(waited, needed)


def clear(total, amount, begin=0):
    def step(block, carry):
        total[block] = jnp.zeros(total.shape[1:], F32)
        return carry

    lax.fori_loop(begin, amount, step, 0)


def gather_list(codes, amount, features, buffer, total, ready):
    def add_group(group, waited):
        waited = ready(waited, codes[jnp.minimum(group * GROUP + GROUP, amount) - 1] & 1023)
        marks = [codes[group * GROUP + lane] for lane in range(GROUP)]
        products = [
            jnp.dot(
                buffer[mark & 1023], features[(mark >> 10) & 15], preferred_element_type=F32
            )
            for mark in marks
        ]
        for mark, product in zip(marks, products):
            total[mark >> 14] += product
        return waited

    return lax.fori_loop(0, (amount + GROUP - 1) // GROUP, add_group, jnp.int32(0))


def emit_blocks(total, target):
    def emit(spot, carry):
        for number in range(3):
            target[spot, pl.ds(number * TILE, TILE), :] = total[spot * 3 + number].astype(BF16)
        return carry

    lax.fori_loop(0, 16, emit, 0)


def gather_send_kernel(
    owner_map,
    targets0, targets1, targets2, sources0, sources1, sources2, counts0, counts1, counts2,
    features, tiles0, tiles1, tiles2,
    send, keep_codes, keep_amount, buffer, held,
    total, table, send_codes, tile_sems, feature_sem,
):
    targets, sources = (targets0, targets1, targets2), (sources0, sources1, sources2)
    counts, tiles = (counts0, counts1, counts2), (tiles0, tiles1, tiles2)
    feature_copy = pltpu.make_async_copy(features, held, feature_sem)
    feature_copy.start()
    begins = start_tiles(tiles, counts, buffer, tile_sems)
    mine = here()

    def fill(slot, carry):
        first, second, away = place_of(slot, mine)
        table[owner_map[slot]] = (first * SIDE + second) * 3 + away * 128
        total[slot] = jnp.zeros(total.shape[1:], F32)
        return carry

    lax.fori_loop(0, 32, fill, 0)
    clear(total, 48, 32)

    sent, kept = jnp.int32(0), jnp.int32(0)
    for number in range(3):
        def sort(group, carry, number=number):
            sent, kept = carry
            for lane in range(GROUP):
                j = group * GROUP + lane
                spot = table[targets[number][j]]
                code = (
                    (begins[number] * GROUP + j)
                    + sources[number][j] * 1024
                    + ((spot & 127) + number) * 16384
                )
                send_codes[sent] = code
                keep_codes[kept] = code
                live = jnp.where(j < counts[number][0], 1, 0)
                away = live & (spot >> 7)
                sent, kept = sent + away, kept + (live - away)
            return sent, kept

        sent, kept = lax.fori_loop(
            0, (counts[number][0] + GROUP - 1) // GROUP, sort, (sent, kept)
        )
    for lane in range(GROUP):
        send_codes[sent + lane] = 48 * 16384
        keep_codes[kept + lane] = 48 * 16384
    keep_amount[0] = kept
    feature_copy.wait()

    def ready(waited, last):
        return wait_tiles(tiles[0], buffer, tile_sems, waited, (last >> 4) + 1)

    waited = gather_list(send_codes, sent, held, buffer, total, ready)
    wait_tiles(tiles[0], buffer, tile_sems, waited, begins[3])
    emit_blocks(total, send)


def gather_keep_kernel(codes, amount, buffer, held, keep, total):
    clear(total, 48)
    gather_list(codes, amount[0], held, buffer, total, lambda waited, last: waited)
    emit_blocks(total, keep)


def in_hbm(value):
    return pltpu.with_memory_space_constraint(value, pltpu.HBM)


def flat_args(owner_map, relations):
    return (
        in_hbm(owner_map),
        *[in_hbm(relation[1]) for relation in relations],
        *[in_hbm(relation[2]) for relation in relations],
        *[relation[3] for relation in relations],
    )


def tile_args(relations):
    return [in_hbm(relation[0]) for relation in relations]


def gather_sums(owner_map, relations, features):
    width = features.shape[-1]
    slots = sum(relation[0].shape[0] for relation in relations)
    blocks = jax.ShapeDtypeStruct((16, 3 * TILE, width), BF16)
    features = features.reshape(-1, TILE, width)
    total = pltpu.VMEM((49, TILE, width), F32)
    common = dict(
        compiler_params=pltpu.CompilerParams(vmem_limit_bytes=GATHER_LIMIT),
        cost_estimate=pl.CostEstimate(
            flops=2 * 10**9, bytes_accessed=12 * 10**6, transcendentals=0
        ),
    )
    send, codes, amount, buffer, held = pl.pallas_call(
        gather_send_kernel,
        out_shape=(
            blocks,
            jax.ShapeDtypeStruct((slots + GROUP,), jnp.int32),
            jax.ShapeDtypeStruct((1,), jnp.int32),
            jax.ShapeDtypeStruct((slots, TILE, TILE), BF16),
            jax.ShapeDtypeStruct(features.shape, BF16),
        ),
        in_specs=[spec(SMEM)] * 10 + [spec(ANY)] * 4,
        out_specs=(spec(VMEM), spec(SMEM), spec(SMEM), spec(VMEM), spec(VMEM)),
        scratch_shapes=[
            total,
            pltpu.SMEM((32,), jnp.int32),
            pltpu.SMEM((slots + GROUP,), jnp.int32),
            pltpu.SemaphoreType.DMA((slots // GROUP,)),
            pltpu.SemaphoreType.DMA(()),
        ],
        name="gather_send",
        **common,
    )(*flat_args(owner_map, relations), in_hbm(features), *tile_args(relations))
    keep = pl.pallas_call(
        gather_keep_kernel,
        out_shape=blocks,
        in_specs=[spec(SMEM)] * 2 + [spec(VMEM)] * 2,
        out_specs=spec(VMEM),
        scratch_shapes=[total],
        name="gather_keep",
        **common,
    )(codes, amount, buffer, held)
    return keep, send


def plan_kernel(
    owner_map,
    targets0, targets1, targets2, sources0, sources1, sources2, counts0, counts1, counts2,
    pair_a, pair_b, pair_spot, amount,
    table, pending,
    *, blank,
):
    targets, sources = (targets0, targets1, targets2), (sources0, sources1, sources2)
    counts = (counts0, counts1, counts2)
    begins = live_parts(counts)[1]
    mine = here()

    def fill(slot, carry):
        first, second, away = place_of(slot, mine)
        table[owner_map[slot]] = (away * 16 + second * SIDE + first) * 3
        return carry

    lax.fori_loop(0, 32, fill, 0)
    for spot in range(17):
        pending[spot] = -1

    def put(found, a, b, spot, yes):
        pair_a[found] = a
        pair_b[found] = b
        pair_spot[found] = spot
        return found + jnp.where(yes, 1, 0)

    found = jnp.int32(0)
    for number in range(3):
        def match(group, found, number=number):
            for lane in range(GROUP):
                j = group * GROUP + lane
                live = j < counts[number][0]
                code = begins[number] * GROUP + j + (table[targets[number][j]] + number) * 1024
                spot = jnp.where(live, sources[number][j], 16)
                waiting = pending[spot]
                hit = live & (waiting >= 0)
                found = put(found, waiting, code, spot, hit)
                pending[spot] = jnp.where(hit, -1, code)
            return found

        found = lax.fori_loop(0, (counts[number][0] + GROUP - 1) // GROUP, match, found)
    for spot in range(16):
        found = put(found, pending[spot], blank, spot, pending[spot] >= 0)
    for lane in range(PAIRS):
        put(found + lane, blank, blank, 16, False)
    amount[0] = found


def plan_spread(owner_map, relations):
    slots = sum(relation[0].shape[0] for relation in relations)
    pairs = jax.ShapeDtypeStruct((slots // 2 + 16 + 2 * PAIRS,), jnp.int32)
    return pl.pallas_call(
        functools.partial(plan_kernel, blank=slots),
        out_shape=(pairs, pairs, pairs, jax.ShapeDtypeStruct((1,), jnp.int32)),
        in_specs=[spec(SMEM)] * 10,
        out_specs=tuple([spec(SMEM)] * 4),
        scratch_shapes=[pltpu.SMEM((32,), jnp.int32), pltpu.SMEM((17,), jnp.int32)],
        compiler_params=pltpu.CompilerParams(vmem_limit_bytes=MIB),
        cost_estimate=pl.CostEstimate(flops=10**9, bytes_accessed=10**6, transcendentals=0),
        name="plan_spread",
    )(*flat_args(owner_map, relations))


PLACES = (0, 8, 12, 4, 16, 24, 28, 20)
FAR = (3, 5, 6, 7)


def spread_kernel(pair_a, pair_b, pair_spot, amount, *refs):
    counts, tiles, pieces, refs = refs[:3], refs[3:6], refs[6:14], refs[14:]
    out, buffer, messages, total, tile_sems, piece_sems = refs
    copies = [
        pltpu.make_async_copy(
            pieces[number], messages.at[pl.ds(PLACES[number] * 3, 12)], piece_sems.at[sem]
        )
        for sem, number in enumerate(FAR)
    ]
    for copy in copies:
        copy.start()
    begins = start_tiles(tiles, counts, buffer, tile_sems)

    def place(block, carry):
        for number, (piece, at) in enumerate(zip(pieces, PLACES)):
            if number not in FAR:
                messages[at * 3 + block] = piece[block]
        return carry

    lax.fori_loop(0, 12, place, 0)
    blank = buffer.shape[0] - 1
    buffer[blank] = jnp.zeros((TILE, TILE), BF16)
    clear(total, 16)
    for copy in copies:
        copy.wait()

    def add_group(group, waited):
        at = group * PAIRS
        needed = jnp.minimum(((pair_b[at + PAIRS - 1] & 1023) >> 4) + 1, begins[3])
        waited = wait_tiles(tiles[0], buffer, tile_sems, waited, needed)
        products = []
        for lane in range(PAIRS):
            marks = (pair_a[at + lane], pair_b[at + lane])
            tile = jnp.concatenate([buffer[mark & 1023] for mark in marks], axis=0)
            block = jnp.concatenate([messages[mark >> 10] for mark in marks], axis=0)
            products.append(
                lax.dot_general(
                    tile, block, (((0,), (0,)), ((), ())), preferred_element_type=F32
                )
            )
        for lane in range(PAIRS):
            total[pair_spot[at + lane]] += products[lane]
        return waited

    waited = lax.fori_loop(0, (amount[0] + PAIRS - 1) // PAIRS, add_group, jnp.int32(0))
    wait_tiles(tiles[0], buffer, tile_sems, waited, begins[3])

    def emit(block, carry):
        out[block] = total[block].astype(out.dtype)
        return carry

    lax.fori_loop(0, 16, emit, 0)


def spread_sums(plan, relations, pieces):
    width = pieces[0].shape[-1]
    slots = sum(relation[0].shape[0] for relation in relations)
    return pl.pallas_call(
        spread_kernel,
        out_shape=jax.ShapeDtypeStruct((16, TILE, width), BF16),
        in_specs=[spec(SMEM)] * 7
        + [spec(ANY)] * 3
        + [spec(ANY if number in FAR else VMEM) for number in range(8)],
        out_specs=spec(VMEM),
        scratch_shapes=[
            pltpu.VMEM((slots + 1, TILE, TILE), BF16),
            pltpu.VMEM((96, TILE, width), BF16),
            pltpu.VMEM((17, TILE, width), F32),
            pltpu.SemaphoreType.DMA((slots // GROUP,)),
            pltpu.SemaphoreType.DMA((len(FAR),)),
        ],
        compiler_params=pltpu.CompilerParams(vmem_limit_bytes=SPREAD_LIMIT),
        cost_estimate=pl.CostEstimate(
            flops=3 * 10**9, bytes_accessed=18 * 10**6, transcendentals=0
        ),
        name="spread_sums",
    )(
        *plan,
        *[relation[3] for relation in relations],
        *tile_args(relations),
        *[in_hbm(piece) if number in FAR else piece for number, piece in enumerate(pieces)],
    )


def columns_at(step, width):
    column = (lax.axis_index("tgt") + step) % SIDE
    return pl.ds(pl.multiple_of(column * width, width), width)


def hidden_kernel(part0, part1, part2, part3, weights, rounded, terms0, terms1, terms2, terms3):
    width = part0.shape[1]
    whole = part0[...].astype(F32)
    for part in (part1, part2, part3):
        whole = whole + part[...].astype(F32)
    whole = whole.astype(BF16)
    rounded[...] = whole
    for step, terms in ((2, terms2), (1, terms1), (3, terms3), (0, terms0)):
        value = jnp.zeros(terms.shape, F32)
        for number in range(3):
            value += jnp.dot(
                whole[number * TILE:(number + 1) * TILE],
                weights[number, :, columns_at(step, width)],
                preferred_element_type=F32,
            )
        terms[...] = value.astype(terms.dtype)


def hidden_terms(parts, weights):
    width = parts[0].shape[1]
    return pl.pallas_call(
        hidden_kernel,
        out_shape=(
            jax.ShapeDtypeStruct((3 * TILE, width), BF16),
            jax.ShapeDtypeStruct((TILE, width), F32),
            jax.ShapeDtypeStruct((TILE, width), BF16),
            jax.ShapeDtypeStruct((TILE, width), BF16),
            jax.ShapeDtypeStruct((TILE, width), BF16),
        ),
        in_specs=[spec(VMEM)] * 5,
        out_specs=tuple([spec(VMEM)] * 5),
        compiler_params=pltpu.CompilerParams(vmem_limit_bytes=8 * MIB),
        name="hidden_terms",
    )(*parts, weights)


def message_kernel(grad0, grad1, grad2, grad3, weights, messages):
    width = grad0.shape[1]
    for number in range(3):
        value = jnp.zeros((TILE, width), F32)
        for step, grad in enumerate((grad0, grad1, grad2, grad3)):
            value += lax.dot_general(
                grad[...],
                weights[number, :, columns_at(step, width)],
                (((1,), (1,)), ((), ())),
                preferred_element_type=F32,
            )
        messages[number] = value.astype(BF16)


def form_messages(grads, weights):
    width = grads[0].shape[1]
    return pl.pallas_call(
        message_kernel,
        out_shape=jax.ShapeDtypeStruct((3, TILE, width), BF16),
        in_specs=[spec(VMEM)] * 5,
        out_specs=spec(VMEM),
        compiler_params=pltpu.CompilerParams(vmem_limit_bytes=8 * MIB),
        name="form_messages",
    )(*grads, weights)


def weight_kernel(grad0, grad1, grad2, grad3, rounded, keep, send, staged, sems):
    mine = here()
    block0 = lax.axis_index("tgt")
    values = jnp.concatenate(
        [rounded[number * TILE:(number + 1) * TILE, :] for number in range(3)], axis=1
    )
    for step, grad in enumerate((grad0, grad1, grad2, grad3)):
        turned = grad[...].astype(F32).T.astype(BF16)
        block = (block0 + step) % SIDE
        for part in range(8):
            first, second, away = place_of(block * 8 + part, mine)
            spot = away * 16 + second * SIDE + first
            value = jnp.dot(
                turned[part * 32:(part + 1) * 32], values, preferred_element_type=F32
            ).astype(BF16)
            for column in range(values.shape[1] // TILE):
                staged[spot, pl.ds(column * 32, 32), :] = value[
                    :, column * TILE:(column + 1) * TILE
                ]
    copies = [
        pltpu.make_async_copy(staged.at[pl.ds(16, 16)], send, sems.at[0]),
        pltpu.make_async_copy(staged.at[pl.ds(0, 16)], keep, sems.at[1]),
    ]
    for copy in copies:
        copy.start()
    for copy in copies:
        copy.wait()


def weight_terms(grads, rounded):
    width = grads[0].shape[1]
    rows = 32 * 3 * width // TILE
    blocks = jax.ShapeDtypeStruct((16, rows, TILE), BF16)
    return pl.pallas_call(
        weight_kernel,
        out_shape=(blocks, blocks),
        in_specs=[spec(VMEM)] * 5,
        out_specs=(spec(ANY), spec(ANY)),
        scratch_shapes=[
            pltpu.VMEM((32, rows, TILE), BF16),
            pltpu.SemaphoreType.DMA((2,)),
        ],
        compiler_params=pltpu.CompilerParams(vmem_limit_bytes=8 * MIB),
        cost_estimate=pl.CostEstimate(flops=10**9, bytes_accessed=3 * 10**6, transcendentals=0),
        name="weight_terms",
    )(*grads, rounded)


def shift_pairs(step, second):
    pairs = []
    for s in range(32):
        x, z, c = s // 8, (s // 2) % 4, s % 2
        if (c == 0) != second:
            x = (x + step) % SIDE
        else:
            z = (z + step) % SIDE
        pairs.append((s, (x * SIDE + z) * 2 + c))
    return pairs


def shift(value, step, second=False):
    return lax.ppermute(value, "src", shift_pairs(step, second))


def swap(value):
    return lax.ppermute(value, "src", [(s, s ^ 1) for s in range(32)])


def add(*values):
    total = values[0].astype(F32)
    for value in values[1:]:
        total = total + value.astype(F32)
    return total.astype(BF16)


def three_starts(values, second=False):
    arrived = []
    for k in (2, 1, 3):
        arrived.append(shift(values[k], k if k < 3 else -1, second))
    return tuple(arrived)


def three_ways(values, second=False):
    return barrier(three_starts(values, second))


def turn(value, step):
    return lax.ppermute(value, "tgt", [(t, (t + step) % SIDE) for t in range(SIDE)])


def shards(
    features,
    cites_tiles,
    cites_targets,
    cites_sources,
    cites_counts,
    writes_tiles,
    writes_targets,
    writes_sources,
    writes_counts,
    topic_tiles,
    topic_targets,
    topic_sources,
    topic_counts,
    owner_map,
    weights,
    bias_row,
    cotangent,
):
    width = features.shape[1]
    relations = (
        (cites_tiles, cites_targets, cites_sources, cites_counts),
        (writes_tiles, writes_targets, writes_sources, writes_counts),
        (topic_tiles, topic_targets, topic_sources, topic_counts),
    )
    keep, send = gather_sums(owner_map, relations, features)
    got = swap(send)
    quarters = [add(keep[4 * k:4 * k + 4], got[4 * k:4 * k + 4]) for k in range(4)]
    owner_map, *quarters = barrier((owner_map, *quarters))
    arrived = three_ways(quarters)
    plan = plan_spread(owner_map, relations)
    *plan, a0, a1, a2 = barrier((*plan, *arrived))
    line = [add(quarters[0][k], *[part[k] for part in (a0, a1, a2)]) for k in range(4)]
    parts = (line[0], *three_ways(line, True))

    rounded, terms0, terms1, terms2, terms3 = hidden_terms(parts, weights)
    turned = barrier((turn(terms2, 2), turn(terms1, 1), turn(terms3, 3)))
    hidden = terms0 + bias_row.astype(F32)[None, :]
    for part in turned:
        hidden = hidden + part.astype(F32)
    mixed_out, pullback = jax.vjp(functools.partial(jax.nn.gelu, approximate=True), hidden)
    grad_hidden = pullback(cotangent.astype(F32))[0].astype(BF16)
    two, one, three = barrier(
        (turn(grad_hidden, -2), turn(grad_hidden, -1), turn(grad_hidden, -3))
    )
    grads = [grad_hidden, one, two, three]

    own = form_messages(grads, weights)
    own, *grads = barrier((own, *grads))
    weight_keep, weight_send = weight_terms(grads, rounded)
    weight_got = swap(weight_send)
    two, three, one = barrier(three_starts((own,) * 4))
    quarters = [
        add(weight_keep[4 * k:4 * k + 4], weight_got[4 * k:4 * k + 4]) for k in range(4)
    ]
    arrived = barrier(three_starts(quarters, True))
    whole = jnp.concatenate([own, one, two, three])
    spread_out = three_starts((whole,) * 4, True)
    beside = swap(whole)
    line = [add(quarters[0][k], *[part[k] for part in arrived]) for k in range(4)]
    weight_parts = three_ways(line)
    *spread_out, beside, l0, w0, w1, w2 = barrier((*spread_out, beside, line[0], *weight_parts))
    weight_parts = (w0, w1, w2)
    siblings = [swap(piece) for piece in spread_out]
    grad_source = spread_sums(plan, relations, [whole, *spread_out, beside, *siblings])
    weight_sum = l0.astype(F32)
    for part in weight_parts:
        weight_sum = weight_sum + part.astype(F32)
    grad_weight = weight_sum.reshape(3 * width // TILE, 32, TILE).transpose(0, 2, 1)
    return (
        mixed_out.astype(BF16),
        grad_weight.reshape(3, width, 32),
        grad_source.reshape(-1, width),
    )


def solution(mesh):
    in_specs = (
        P("src", "tgt"),
        P("src", None, None),
        P("src"),
        P("src"),
        P("src"),
        P("src", None, None),
        P("src"),
        P("src"),
        P("src"),
        P("src", None, None),
        P("src"),
        P("src"),
        P("src"),
        P(),
        P(None, "tgt", None),
        P("tgt"),
        P("src", "tgt"),
    )
    out_specs = (P("src", "tgt"), P(None, "tgt", "src"), P("src", "tgt"))

    return jax.shard_map(shards, mesh=mesh, in_specs=in_specs, out_specs=out_specs, check_vma=False)
```

```python
import functools

import jax
import jax.numpy as jnp
from jax import lax
from jax.experimental import pallas as pl
from jax.experimental.pallas import tpu as pltpu
from jax.sharding import PartitionSpec as P


TILE = 128
SIDE = 4
GROUP = 16
PAIRS = 16
BF16 = jnp.bfloat16
F32 = jnp.float32
MIB = 1024 * 1024
GATHER_LIMIT = 36 * MIB
SPREAD_LIMIT = 28 * MIB
barrier = lax.optimization_barrier


def spec(space):
    return pl.BlockSpec(memory_space=space)


ANY, SMEM, VMEM = pl.ANY, pltpu.SMEM, pltpu.VMEM


def here():
    s = lax.axis_index("src")
    return s >> 3, (s >> 1) & 3, s & 1


def place_of(slot, mine):
    c = slot & 1
    dx = ((slot >> 3) - mine[0]) & 3
    dz = ((slot >> 1) - mine[1]) & 3
    first = jnp.where(c == 0, dx, dz)
    second = jnp.where(c == 0, dz, dx)
    return first, second, c ^ mine[2]


def live_parts(counts):
    parts = [(count[0] + GROUP - 1) // GROUP for count in counts]
    return parts, [0, parts[0], parts[0] + parts[1], parts[0] + parts[1] + parts[2]]


def start_tiles(tiles, counts, buffer, sems):
    parts, begins = live_parts(counts)
    for number in range(3):
        def step(part, carry, number=number):
            at = begins[number] + part
            pltpu.make_async_copy(
                tiles[number].at[pl.ds(part * GROUP, GROUP)],
                buffer.at[pl.ds(at * GROUP, GROUP)],
                sems.at[at],
            ).start()
            return carry

        lax.fori_loop(0, parts[number], step, 0)
    return begins


def wait_tiles(tile, buffer, sems, waited, needed):
    def step(at, carry):
        pltpu.make_async_copy(
            tile.at[pl.ds(0, GROUP)], buffer.at[pl.ds(at * GROUP, GROUP)], sems.at[at]
        ).wait()
        return carry

    lax.fori_loop(waited, needed, step, 0)
    return jnp.maximum(waited, needed)


def clear(total, amount, begin=0):
    def step(block, carry):
        total[block] = jnp.zeros(total.shape[1:], F32)
        return carry

    lax.fori_loop(begin, amount, step, 0)


def gather_list(codes, amount, features, buffer, total, ready):
    def add_group(group, waited):
        waited = ready(waited, codes[jnp.minimum(group * GROUP + GROUP, amount) - 1] & 1023)
        marks = [codes[group * GROUP + lane] for lane in range(GROUP)]
        products = [
            jnp.dot(
                buffer[mark & 1023], features[(mark >> 10) & 15], preferred_element_type=F32
            )
            for mark in marks
        ]
        for mark, product in zip(marks, products):
            total[mark >> 14] += product
        return waited

    return lax.fori_loop(0, (amount + GROUP - 1) // GROUP, add_group, jnp.int32(0))


def emit_blocks(total, target):
    def emit(spot, carry):
        for number in range(3):
            target[spot, pl.ds(number * TILE, TILE), :] = total[spot * 3 + number].astype(BF16)
        return carry

    lax.fori_loop(0, 16, emit, 0)


def gather_send_kernel(
    owner_map,
    targets0, targets1, targets2, sources0, sources1, sources2, counts0, counts1, counts2,
    features, tiles0, tiles1, tiles2,
    send, keep_codes, keep_amount, buffer, held,
    total, table, send_codes, tile_sems, feature_sem,
):
    targets, sources = (targets0, targets1, targets2), (sources0, sources1, sources2)
    counts, tiles = (counts0, counts1, counts2), (tiles0, tiles1, tiles2)
    feature_copy = pltpu.make_async_copy(features, held, feature_sem)
    feature_copy.start()
    begins = start_tiles(tiles, counts, buffer, tile_sems)
    mine = here()

    def fill(slot, carry):
        first, second, away = place_of(slot, mine)
        table[owner_map[slot]] = (first * SIDE + second) * 3 + away * 128
        total[slot] = jnp.zeros(total.shape[1:], F32)
        return carry

    lax.fori_loop(0, 32, fill, 0)
    clear(total, 48, 32)

    sent, kept = jnp.int32(0), jnp.int32(0)
    for number in range(3):
        def sort(group, carry, number=number):
            sent, kept = carry
            for lane in range(GROUP):
                j = group * GROUP + lane
                spot = table[targets[number][j]]
                code = (
                    (begins[number] * GROUP + j)
                    + sources[number][j] * 1024
                    + ((spot & 127) + number) * 16384
                )
                send_codes[sent] = code
                keep_codes[kept] = code
                live = jnp.where(j < counts[number][0], 1, 0)
                away = live & (spot >> 7)
                sent, kept = sent + away, kept + (live - away)
            return sent, kept

        sent, kept = lax.fori_loop(
            0, (counts[number][0] + GROUP - 1) // GROUP, sort, (sent, kept)
        )
    for lane in range(GROUP):
        send_codes[sent + lane] = 48 * 16384
        keep_codes[kept + lane] = 48 * 16384
    keep_amount[0] = kept
    feature_copy.wait()

    def ready(waited, last):
        return wait_tiles(tiles[0], buffer, tile_sems, waited, (last >> 4) + 1)

    waited = gather_list(send_codes, sent, held, buffer, total, ready)
    wait_tiles(tiles[0], buffer, tile_sems, waited, begins[3])
    emit_blocks(total, send)


def gather_keep_kernel(codes, amount, buffer, held, keep, total):
    clear(total, 48)
    gather_list(codes, amount[0], held, buffer, total, lambda waited, last: waited)
    emit_blocks(total, keep)


def in_hbm(value):
    return pltpu.with_memory_space_constraint(value, pltpu.HBM)


def flat_args(owner_map, relations):
    return (
        in_hbm(owner_map),
        *[in_hbm(relation[1]) for relation in relations],
        *[in_hbm(relation[2]) for relation in relations],
        *[relation[3] for relation in relations],
    )


def tile_args(relations):
    return [in_hbm(relation[0]) for relation in relations]


def gather_sums(owner_map, relations, features):
    width = features.shape[-1]
    slots = sum(relation[0].shape[0] for relation in relations)
    blocks = jax.ShapeDtypeStruct((16, 3 * TILE, width), BF16)
    features = features.reshape(-1, TILE, width)
    total = pltpu.VMEM((49, TILE, width), F32)
    common = dict(
        compiler_params=pltpu.CompilerParams(vmem_limit_bytes=GATHER_LIMIT),
        cost_estimate=pl.CostEstimate(
            flops=2 * 10**9, bytes_accessed=12 * 10**6, transcendentals=0
        ),
    )
    send, codes, amount, buffer, held = pl.pallas_call(
        gather_send_kernel,
        out_shape=(
            blocks,
            jax.ShapeDtypeStruct((slots + GROUP,), jnp.int32),
            jax.ShapeDtypeStruct((1,), jnp.int32),
            jax.ShapeDtypeStruct((slots, TILE, TILE), BF16),
            jax.ShapeDtypeStruct(features.shape, BF16),
        ),
        in_specs=[spec(SMEM)] * 10 + [spec(ANY)] * 4,
        out_specs=(spec(VMEM), spec(SMEM), spec(SMEM), spec(VMEM), spec(VMEM)),
        scratch_shapes=[
            total,
            pltpu.SMEM((32,), jnp.int32),
            pltpu.SMEM((slots + GROUP,), jnp.int32),
            pltpu.SemaphoreType.DMA((slots // GROUP,)),
            pltpu.SemaphoreType.DMA(()),
        ],
        name="gather_send",
        **common,
    )(*flat_args(owner_map, relations), in_hbm(features), *tile_args(relations))
    keep = pl.pallas_call(
        gather_keep_kernel,
        out_shape=blocks,
        in_specs=[spec(SMEM)] * 2 + [spec(VMEM)] * 2,
        out_specs=spec(VMEM),
        scratch_shapes=[total],
        name="gather_keep",
        **common,
    )(codes, amount, buffer, held)
    return keep, send


def plan_kernel(
    owner_map,
    targets0, targets1, targets2, sources0, sources1, sources2, counts0, counts1, counts2,
    pair_a, pair_b, pair_spot, amount,
    table, pending,
    *, blank,
):
    targets, sources = (targets0, targets1, targets2), (sources0, sources1, sources2)
    counts = (counts0, counts1, counts2)
    begins = live_parts(counts)[1]
    mine = here()

    def fill(slot, carry):
        first, second, away = place_of(slot, mine)
        table[owner_map[slot]] = (away * 16 + second * SIDE + first) * 3
        return carry

    lax.fori_loop(0, 32, fill, 0)
    for spot in range(17):
        pending[spot] = -1

    def put(found, a, b, spot, yes):
        pair_a[found] = a
        pair_b[found] = b
        pair_spot[found] = spot
        return found + jnp.where(yes, 1, 0)

    found = jnp.int32(0)
    for number in range(3):
        def match(group, found, number=number):
            for lane in range(GROUP):
                j = group * GROUP + lane
                live = j < counts[number][0]
                code = begins[number] * GROUP + j + (table[targets[number][j]] + number) * 1024
                spot = jnp.where(live, sources[number][j], 16)
                waiting = pending[spot]
                hit = live & (waiting >= 0)
                found = put(found, waiting, code, spot, hit)
                pending[spot] = jnp.where(hit, -1, code)
            return found

        found = lax.fori_loop(0, (counts[number][0] + GROUP - 1) // GROUP, match, found)
    for spot in range(16):
        found = put(found, pending[spot], blank, spot, pending[spot] >= 0)
    for lane in range(PAIRS):
        put(found + lane, blank, blank, 16, False)
    amount[0] = found


def plan_spread(owner_map, relations):
    slots = sum(relation[0].shape[0] for relation in relations)
    pairs = jax.ShapeDtypeStruct((slots // 2 + 16 + 2 * PAIRS,), jnp.int32)
    return pl.pallas_call(
        functools.partial(plan_kernel, blank=slots),
        out_shape=(pairs, pairs, pairs, jax.ShapeDtypeStruct((1,), jnp.int32)),
        in_specs=[spec(SMEM)] * 10,
        out_specs=tuple([spec(SMEM)] * 4),
        scratch_shapes=[pltpu.SMEM((32,), jnp.int32), pltpu.SMEM((17,), jnp.int32)],
        compiler_params=pltpu.CompilerParams(vmem_limit_bytes=MIB),
        cost_estimate=pl.CostEstimate(flops=10**9, bytes_accessed=10**6, transcendentals=0),
        name="plan_spread",
    )(*flat_args(owner_map, relations))


PLACES = (0, 8, 12, 4, 16, 24, 28, 20)
FAR = (3, 5, 6, 7)


def spread_kernel(pair_a, pair_b, pair_spot, amount, *refs):
    counts, tiles, pieces, refs = refs[:3], refs[3:6], refs[6:14], refs[14:]
    out, buffer, messages, total, tile_sems, piece_sems = refs
    copies = [
        pltpu.make_async_copy(
            pieces[number], messages.at[pl.ds(PLACES[number] * 3, 12)], piece_sems.at[sem]
        )
        for sem, number in enumerate(FAR)
    ]
    for copy in copies:
        copy.start()
    begins = start_tiles(tiles, counts, buffer, tile_sems)

    def place(block, carry):
        for number, (piece, at) in enumerate(zip(pieces, PLACES)):
            if number not in FAR:
                messages[at * 3 + block] = piece[block]
        return carry

    lax.fori_loop(0, 12, place, 0)
    blank = buffer.shape[0] - 1
    buffer[blank] = jnp.zeros((TILE, TILE), BF16)
    clear(total, 16)
    for copy in copies:
        copy.wait()

    def add_group(group, waited):
        at = group * PAIRS
        needed = jnp.minimum(((pair_b[at + PAIRS - 1] & 1023) >> 4) + 1, begins[3])
        waited = wait_tiles(tiles[0], buffer, tile_sems, waited, needed)
        products = []
        for lane in range(PAIRS):
            marks = (pair_a[at + lane], pair_b[at + lane])
            tile = jnp.concatenate([buffer[mark & 1023] for mark in marks], axis=0)
            block = jnp.concatenate([messages[mark >> 10] for mark in marks], axis=0)
            products.append(
                lax.dot_general(
                    tile, block, (((0,), (0,)), ((), ())), preferred_element_type=F32
                )
            )
        for lane in range(PAIRS):
            total[pair_spot[at + lane]] += products[lane]
        return waited

    waited = lax.fori_loop(0, (amount[0] + PAIRS - 1) // PAIRS, add_group, jnp.int32(0))
    wait_tiles(tiles[0], buffer, tile_sems, waited, begins[3])

    def emit(block, carry):
        out[block] = total[block].astype(out.dtype)
        return carry

    lax.fori_loop(0, 16, emit, 0)


def spread_sums(plan, relations, pieces):
    width = pieces[0].shape[-1]
    slots = sum(relation[0].shape[0] for relation in relations)
    return pl.pallas_call(
        spread_kernel,
        out_shape=jax.ShapeDtypeStruct((16, TILE, width), BF16),
        in_specs=[spec(SMEM)] * 7
        + [spec(ANY)] * 3
        + [spec(ANY if number in FAR else VMEM) for number in range(8)],
        out_specs=spec(VMEM),
        scratch_shapes=[
            pltpu.VMEM((slots + 1, TILE, TILE), BF16),
            pltpu.VMEM((96, TILE, width), BF16),
            pltpu.VMEM((17, TILE, width), F32),
            pltpu.SemaphoreType.DMA((slots // GROUP,)),
            pltpu.SemaphoreType.DMA((len(FAR),)),
        ],
        compiler_params=pltpu.CompilerParams(vmem_limit_bytes=SPREAD_LIMIT),
        cost_estimate=pl.CostEstimate(
            flops=3 * 10**9, bytes_accessed=18 * 10**6, transcendentals=0
        ),
        name="spread_sums",
    )(
        *plan,
        *[relation[3] for relation in relations],
        *tile_args(relations),
        *[in_hbm(piece) if number in FAR else piece for number, piece in enumerate(pieces)],
    )


def columns_at(step, width):
    column = (lax.axis_index("tgt") + step) % SIDE
    return pl.ds(pl.multiple_of(column * width, width), width)


def hidden_kernel(part0, part1, part2, part3, weights, rounded, terms0, terms1, terms2, terms3):
    width = part0.shape[1]
    whole = part0[...].astype(F32)
    for part in (part1, part2, part3):
        whole = whole + part[...].astype(F32)
    whole = whole.astype(BF16)
    rounded[...] = whole
    for step, terms in ((2, terms2), (1, terms1), (3, terms3), (0, terms0)):
        value = jnp.zeros(terms.shape, F32)
        for number in range(3):
            value += jnp.dot(
                whole[number * TILE:(number + 1) * TILE],
                weights[number, :, columns_at(step, width)],
                preferred_element_type=F32,
            )
        terms[...] = value.astype(terms.dtype)


def hidden_terms(parts, weights):
    width = parts[0].shape[1]
    return pl.pallas_call(
        hidden_kernel,
        out_shape=(
            jax.ShapeDtypeStruct((3 * TILE, width), BF16),
            jax.ShapeDtypeStruct((TILE, width), F32),
            jax.ShapeDtypeStruct((TILE, width), BF16),
            jax.ShapeDtypeStruct((TILE, width), BF16),
            jax.ShapeDtypeStruct((TILE, width), BF16),
        ),
        in_specs=[spec(VMEM)] * 5,
        out_specs=tuple([spec(VMEM)] * 5),
        compiler_params=pltpu.CompilerParams(vmem_limit_bytes=8 * MIB),
        name="hidden_terms",
    )(*parts, weights)


def message_kernel(grad0, grad1, grad2, grad3, weights, messages):
    width = grad0.shape[1]
    for number in range(3):
        value = jnp.zeros((TILE, width), F32)
        for step, grad in enumerate((grad0, grad1, grad2, grad3)):
            value += lax.dot_general(
                grad[...],
                weights[number, :, columns_at(step, width)],
                (((1,), (1,)), ((), ())),
                preferred_element_type=F32,
            )
        messages[number] = value.astype(BF16)


def form_messages(grads, weights):
    width = grads[0].shape[1]
    return pl.pallas_call(
        message_kernel,
        out_shape=jax.ShapeDtypeStruct((3, TILE, width), BF16),
        in_specs=[spec(VMEM)] * 5,
        out_specs=spec(VMEM),
        compiler_params=pltpu.CompilerParams(vmem_limit_bytes=8 * MIB),
        name="form_messages",
    )(*grads, weights)


def add_kernel(left, right, out):
    out[...] = (left[...].astype(F32) + right[...].astype(F32)).astype(BF16)


def add_blocks(left, right):
    return pl.pallas_call(
        add_kernel,
        out_shape=jax.ShapeDtypeStruct(left.shape, BF16),
        in_specs=[spec(VMEM)] * 2,
        out_specs=spec(VMEM),
        compiler_params=pltpu.CompilerParams(vmem_limit_bytes=8 * MIB),
        name="add_blocks",
    )(left, right)


def join_kernel(*refs):
    for number, ref in enumerate(refs[:-1]):
        refs[-1][pl.ds(number * ref.shape[0], ref.shape[0])] = ref[...]


def join(blocks):
    shape = (sum(block.shape[0] for block in blocks), *blocks[0].shape[1:])
    return pl.pallas_call(
        join_kernel,
        out_shape=jax.ShapeDtypeStruct(shape, BF16),
        in_specs=[spec(VMEM)] * len(blocks),
        out_specs=spec(VMEM),
        compiler_params=pltpu.CompilerParams(vmem_limit_bytes=8 * MIB),
        name="join_blocks",
    )(*blocks)


def weight_kernel(grad0, grad1, grad2, grad3, rounded, keep, send, staged, sems):
    mine = here()
    block0 = lax.axis_index("tgt")
    values = jnp.concatenate(
        [rounded[number * TILE:(number + 1) * TILE, :] for number in range(3)], axis=1
    )
    for step, grad in enumerate((grad0, grad1, grad2, grad3)):
        turned = grad[...].astype(F32).T.astype(BF16)
        block = (block0 + step) % SIDE
        for part in range(8):
            first, second, away = place_of(block * 8 + part, mine)
            spot = away * 16 + second * SIDE + first
            value = jnp.dot(
                turned[part * 32:(part + 1) * 32], values, preferred_element_type=F32
            ).astype(BF16)
            for column in range(values.shape[1] // TILE):
                staged[spot, pl.ds(column * 32, 32), :] = value[
                    :, column * TILE:(column + 1) * TILE
                ]
    copies = [
        pltpu.make_async_copy(staged.at[pl.ds(16, 16)], send, sems.at[0]),
        pltpu.make_async_copy(staged.at[pl.ds(0, 16)], keep, sems.at[1]),
    ]
    for copy in copies:
        copy.start()
    for copy in copies:
        copy.wait()


def weight_terms(grads, rounded):
    width = grads[0].shape[1]
    rows = 32 * 3 * width // TILE
    blocks = jax.ShapeDtypeStruct((16, rows, TILE), BF16)
    return pl.pallas_call(
        weight_kernel,
        out_shape=(blocks, blocks),
        in_specs=[spec(VMEM)] * 5,
        out_specs=(spec(ANY), spec(ANY)),
        scratch_shapes=[
            pltpu.VMEM((32, rows, TILE), BF16),
            pltpu.SemaphoreType.DMA((2,)),
        ],
        compiler_params=pltpu.CompilerParams(vmem_limit_bytes=8 * MIB),
        cost_estimate=pl.CostEstimate(flops=10**9, bytes_accessed=3 * 10**6, transcendentals=0),
        name="weight_terms",
    )(*grads, rounded)


def shift_pairs(step, second):
    pairs = []
    for s in range(32):
        x, z, c = s // 8, (s // 2) % 4, s % 2
        if (c == 0) != second:
            x = (x + step) % SIDE
        else:
            z = (z + step) % SIDE
        pairs.append((s, (x * SIDE + z) * 2 + c))
    return pairs


def shift(value, step, second=False):
    return lax.ppermute(value, "src", shift_pairs(step, second))


def swap(value):
    return lax.ppermute(value, "src", [(s, s ^ 1) for s in range(32)])


def add(*values):
    total = values[0].astype(F32)
    for value in values[1:]:
        total = total + value.astype(F32)
    return total.astype(BF16)


def three_starts(values, second=False):
    arrived = []
    for k in (2, 1, 3):
        arrived.append(shift(values[k], k if k < 3 else -1, second))
    return tuple(arrived)


def three_ways(values, second=False):
    return barrier(three_starts(values, second))


def turn(value, step):
    return lax.ppermute(value, "tgt", [(t, (t + step) % SIDE) for t in range(SIDE)])


def shards(
    features,
    cites_tiles,
    cites_targets,
    cites_sources,
    cites_counts,
    writes_tiles,
    writes_targets,
    writes_sources,
    writes_counts,
    topic_tiles,
    topic_targets,
    topic_sources,
    topic_counts,
    owner_map,
    weights,
    bias_row,
    cotangent,
):
    width = features.shape[1]
    relations = (
        (cites_tiles, cites_targets, cites_sources, cites_counts),
        (writes_tiles, writes_targets, writes_sources, writes_counts),
        (topic_tiles, topic_targets, topic_sources, topic_counts),
    )
    keep, send = gather_sums(owner_map, relations, features)
    got = swap(send)
    quarters = [add(keep[4 * k:4 * k + 4], got[4 * k:4 * k + 4]) for k in range(4)]
    owner_map, *quarters = barrier((owner_map, *quarters))
    arrived = three_ways(quarters)
    plan = plan_spread(owner_map, relations)
    *plan, a0, a1, a2 = barrier((*plan, *arrived))
    line = [add(quarters[0][k], *[part[k] for part in (a0, a1, a2)]) for k in range(4)]
    parts = (line[0], *three_ways(line, True))

    rounded, terms0, terms1, terms2, terms3 = hidden_terms(parts, weights)
    turned = barrier((turn(terms2, 2), turn(terms1, 1), turn(terms3, 3)))
    hidden = terms0 + bias_row.astype(F32)[None, :]
    for part in turned:
        hidden = hidden + part.astype(F32)
    mixed_out, pullback = jax.vjp(functools.partial(jax.nn.gelu, approximate=True), hidden)
    grad_hidden = pullback(cotangent.astype(F32))[0].astype(BF16)
    two, one, three = barrier(
        (turn(grad_hidden, -2), turn(grad_hidden, -1), turn(grad_hidden, -3))
    )
    grads = [grad_hidden, one, two, three]

    own = form_messages(grads, weights)
    own, *grads = barrier((own, *grads))
    weight_keep, weight_send = weight_terms(grads, rounded)
    weight_got = swap(weight_send)
    two, three, one = barrier(three_starts((own,) * 4))
    quarters = [
        add(weight_keep[4 * k:4 * k + 4], weight_got[4 * k:4 * k + 4]) for k in range(1, 4)
    ]
    quarters = [add_blocks(weight_keep[:4], weight_got[:4]), *quarters]
    arrived = barrier(three_starts(quarters, True))
    whole = join((own, one, two, three))
    spread_out = three_starts((whole,) * 4, True)
    beside = swap(whole)
    line = [add(quarters[0][k], *[part[k] for part in arrived]) for k in range(4)]
    weight_parts = three_ways(line)
    *spread_out, beside, l0, w0, w1, w2 = barrier((*spread_out, beside, line[0], *weight_parts))
    weight_parts = (w0, w1, w2)
    siblings = [swap(piece) for piece in spread_out]
    grad_source = spread_sums(plan, relations, [whole, *spread_out, beside, *siblings])
    weight_sum = l0.astype(F32)
    for part in weight_parts:
        weight_sum = weight_sum + part.astype(F32)
    grad_weight = weight_sum.reshape(3 * width // TILE, 32, TILE).transpose(0, 2, 1)
    return (
        mixed_out.astype(BF16),
        grad_weight.reshape(3, width, 32),
        grad_source.reshape(-1, width),
    )


def solution(mesh):
    in_specs = (
        P("src", "tgt"),
        P("src", None, None),
        P("src"),
        P("src"),
        P("src"),
        P("src", None, None),
        P("src"),
        P("src"),
        P("src"),
        P("src", None, None),
        P("src"),
        P("src"),
        P("src"),
        P(),
        P(None, "tgt", None),
        P("tgt"),
        P("src", "tgt"),
    )
    out_specs = (P("src", "tgt"), P(None, "tgt", "src"), P("src", "tgt"))

    return jax.shard_map(shards, mesh=mesh, in_specs=in_specs, out_specs=out_specs, check_vma=False)
```

```python
import functools

import jax
import jax.numpy as jnp
from jax import lax
from jax.experimental import pallas as pl
from jax.experimental.pallas import tpu as pltpu
from jax.sharding import PartitionSpec as P


TILE = 128
SIDE = 4
GROUP = 16
PAIRS = 16
BF16 = jnp.bfloat16
F32 = jnp.float32
MIB = 1024 * 1024
GATHER_LIMIT = 36 * MIB
SPREAD_LIMIT = 20 * MIB
barrier = lax.optimization_barrier


def spec(space):
    return pl.BlockSpec(memory_space=space)


ANY, SMEM, VMEM = pl.ANY, pltpu.SMEM, pltpu.VMEM


def here():
    s = lax.axis_index("src")
    return s >> 3, (s >> 1) & 3, s & 1


def place_of(slot, mine):
    c = slot & 1
    dx = ((slot >> 3) - mine[0]) & 3
    dz = ((slot >> 1) - mine[1]) & 3
    first = jnp.where(c == 0, dx, dz)
    second = jnp.where(c == 0, dz, dx)
    return first, second, c ^ mine[2]


def live_parts(counts):
    parts = [(count[0] + GROUP - 1) // GROUP for count in counts]
    return parts, [0, parts[0], parts[0] + parts[1], parts[0] + parts[1] + parts[2]]


def start_tiles(tiles, counts, buffer, sems):
    parts, begins = live_parts(counts)
    for number in range(3):
        def step(part, carry, number=number):
            at = begins[number] + part
            pltpu.make_async_copy(
                tiles[number].at[pl.ds(part * GROUP, GROUP)],
                buffer.at[pl.ds(at * GROUP, GROUP)],
                sems.at[at],
            ).start()
            return carry

        lax.fori_loop(0, parts[number], step, 0)
    return begins


def wait_tiles(tile, buffer, sems, waited, needed):
    def step(at, carry):
        pltpu.make_async_copy(
            tile.at[pl.ds(0, GROUP)], buffer.at[pl.ds(at * GROUP, GROUP)], sems.at[at]
        ).wait()
        return carry

    lax.fori_loop(waited, needed, step, 0)
    return jnp.maximum(waited, needed)


def clear(total, amount, begin=0):
    def step(block, carry):
        total[block] = jnp.zeros(total.shape[1:], F32)
        return carry

    lax.fori_loop(begin, amount, step, 0)


def gather_list(codes, amount, features, buffer, total, ready):
    def add_group(group, waited):
        waited = ready(waited, codes[jnp.minimum(group * GROUP + GROUP, amount) - 1] & 1023)
        marks = [codes[group * GROUP + lane] for lane in range(GROUP)]
        products = [
            jnp.dot(
                buffer[mark & 1023], features[(mark >> 10) & 15], preferred_element_type=F32
            )
            for mark in marks
        ]
        for mark, product in zip(marks, products):
            total[mark >> 14] += product
        return waited

    return lax.fori_loop(0, (amount + GROUP - 1) // GROUP, add_group, jnp.int32(0))


def emit_blocks(total, target):
    def emit(spot, carry):
        for number in range(3):
            target[spot, pl.ds(number * TILE, TILE), :] = total[spot * 3 + number].astype(BF16)
        return carry

    lax.fori_loop(0, 16, emit, 0)


def gather_send_kernel(
    owner_map,
    targets0, targets1, targets2, sources0, sources1, sources2, counts0, counts1, counts2,
    features, tiles0, tiles1, tiles2,
    send, keep_codes, keep_amount, buffer, held,
    total, table, send_codes, tile_sems, feature_sem,
):
    targets, sources = (targets0, targets1, targets2), (sources0, sources1, sources2)
    counts, tiles = (counts0, counts1, counts2), (tiles0, tiles1, tiles2)
    feature_copy = pltpu.make_async_copy(features, held, feature_sem)
    feature_copy.start()
    begins = start_tiles(tiles, counts, buffer, tile_sems)
    mine = here()

    def fill(slot, carry):
        first, second, away = place_of(slot, mine)
        table[owner_map[slot]] = (first * SIDE + second) * 3 + away * 128
        total[slot] = jnp.zeros(total.shape[1:], F32)
        return carry

    lax.fori_loop(0, 32, fill, 0)
    clear(total, 48, 32)

    sent, kept = jnp.int32(0), jnp.int32(0)
    for number in range(3):
        def sort(group, carry, number=number):
            sent, kept = carry
            for lane in range(GROUP):
                j = group * GROUP + lane
                spot = table[targets[number][j]]
                code = (
                    (begins[number] * GROUP + j)
                    + sources[number][j] * 1024
                    + ((spot & 127) + number) * 16384
                )
                send_codes[sent] = code
                keep_codes[kept] = code
                live = jnp.where(j < counts[number][0], 1, 0)
                away = live & (spot >> 7)
                sent, kept = sent + away, kept + (live - away)
            return sent, kept

        sent, kept = lax.fori_loop(
            0, (counts[number][0] + GROUP - 1) // GROUP, sort, (sent, kept)
        )
    for lane in range(GROUP):
        send_codes[sent + lane] = 48 * 16384
        keep_codes[kept + lane] = 48 * 16384
    keep_amount[0] = kept
    feature_copy.wait()

    def ready(waited, last):
        return wait_tiles(tiles[0], buffer, tile_sems, waited, (last >> 4) + 1)

    waited = gather_list(send_codes, sent, held, buffer, total, ready)
    wait_tiles(tiles[0], buffer, tile_sems, waited, begins[3])
    emit_blocks(total, send)


def gather_keep_kernel(codes, amount, buffer, held, keep, total):
    clear(total, 48)
    gather_list(codes, amount[0], held, buffer, total, lambda waited, last: waited)
    emit_blocks(total, keep)


def in_hbm(value):
    return pltpu.with_memory_space_constraint(value, pltpu.HBM)


def flat_args(owner_map, relations):
    return (
        in_hbm(owner_map),
        *[in_hbm(relation[1]) for relation in relations],
        *[in_hbm(relation[2]) for relation in relations],
        *[relation[3] for relation in relations],
    )


def tile_args(relations):
    return [in_hbm(relation[0]) for relation in relations]


def gather_sums(owner_map, relations, features):
    width = features.shape[-1]
    slots = sum(relation[0].shape[0] for relation in relations)
    blocks = jax.ShapeDtypeStruct((16, 3 * TILE, width), BF16)
    features = features.reshape(-1, TILE, width)
    total = pltpu.VMEM((49, TILE, width), F32)
    common = dict(
        compiler_params=pltpu.CompilerParams(vmem_limit_bytes=GATHER_LIMIT),
        cost_estimate=pl.CostEstimate(
            flops=2 * 10**9, bytes_accessed=12 * 10**6, transcendentals=0
        ),
    )
    send, codes, amount, buffer, held = pl.pallas_call(
        gather_send_kernel,
        out_shape=(
            blocks,
            jax.ShapeDtypeStruct((slots + GROUP,), jnp.int32),
            jax.ShapeDtypeStruct((1,), jnp.int32),
            jax.ShapeDtypeStruct((slots, TILE, TILE), BF16),
            jax.ShapeDtypeStruct(features.shape, BF16),
        ),
        in_specs=[spec(SMEM)] * 10 + [spec(ANY)] * 4,
        out_specs=(spec(VMEM), spec(SMEM), spec(SMEM), spec(VMEM), spec(VMEM)),
        scratch_shapes=[
            total,
            pltpu.SMEM((32,), jnp.int32),
            pltpu.SMEM((slots + GROUP,), jnp.int32),
            pltpu.SemaphoreType.DMA((slots // GROUP,)),
            pltpu.SemaphoreType.DMA(()),
        ],
        name="gather_send",
        **common,
    )(*flat_args(owner_map, relations), in_hbm(features), *tile_args(relations))
    keep = pl.pallas_call(
        gather_keep_kernel,
        out_shape=blocks,
        in_specs=[spec(SMEM)] * 2 + [spec(VMEM)] * 2,
        out_specs=spec(VMEM),
        scratch_shapes=[total],
        name="gather_keep",
        **common,
    )(codes, amount, buffer, held)
    return keep, send


EARLY = 20


def plan_kernel(
    owner_map,
    targets0, targets1, targets2, sources0, sources1, sources2, counts0, counts1, counts2,
    pair_a, pair_b, pair_spot, amounts,
    table, pending,
    *, room, blank,
):
    targets, sources = (targets0, targets1, targets2), (sources0, sources1, sources2)
    counts = (counts0, counts1, counts2)
    begins = live_parts(counts)[1]
    mine = here()

    def fill(slot, carry):
        first, second, away = place_of(slot, mine)
        place = away * 16 + second * SIDE + first
        late = jnp.where(place >= EARLY, 1, 0)
        table[owner_map[slot]] = (place - late * EARLY) * 3 + late * 128
        pending[slot] = -1
        return carry

    lax.fori_loop(0, 32, fill, 0)
    pending[32] = -1

    def put(found, late, a, b, spot, yes):
        at = jnp.where(late == 1, room + found[1], found[0])
        pair_a[at] = a
        pair_b[at] = b
        pair_spot[at] = spot
        return found[0] + yes * (1 - late), found[1] + yes * late

    found = (jnp.int32(0), jnp.int32(0))
    for number in range(3):
        def match(group, found, number=number):
            for lane in range(GROUP):
                j = group * GROUP + lane
                live = j < counts[number][0]
                place = table[targets[number][j]]
                late = place >> 7
                source = sources[number][j]
                code = begins[number] * GROUP + j + ((place & 127) + number) * 1024
                spot = jnp.where(live, late * 16 + source, 32)
                waiting = pending[spot]
                hit = live & (waiting >= 0)
                found = put(found, late, waiting, code, source, jnp.where(hit, 1, 0))
                pending[spot] = jnp.where(hit, -1, code)
            return found

        found = lax.fori_loop(0, (counts[number][0] + GROUP - 1) // GROUP, match, found)

    def flush(spot, found):
        waiting = pending[spot]
        yes = jnp.where(waiting >= 0, 1, 0)
        return put(found, spot >> 4, waiting, blank, spot & 15, yes)

    found = lax.fori_loop(0, 32, flush, found)
    for late in range(2):
        for lane in range(PAIRS):
            pair_a[late * room + found[late] + lane] = blank
            pair_b[late * room + found[late] + lane] = blank
            pair_spot[late * room + found[late] + lane] = 16
        amounts[late] = found[late]


def pair_room(slots):
    return slots // 2 + 32 + PAIRS


def plan_spread(owner_map, relations):
    slots = sum(relation[0].shape[0] for relation in relations)
    room = pair_room(slots)
    pairs = jax.ShapeDtypeStruct((2 * room,), jnp.int32)
    return pl.pallas_call(
        functools.partial(plan_kernel, room=room, blank=slots),
        out_shape=(pairs, pairs, pairs, jax.ShapeDtypeStruct((2,), jnp.int32)),
        in_specs=[spec(SMEM)] * 10,
        out_specs=tuple([spec(SMEM)] * 4),
        scratch_shapes=[pltpu.SMEM((32,), jnp.int32), pltpu.SMEM((33,), jnp.int32)],
        compiler_params=pltpu.CompilerParams(vmem_limit_bytes=MIB),
        cost_estimate=pl.CostEstimate(flops=10**9, bytes_accessed=10**6, transcendentals=0),
        name="plan_spread",
    )(*flat_args(owner_map, relations))


def spread_list(plan, offset, amount, messages, buffer, total, ready):
    pair_a, pair_b, pair_spot = plan

    def add_group(group, waited):
        at = offset + group * PAIRS
        waited = ready(waited, pair_b[at + PAIRS - 1] & 1023)
        products = []
        for lane in range(PAIRS):
            marks = (pair_a[at + lane], pair_b[at + lane])
            tile = jnp.concatenate([buffer[mark & 1023] for mark in marks], axis=0)
            block = jnp.concatenate([messages[mark >> 10] for mark in marks], axis=0)
            products.append(
                lax.dot_general(
                    tile, block, (((0,), (0,)), ((), ())), preferred_element_type=F32
                )
            )
        for lane in range(PAIRS):
            total[pair_spot[at + lane]] += products[lane]
        return waited

    return lax.fori_loop(0, (amount + PAIRS - 1) // PAIRS, add_group, jnp.int32(0))


def start_pieces(pieces, places, messages, sems):
    copies = [
        pltpu.make_async_copy(piece, messages.at[pl.ds(at * 3, 12)], sems.at[number])
        for number, (piece, at) in enumerate(zip(pieces, places))
    ]
    for copy in copies:
        copy.start()
    return copies


def spread_early_kernel(
    pair_a, pair_b, pair_spot, amounts, counts0, counts1, counts2, tiles0, tiles1, tiles2,
    own0, own2, own3, own1, sib0,
    out, buffer, messages, total, tile_sems, piece_sems,
):
    tiles = (tiles0, tiles1, tiles2)
    copies = start_pieces((own1,), (4,), messages, piece_sems)
    begins = start_tiles(tiles, (counts0, counts1, counts2), buffer, tile_sems)

    def place(block, carry):
        for piece, at in ((own0, 0), (own2, 8), (own3, 12), (sib0, 16)):
            messages[at * 3 + block] = piece[block]
        return carry

    lax.fori_loop(0, 12, place, 0)
    buffer[buffer.shape[0] - 1] = jnp.zeros((TILE, TILE), BF16)
    clear(total, 16)
    for copy in copies:
        copy.wait()

    def ready(waited, last):
        needed = jnp.minimum((last >> 4) + 1, begins[3])
        return wait_tiles(tiles0, buffer, tile_sems, waited, needed)

    waited = spread_list(
        (pair_a, pair_b, pair_spot), 0, amounts[0], messages, buffer, total, ready
    )
    wait_tiles(tiles0, buffer, tile_sems, waited, begins[3])

    def emit(block, carry):
        out[block] = total[block]
        return carry

    lax.fori_loop(0, 16, emit, 0)


def spread_late_kernel(
    pair_a, pair_b, pair_spot, amounts, buffer, before, sib2, sib3, sib1,
    out, messages, total, piece_sems,
):
    copies = start_pieces((sib2, sib3, sib1), (4, 8, 0), messages, piece_sems)

    def take(block, carry):
        total[block] = before[block]
        return carry

    lax.fori_loop(0, 16, take, 0)
    for copy in copies:
        copy.wait()
    spread_list(
        (pair_a, pair_b, pair_spot),
        pair_a.shape[0] // 2,
        amounts[1],
        messages,
        buffer,
        total,
        lambda waited, last: waited,
    )

    def emit(block, carry):
        out[block] = total[block].astype(BF16)
        return carry

    lax.fori_loop(0, 16, emit, 0)


def spread_early(plan, relations, pieces):
    width = pieces[0].shape[-1]
    slots = sum(relation[0].shape[0] for relation in relations)
    whole, own2, own3, own1, beside = pieces
    return pl.pallas_call(
        spread_early_kernel,
        out_shape=(
            jax.ShapeDtypeStruct((16, TILE, width), F32),
            jax.ShapeDtypeStruct((slots + 1, TILE, TILE), BF16),
        ),
        in_specs=[spec(SMEM)] * 7
        + [spec(ANY)] * 3
        + [spec(VMEM)] * 3
        + [spec(ANY), spec(VMEM)],
        out_specs=(spec(VMEM), spec(VMEM)),
        scratch_shapes=[
            pltpu.VMEM((3 * EARLY, TILE, width), BF16),
            pltpu.VMEM((17, TILE, width), F32),
            pltpu.SemaphoreType.DMA((slots // GROUP,)),
            pltpu.SemaphoreType.DMA((1,)),
        ],
        compiler_params=pltpu.CompilerParams(vmem_limit_bytes=SPREAD_LIMIT),
        cost_estimate=pl.CostEstimate(
            flops=2 * 10**9, bytes_accessed=14 * 10**6, transcendentals=0
        ),
        name="spread_early",
    )(
        *plan,
        *[relation[3] for relation in relations],
        *tile_args(relations),
        whole, own2, own3, in_hbm(own1), beside,
    )


def spread_late(plan, early, pieces):
    before, buffer = early
    width = pieces[0].shape[-1]
    return pl.pallas_call(
        spread_late_kernel,
        out_shape=jax.ShapeDtypeStruct((16, TILE, width), BF16),
        in_specs=[spec(SMEM)] * 4 + [spec(VMEM)] * 2 + [spec(ANY)] * 3,
        out_specs=spec(VMEM),
        scratch_shapes=[
            pltpu.VMEM((3 * (32 - EARLY), TILE, width), BF16),
            pltpu.VMEM((17, TILE, width), F32),
            pltpu.SemaphoreType.DMA((3,)),
        ],
        compiler_params=pltpu.CompilerParams(vmem_limit_bytes=SPREAD_LIMIT),
        cost_estimate=pl.CostEstimate(
            flops=10**9, bytes_accessed=4 * 10**6, transcendentals=0
        ),
        name="spread_late",
    )(*plan, buffer, before, *[in_hbm(piece) for piece in pieces])


def columns_at(step, width):
    column = (lax.axis_index("tgt") + step) % SIDE
    return pl.ds(pl.multiple_of(column * width, width), width)


def hidden_kernel(part0, part1, part2, part3, weights, rounded, terms0, terms1, terms2, terms3):
    width = part0.shape[1]
    whole = part0[...].astype(F32)
    for part in (part1, part2, part3):
        whole = whole + part[...].astype(F32)
    whole = whole.astype(BF16)
    rounded[...] = whole
    for step, terms in ((2, terms2), (1, terms1), (3, terms3), (0, terms0)):
        value = jnp.zeros(terms.shape, F32)
        for number in range(3):
            value += jnp.dot(
                whole[number * TILE:(number + 1) * TILE],
                weights[number, :, columns_at(step, width)],
                preferred_element_type=F32,
            )
        terms[...] = value.astype(terms.dtype)


def hidden_terms(parts, weights):
    width = parts[0].shape[1]
    return pl.pallas_call(
        hidden_kernel,
        out_shape=(
            jax.ShapeDtypeStruct((3 * TILE, width), BF16),
            jax.ShapeDtypeStruct((TILE, width), F32),
            jax.ShapeDtypeStruct((TILE, width), BF16),
            jax.ShapeDtypeStruct((TILE, width), BF16),
            jax.ShapeDtypeStruct((TILE, width), BF16),
        ),
        in_specs=[spec(VMEM)] * 5,
        out_specs=tuple([spec(VMEM)] * 5),
        compiler_params=pltpu.CompilerParams(vmem_limit_bytes=8 * MIB),
        name="hidden_terms",
    )(*parts, weights)


def message_kernel(grad0, grad1, grad2, grad3, weights, messages):
    width = grad0.shape[1]
    for number in range(3):
        value = jnp.zeros((TILE, width), F32)
        for step, grad in enumerate((grad0, grad1, grad2, grad3)):
            value += lax.dot_general(
                grad[...],
                weights[number, :, columns_at(step, width)],
                (((1,), (1,)), ((), ())),
                preferred_element_type=F32,
            )
        messages[number] = value.astype(BF16)


def form_messages(grads, weights):
    width = grads[0].shape[1]
    return pl.pallas_call(
        message_kernel,
        out_shape=jax.ShapeDtypeStruct((3, TILE, width), BF16),
        in_specs=[spec(VMEM)] * 5,
        out_specs=spec(VMEM),
        compiler_params=pltpu.CompilerParams(vmem_limit_bytes=8 * MIB),
        name="form_messages",
    )(*grads, weights)


def add_kernel(left, right, out):
    out[...] = (left[...].astype(F32) + right[...].astype(F32)).astype(BF16)


def add_blocks(left, right):
    return pl.pallas_call(
        add_kernel,
        out_shape=jax.ShapeDtypeStruct(left.shape, BF16),
        in_specs=[spec(VMEM)] * 2,
        out_specs=spec(VMEM),
        compiler_params=pltpu.CompilerParams(vmem_limit_bytes=8 * MIB),
        name="add_blocks",
    )(left, right)


def join_kernel(*refs):
    for number, ref in enumerate(refs[:-1]):
        refs[-1][pl.ds(number * ref.shape[0], ref.shape[0])] = ref[...]


def join(blocks):
    shape = (sum(block.shape[0] for block in blocks), *blocks[0].shape[1:])
    return pl.pallas_call(
        join_kernel,
        out_shape=jax.ShapeDtypeStruct(shape, BF16),
        in_specs=[spec(VMEM)] * len(blocks),
        out_specs=spec(VMEM),
        compiler_params=pltpu.CompilerParams(vmem_limit_bytes=8 * MIB),
        name="join_blocks",
    )(*blocks)


def weight_kernel(grad0, grad1, grad2, grad3, rounded, keep, send, staged, sems):
    mine = here()
    block0 = lax.axis_index("tgt")
    values = jnp.concatenate(
        [rounded[number * TILE:(number + 1) * TILE, :] for number in range(3)], axis=1
    )
    for step, grad in enumerate((grad0, grad1, grad2, grad3)):
        turned = grad[...].astype(F32).T.astype(BF16)
        block = (block0 + step) % SIDE
        for part in range(8):
            first, second, away = place_of(block * 8 + part, mine)
            spot = away * 16 + second * SIDE + first
            value = jnp.dot(
                turned[part * 32:(part + 1) * 32], values, preferred_element_type=F32
            ).astype(BF16)
            for column in range(values.shape[1] // TILE):
                staged[spot, pl.ds(column * 32, 32), :] = value[
                    :, column * TILE:(column + 1) * TILE
                ]
    copies = [
        pltpu.make_async_copy(staged.at[pl.ds(16, 16)], send, sems.at[0]),
        pltpu.make_async_copy(staged.at[pl.ds(0, 16)], keep, sems.at[1]),
    ]
    for copy in copies:
        copy.start()
    for copy in copies:
        copy.wait()


def weight_terms(grads, rounded):
    width = grads[0].shape[1]
    rows = 32 * 3 * width // TILE
    blocks = jax.ShapeDtypeStruct((16, rows, TILE), BF16)
    return pl.pallas_call(
        weight_kernel,
        out_shape=(blocks, blocks),
        in_specs=[spec(VMEM)] * 5,
        out_specs=(spec(ANY), spec(ANY)),
        scratch_shapes=[
            pltpu.VMEM((32, rows, TILE), BF16),
            pltpu.SemaphoreType.DMA((2,)),
        ],
        compiler_params=pltpu.CompilerParams(vmem_limit_bytes=8 * MIB),
        cost_estimate=pl.CostEstimate(flops=10**9, bytes_accessed=3 * 10**6, transcendentals=0),
        name="weight_terms",
    )(*grads, rounded)


def shift_pairs(step, second):
    pairs = []
    for s in range(32):
        x, z, c = s // 8, (s // 2) % 4, s % 2
        if (c == 0) != second:
            x = (x + step) % SIDE
        else:
            z = (z + step) % SIDE
        pairs.append((s, (x * SIDE + z) * 2 + c))
    return pairs


def shift(value, step, second=False):
    return lax.ppermute(value, "src", shift_pairs(step, second))


def swap(value):
    return lax.ppermute(value, "src", [(s, s ^ 1) for s in range(32)])


def add(*values):
    total = values[0].astype(F32)
    for value in values[1:]:
        total = total + value.astype(F32)
    return total.astype(BF16)


def three_starts(values, second=False):
    arrived = []
    for k in (2, 1, 3):
        arrived.append(shift(values[k], k if k < 3 else -1, second))
    return tuple(arrived)


def three_ways(values, second=False):
    return barrier(three_starts(values, second))


def turn(value, step):
    return lax.ppermute(value, "tgt", [(t, (t + step) % SIDE) for t in range(SIDE)])


def shards(
    features,
    cites_tiles,
    cites_targets,
    cites_sources,
    cites_counts,
    writes_tiles,
    writes_targets,
    writes_sources,
    writes_counts,
    topic_tiles,
    topic_targets,
    topic_sources,
    topic_counts,
    owner_map,
    weights,
    bias_row,
    cotangent,
):
    width = features.shape[1]
    relations = (
        (cites_tiles, cites_targets, cites_sources, cites_counts),
        (writes_tiles, writes_targets, writes_sources, writes_counts),
        (topic_tiles, topic_targets, topic_sources, topic_counts),
    )
    keep, send = gather_sums(owner_map, relations, features)
    got = swap(send)
    quarters = [add(keep[4 * k:4 * k + 4], got[4 * k:4 * k + 4]) for k in range(4)]
    owner_map, *quarters = barrier((owner_map, *quarters))
    arrived = three_ways(quarters)
    plan = plan_spread(owner_map, relations)
    *plan, a0, a1, a2 = barrier((*plan, *arrived))
    line = [add(quarters[0][k], *[part[k] for part in (a0, a1, a2)]) for k in range(4)]
    parts = (line[0], *three_ways(line, True))

    rounded, terms0, terms1, terms2, terms3 = hidden_terms(parts, weights)
    turned = barrier((turn(terms2, 2), turn(terms1, 1), turn(terms3, 3)))
    hidden = terms0 + bias_row.astype(F32)[None, :]
    for part in turned:
        hidden = hidden + part.astype(F32)
    mixed_out, pullback = jax.vjp(functools.partial(jax.nn.gelu, approximate=True), hidden)
    grad_hidden = pullback(cotangent.astype(F32))[0].astype(BF16)
    two, one, three = barrier(
        (turn(grad_hidden, -2), turn(grad_hidden, -1), turn(grad_hidden, -3))
    )
    grads = [grad_hidden, one, two, three]

    own = form_messages(grads, weights)
    own, *grads = barrier((own, *grads))
    weight_keep, weight_send = weight_terms(grads, rounded)
    weight_got = swap(weight_send)
    two, three, one = barrier(three_starts((own,) * 4))
    quarters = [
        add(weight_keep[4 * k:4 * k + 4], weight_got[4 * k:4 * k + 4]) for k in range(1, 4)
    ]
    quarters = [add_blocks(weight_keep[:4], weight_got[:4]), *quarters]
    arrived = barrier(three_starts(quarters, True))
    whole = join((own, one, two, three))
    spread_out = three_starts((whole,) * 4, True)
    beside = swap(whole)
    line = [add(quarters[0][k], *[part[k] for part in arrived]) for k in range(4)]
    weight_parts = three_ways(line)
    *spread_out, beside, l0, w0, w1, w2 = barrier((*spread_out, beside, line[0], *weight_parts))
    weight_parts = (w0, w1, w2)
    siblings = [swap(piece) for piece in spread_out]
    early = spread_early(plan, relations, [whole, *spread_out, beside])
    grad_source = spread_late(plan, early, siblings)
    weight_sum = l0.astype(F32)
    for part in weight_parts:
        weight_sum = weight_sum + part.astype(F32)
    grad_weight = weight_sum.reshape(3 * width // TILE, 32, TILE).transpose(0, 2, 1)
    return (
        mixed_out.astype(BF16),
        grad_weight.reshape(3, width, 32),
        grad_source.reshape(-1, width),
    )


def solution(mesh):
    in_specs = (
        P("src", "tgt"),
        P("src", None, None),
        P("src"),
        P("src"),
        P("src"),
        P("src", None, None),
        P("src"),
        P("src"),
        P("src"),
        P("src", None, None),
        P("src"),
        P("src"),
        P("src"),
        P(),
        P(None, "tgt", None),
        P("tgt"),
        P("src", "tgt"),
    )
    out_specs = (P("src", "tgt"), P(None, "tgt", "src"), P("src", "tgt"))

    return jax.shard_map(shards, mesh=mesh, in_specs=in_specs, out_specs=out_specs, check_vma=False)
```

```python
import functools

import jax
import jax.numpy as jnp
from jax import lax
from jax.experimental import pallas as pl
from jax.experimental.pallas import tpu as pltpu
from jax.sharding import PartitionSpec as P


TILE = 128
SIDE = 4
GROUP = 16
PAIRS = 16
BF16 = jnp.bfloat16
F32 = jnp.float32
MIB = 1024 * 1024
GATHER_LIMIT = 36 * MIB
SPREAD_LIMIT = 12 * MIB
barrier = lax.optimization_barrier


def spec(space):
    return pl.BlockSpec(memory_space=space)


ANY, SMEM, VMEM = pl.ANY, pltpu.SMEM, pltpu.VMEM


def here():
    s = lax.axis_index("src")
    return s >> 3, (s >> 1) & 3, s & 1


def place_of(slot, mine):
    c = slot & 1
    dx = ((slot >> 3) - mine[0]) & 3
    dz = ((slot >> 1) - mine[1]) & 3
    first = jnp.where(c == 0, dx, dz)
    second = jnp.where(c == 0, dz, dx)
    return first, second, c ^ mine[2]


def live_parts(counts):
    parts = [(count[0] + GROUP - 1) // GROUP for count in counts]
    return parts, [0, parts[0], parts[0] + parts[1], parts[0] + parts[1] + parts[2]]


def start_tiles(tiles, counts, buffer, sems):
    parts, begins = live_parts(counts)
    for number in range(3):
        def step(part, carry, number=number):
            at = begins[number] + part
            pltpu.make_async_copy(
                tiles[number].at[pl.ds(part * GROUP, GROUP)],
                buffer.at[pl.ds(at * GROUP, GROUP)],
                sems.at[at],
            ).start()
            return carry

        lax.fori_loop(0, parts[number], step, 0)
    return begins


def wait_tiles(tile, buffer, sems, waited, needed):
    def step(at, carry):
        pltpu.make_async_copy(
            tile.at[pl.ds(0, GROUP)], buffer.at[pl.ds(at * GROUP, GROUP)], sems.at[at]
        ).wait()
        return carry

    lax.fori_loop(waited, needed, step, 0)
    return jnp.maximum(waited, needed)


def clear(total, amount, begin=0):
    def step(block, carry):
        total[block] = jnp.zeros(total.shape[1:], F32)
        return carry

    lax.fori_loop(begin, amount, step, 0)


def gather_list(codes, amount, features, buffer, total, ready):
    def add_group(group, waited):
        waited = ready(waited, codes[jnp.minimum(group * GROUP + GROUP, amount) - 1] & 1023)
        marks = [codes[group * GROUP + lane] for lane in range(GROUP)]
        products = [
            jnp.dot(
                buffer[mark & 1023], features[(mark >> 10) & 15], preferred_element_type=F32
            )
            for mark in marks
        ]
        for mark, product in zip(marks, products):
            total[mark >> 14] += product
        return waited

    return lax.fori_loop(0, (amount + GROUP - 1) // GROUP, add_group, jnp.int32(0))


def emit_blocks(total, target):
    def emit(spot, carry):
        for number in range(3):
            target[spot, pl.ds(number * TILE, TILE), :] = total[spot * 3 + number].astype(BF16)
        return carry

    lax.fori_loop(0, 16, emit, 0)


def gather_send_kernel(
    owner_map,
    targets0, targets1, targets2, sources0, sources1, sources2, counts0, counts1, counts2,
    features, tiles0, tiles1, tiles2,
    send, keep_codes, keep_amount, buffer, held,
    total, table, send_codes, tile_sems, feature_sem,
):
    targets, sources = (targets0, targets1, targets2), (sources0, sources1, sources2)
    counts, tiles = (counts0, counts1, counts2), (tiles0, tiles1, tiles2)
    feature_copy = pltpu.make_async_copy(features, held, feature_sem)
    feature_copy.start()
    begins = start_tiles(tiles, counts, buffer, tile_sems)
    mine = here()

    def fill(slot, carry):
        first, second, away = place_of(slot, mine)
        table[owner_map[slot]] = (first * SIDE + second) * 3 + away * 128
        total[slot] = jnp.zeros(total.shape[1:], F32)
        return carry

    lax.fori_loop(0, 32, fill, 0)
    clear(total, 48, 32)

    sent, kept = jnp.int32(0), jnp.int32(0)
    for number in range(3):
        def sort(group, carry, number=number):
            sent, kept = carry
            for lane in range(GROUP):
                j = group * GROUP + lane
                spot = table[targets[number][j]]
                code = (
                    (begins[number] * GROUP + j)
                    + sources[number][j] * 1024
                    + ((spot & 127) + number) * 16384
                )
                send_codes[sent] = code
                keep_codes[kept] = code
                live = jnp.where(j < counts[number][0], 1, 0)
                away = live & (spot >> 7)
                sent, kept = sent + away, kept + (live - away)
            return sent, kept

        sent, kept = lax.fori_loop(
            0, (counts[number][0] + GROUP - 1) // GROUP, sort, (sent, kept)
        )
    for lane in range(GROUP):
        send_codes[sent + lane] = 48 * 16384
        keep_codes[kept + lane] = 48 * 16384
    keep_amount[0] = kept
    feature_copy.wait()

    def ready(waited, last):
        return wait_tiles(tiles[0], buffer, tile_sems, waited, (last >> 4) + 1)

    waited = gather_list(send_codes, sent, held, buffer, total, ready)
    wait_tiles(tiles[0], buffer, tile_sems, waited, begins[3])
    emit_blocks(total, send)


def gather_keep_kernel(codes, amount, buffer, held, keep, total):
    clear(total, 48)
    gather_list(codes, amount[0], held, buffer, total, lambda waited, last: waited)
    emit_blocks(total, keep)


def in_hbm(value):
    return pltpu.with_memory_space_constraint(value, pltpu.HBM)


def flat_args(owner_map, relations):
    return (
        in_hbm(owner_map),
        *[in_hbm(relation[1]) for relation in relations],
        *[in_hbm(relation[2]) for relation in relations],
        *[relation[3] for relation in relations],
    )


def tile_args(relations):
    return [in_hbm(relation[0]) for relation in relations]


def gather_sums(owner_map, relations, features):
    width = features.shape[-1]
    slots = sum(relation[0].shape[0] for relation in relations)
    blocks = jax.ShapeDtypeStruct((16, 3 * TILE, width), BF16)
    features = features.reshape(-1, TILE, width)
    total = pltpu.VMEM((49, TILE, width), F32)
    common = dict(
        compiler_params=pltpu.CompilerParams(vmem_limit_bytes=GATHER_LIMIT),
        cost_estimate=pl.CostEstimate(
            flops=2 * 10**9, bytes_accessed=12 * 10**6, transcendentals=0
        ),
    )
    send, codes, amount, buffer, held = pl.pallas_call(
        gather_send_kernel,
        out_shape=(
            blocks,
            jax.ShapeDtypeStruct((slots + GROUP,), jnp.int32),
            jax.ShapeDtypeStruct((1,), jnp.int32),
            jax.ShapeDtypeStruct((slots, TILE, TILE), BF16),
            jax.ShapeDtypeStruct(features.shape, BF16),
        ),
        in_specs=[spec(SMEM)] * 10 + [spec(ANY)] * 4,
        out_specs=(spec(VMEM), spec(SMEM), spec(SMEM), spec(VMEM), spec(VMEM)),
        scratch_shapes=[
            total,
            pltpu.SMEM((32,), jnp.int32),
            pltpu.SMEM((slots + GROUP,), jnp.int32),
            pltpu.SemaphoreType.DMA((slots // GROUP,)),
            pltpu.SemaphoreType.DMA(()),
        ],
        name="gather_send",
        **common,
    )(*flat_args(owner_map, relations), in_hbm(features), *tile_args(relations))
    keep = pl.pallas_call(
        gather_keep_kernel,
        out_shape=blocks,
        in_specs=[spec(SMEM)] * 2 + [spec(VMEM)] * 2,
        out_specs=spec(VMEM),
        scratch_shapes=[total],
        name="gather_keep",
        **common,
    )(codes, amount, buffer, held)
    return keep, send


EARLY = 20


def plan_kernel(
    owner_map,
    targets0, targets1, targets2, sources0, sources1, sources2, counts0, counts1, counts2,
    pair_a, pair_b, pair_spot, amounts,
    table, pending,
    *, room, blank,
):
    targets, sources = (targets0, targets1, targets2), (sources0, sources1, sources2)
    counts = (counts0, counts1, counts2)
    begins = live_parts(counts)[1]
    mine = here()

    def fill(slot, carry):
        first, second, away = place_of(slot, mine)
        place = away * 16 + second * SIDE + first
        late = jnp.where(place >= EARLY, 1, 0)
        table[owner_map[slot]] = (place - late * EARLY) * 3 + late * 128
        pending[slot] = -1
        return carry

    lax.fori_loop(0, 32, fill, 0)
    pending[32] = -1

    def put(found, late, a, b, spot, yes):
        at = jnp.where(late == 1, room + found[1], found[0])
        pair_a[at] = a
        pair_b[at] = b
        pair_spot[at] = spot
        return found[0] + yes * (1 - late), found[1] + yes * late

    found = (jnp.int32(0), jnp.int32(0))
    for number in range(3):
        def match(group, found, number=number):
            for lane in range(GROUP):
                j = group * GROUP + lane
                live = j < counts[number][0]
                place = table[targets[number][j]]
                late = place >> 7
                source = sources[number][j]
                code = begins[number] * GROUP + j + ((place & 127) + number) * 1024
                spot = jnp.where(live, late * 16 + source, 32)
                waiting = pending[spot]
                hit = live & (waiting >= 0)
                found = put(found, late, waiting, code, source, jnp.where(hit, 1, 0))
                pending[spot] = jnp.where(hit, -1, code)
            return found

        found = lax.fori_loop(0, (counts[number][0] + GROUP - 1) // GROUP, match, found)

    def flush(spot, found):
        waiting = pending[spot]
        yes = jnp.where(waiting >= 0, 1, 0)
        return put(found, spot >> 4, waiting, blank, spot & 15, yes)

    found = lax.fori_loop(0, 32, flush, found)
    for late in range(2):
        for lane in range(PAIRS):
            pair_a[late * room + found[late] + lane] = blank
            pair_b[late * room + found[late] + lane] = blank
            pair_spot[late * room + found[late] + lane] = 16
        amounts[late] = found[late]


def pair_room(slots):
    return slots // 2 + 32 + PAIRS


def plan_spread(owner_map, relations):
    slots = sum(relation[0].shape[0] for relation in relations)
    room = pair_room(slots)
    pairs = jax.ShapeDtypeStruct((2 * room,), jnp.int32)
    return pl.pallas_call(
        functools.partial(plan_kernel, room=room, blank=slots),
        out_shape=(pairs, pairs, pairs, jax.ShapeDtypeStruct((2,), jnp.int32)),
        in_specs=[spec(SMEM)] * 10,
        out_specs=tuple([spec(SMEM)] * 4),
        scratch_shapes=[pltpu.SMEM((32,), jnp.int32), pltpu.SMEM((33,), jnp.int32)],
        compiler_params=pltpu.CompilerParams(vmem_limit_bytes=MIB),
        cost_estimate=pl.CostEstimate(flops=10**9, bytes_accessed=10**6, transcendentals=0),
        name="plan_spread",
    )(*flat_args(owner_map, relations))


def spread_list(plan, offset, amount, messages, buffer, total, ready):
    pair_a, pair_b, pair_spot = plan

    def add_group(group, waited):
        at = offset + group * PAIRS
        waited = ready(waited, pair_b[at + PAIRS - 1] & 1023)
        products = []
        for lane in range(PAIRS):
            marks = (pair_a[at + lane], pair_b[at + lane])
            tile = jnp.concatenate([buffer[mark & 1023] for mark in marks], axis=0)
            block = jnp.concatenate([messages[mark >> 10] for mark in marks], axis=0)
            products.append(
                lax.dot_general(
                    tile, block, (((0,), (0,)), ((), ())), preferred_element_type=F32
                )
            )
        for lane in range(PAIRS):
            total[pair_spot[at + lane]] += products[lane]
        return waited

    return lax.fori_loop(0, (amount + PAIRS - 1) // PAIRS, add_group, jnp.int32(0))


def spread_early_kernel(
    pair_a, pair_b, pair_spot, amounts, counts0, counts1, counts2, tiles0, tiles1, tiles2,
    own0, own2, own3, own1, sib0,
    out, buffer, messages, total, tile_sems, piece_sem,
):
    tiles = (tiles0, tiles1, tiles2)
    copy = pltpu.make_async_copy(sib0, messages.at[pl.ds(48, 12)], piece_sem)
    copy.start()
    begins = start_tiles(tiles, (counts0, counts1, counts2), buffer, tile_sems)

    def place(block, carry):
        for piece, at in ((own0, 0), (own2, 8), (own3, 12), (own1, 4)):
            messages[at * 3 + block] = piece[block]
        return carry

    lax.fori_loop(0, 12, place, 0)
    buffer[buffer.shape[0] - 1] = jnp.zeros((TILE, TILE), BF16)
    clear(total, 16)
    copy.wait()

    def ready(waited, last):
        needed = jnp.minimum((last >> 4) + 1, begins[3])
        return wait_tiles(tiles0, buffer, tile_sems, waited, needed)

    waited = spread_list(
        (pair_a, pair_b, pair_spot), 0, amounts[0], messages, buffer, total, ready
    )
    wait_tiles(tiles0, buffer, tile_sems, waited, begins[3])

    def emit(block, carry):
        out[block] = total[block]
        return carry

    lax.fori_loop(0, 16, emit, 0)


def spread_late_kernel(
    pair_a, pair_b, pair_spot, amounts, buffer, before, sib2, sib3, sib1,
    out, messages, total,
):
    def place(block, carry):
        for piece, at in ((sib2, 4), (sib3, 8), (sib1, 0)):
            messages[at * 3 + block] = piece[block]
        return carry

    lax.fori_loop(0, 12, place, 0)

    def take(block, carry):
        total[block] = before[block]
        return carry

    lax.fori_loop(0, 16, take, 0)
    spread_list(
        (pair_a, pair_b, pair_spot),
        pair_a.shape[0] // 2,
        amounts[1],
        messages,
        buffer,
        total,
        lambda waited, last: waited,
    )

    def emit(block, carry):
        out[block] = total[block].astype(BF16)
        return carry

    lax.fori_loop(0, 16, emit, 0)


def spread_early(plan, relations, pieces):
    width = pieces[0].shape[-1]
    slots = sum(relation[0].shape[0] for relation in relations)
    whole, own2, own3, own1, beside = pieces
    return pl.pallas_call(
        spread_early_kernel,
        out_shape=(
            jax.ShapeDtypeStruct((16, TILE, width), F32),
            jax.ShapeDtypeStruct((slots + 1, TILE, TILE), BF16),
        ),
        in_specs=[spec(SMEM)] * 7
        + [spec(ANY)] * 3
        + [spec(VMEM)] * 4
        + [spec(ANY)],
        out_specs=(spec(VMEM), spec(VMEM)),
        scratch_shapes=[
            pltpu.VMEM((3 * EARLY, TILE, width), BF16),
            pltpu.VMEM((17, TILE, width), F32),
            pltpu.SemaphoreType.DMA((slots // GROUP,)),
            pltpu.SemaphoreType.DMA(()),
        ],
        compiler_params=pltpu.CompilerParams(vmem_limit_bytes=SPREAD_LIMIT),
        cost_estimate=pl.CostEstimate(
            flops=2 * 10**9, bytes_accessed=14 * 10**6, transcendentals=0
        ),
        name="spread_early",
    )(
        *plan,
        *[relation[3] for relation in relations],
        *tile_args(relations),
        whole, own2, own3, own1, in_hbm(beside),
    )


def spread_late(plan, early, pieces):
    before, buffer = early
    width = pieces[0].shape[-1]
    return pl.pallas_call(
        spread_late_kernel,
        out_shape=jax.ShapeDtypeStruct((16, TILE, width), BF16),
        in_specs=[spec(SMEM)] * 4 + [spec(VMEM)] * 5,
        out_specs=spec(VMEM),
        scratch_shapes=[
            pltpu.VMEM((3 * (32 - EARLY), TILE, width), BF16),
            pltpu.VMEM((17, TILE, width), F32),
        ],
        compiler_params=pltpu.CompilerParams(vmem_limit_bytes=SPREAD_LIMIT),
        cost_estimate=pl.CostEstimate(
            flops=10**9, bytes_accessed=4 * 10**6, transcendentals=0
        ),
        name="spread_late",
    )(*plan, buffer, before, *pieces)


def columns_at(step, width):
    column = (lax.axis_index("tgt") + step) % SIDE
    return pl.ds(pl.multiple_of(column * width, width), width)


def hidden_kernel(part0, part1, part2, part3, weights, rounded, terms0, terms1, terms2, terms3):
    width = part0.shape[1]
    whole = part0[...].astype(F32)
    for part in (part1, part2, part3):
        whole = whole + part[...].astype(F32)
    whole = whole.astype(BF16)
    rounded[...] = whole
    for step, terms in ((2, terms2), (1, terms1), (3, terms3), (0, terms0)):
        value = jnp.zeros(terms.shape, F32)
        for number in range(3):
            value += jnp.dot(
                whole[number * TILE:(number + 1) * TILE],
                weights[number, :, columns_at(step, width)],
                preferred_element_type=F32,
            )
        terms[...] = value.astype(terms.dtype)


def hidden_terms(parts, weights):
    width = parts[0].shape[1]
    return pl.pallas_call(
        hidden_kernel,
        out_shape=(
            jax.ShapeDtypeStruct((3 * TILE, width), BF16),
            jax.ShapeDtypeStruct((TILE, width), F32),
            jax.ShapeDtypeStruct((TILE, width), BF16),
            jax.ShapeDtypeStruct((TILE, width), BF16),
            jax.ShapeDtypeStruct((TILE, width), BF16),
        ),
        in_specs=[spec(VMEM)] * 5,
        out_specs=tuple([spec(VMEM)] * 5),
        compiler_params=pltpu.CompilerParams(vmem_limit_bytes=8 * MIB),
        name="hidden_terms",
    )(*parts, weights)


def message_kernel(grad0, grad1, grad2, grad3, weights, messages):
    width = grad0.shape[1]
    for number in range(3):
        value = jnp.zeros((TILE, width), F32)
        for step, grad in enumerate((grad0, grad1, grad2, grad3)):
            value += lax.dot_general(
                grad[...],
                weights[number, :, columns_at(step, width)],
                (((1,), (1,)), ((), ())),
                preferred_element_type=F32,
            )
        messages[number] = value.astype(BF16)


def form_messages(grads, weights):
    width = grads[0].shape[1]
    return pl.pallas_call(
        message_kernel,
        out_shape=jax.ShapeDtypeStruct((3, TILE, width), BF16),
        in_specs=[spec(VMEM)] * 5,
        out_specs=spec(VMEM),
        compiler_params=pltpu.CompilerParams(vmem_limit_bytes=8 * MIB),
        name="form_messages",
    )(*grads, weights)


def add_kernel(left, right, out):
    out[...] = (left[...].astype(F32) + right[...].astype(F32)).astype(BF16)


def add_blocks(left, right):
    return pl.pallas_call(
        add_kernel,
        out_shape=jax.ShapeDtypeStruct(left.shape, BF16),
        in_specs=[spec(VMEM)] * 2,
        out_specs=spec(VMEM),
        compiler_params=pltpu.CompilerParams(vmem_limit_bytes=8 * MIB),
        name="add_blocks",
    )(left, right)


def join_kernel(*refs):
    for number, ref in enumerate(refs[:-1]):
        refs[-1][pl.ds(number * ref.shape[0], ref.shape[0])] = ref[...]


def join(blocks):
    shape = (sum(block.shape[0] for block in blocks), *blocks[0].shape[1:])
    return pl.pallas_call(
        join_kernel,
        out_shape=jax.ShapeDtypeStruct(shape, BF16),
        in_specs=[spec(VMEM)] * len(blocks),
        out_specs=spec(VMEM),
        compiler_params=pltpu.CompilerParams(vmem_limit_bytes=8 * MIB),
        name="join_blocks",
    )(*blocks)


def weight_kernel(grad0, grad1, grad2, grad3, rounded, keep, send, staged, sems):
    mine = here()
    block0 = lax.axis_index("tgt")
    values = jnp.concatenate(
        [rounded[number * TILE:(number + 1) * TILE, :] for number in range(3)], axis=1
    )
    for step, grad in enumerate((grad0, grad1, grad2, grad3)):
        turned = grad[...].astype(F32).T.astype(BF16)
        block = (block0 + step) % SIDE
        for part in range(8):
            first, second, away = place_of(block * 8 + part, mine)
            spot = away * 16 + second * SIDE + first
            value = jnp.dot(
                turned[part * 32:(part + 1) * 32], values, preferred_element_type=F32
            ).astype(BF16)
            for column in range(values.shape[1] // TILE):
                staged[spot, pl.ds(column * 32, 32), :] = value[
                    :, column * TILE:(column + 1) * TILE
                ]
    copies = [
        pltpu.make_async_copy(staged.at[pl.ds(16, 16)], send, sems.at[0]),
        pltpu.make_async_copy(staged.at[pl.ds(0, 16)], keep, sems.at[1]),
    ]
    for copy in copies:
        copy.start()
    for copy in copies:
        copy.wait()


def weight_terms(grads, rounded):
    width = grads[0].shape[1]
    rows = 32 * 3 * width // TILE
    blocks = jax.ShapeDtypeStruct((16, rows, TILE), BF16)
    return pl.pallas_call(
        weight_kernel,
        out_shape=(blocks, blocks),
        in_specs=[spec(VMEM)] * 5,
        out_specs=(spec(ANY), spec(ANY)),
        scratch_shapes=[
            pltpu.VMEM((32, rows, TILE), BF16),
            pltpu.SemaphoreType.DMA((2,)),
        ],
        compiler_params=pltpu.CompilerParams(vmem_limit_bytes=8 * MIB),
        cost_estimate=pl.CostEstimate(flops=10**9, bytes_accessed=3 * 10**6, transcendentals=0),
        name="weight_terms",
    )(*grads, rounded)


def shift_pairs(step, second):
    pairs = []
    for s in range(32):
        x, z, c = s // 8, (s // 2) % 4, s % 2
        if (c == 0) != second:
            x = (x + step) % SIDE
        else:
            z = (z + step) % SIDE
        pairs.append((s, (x * SIDE + z) * 2 + c))
    return pairs


def shift(value, step, second=False):
    return lax.ppermute(value, "src", shift_pairs(step, second))


def swap(value):
    return lax.ppermute(value, "src", [(s, s ^ 1) for s in range(32)])


def add(*values):
    total = values[0].astype(F32)
    for value in values[1:]:
        total = total + value.astype(F32)
    return total.astype(BF16)


def three_starts(values, second=False):
    arrived = []
    for k in (2, 1, 3):
        arrived.append(shift(values[k], k if k < 3 else -1, second))
    return tuple(arrived)


def three_ways(values, second=False):
    return barrier(three_starts(values, second))


def turn(value, step):
    return lax.ppermute(value, "tgt", [(t, (t + step) % SIDE) for t in range(SIDE)])


def shards(
    features,
    cites_tiles,
    cites_targets,
    cites_sources,
    cites_counts,
    writes_tiles,
    writes_targets,
    writes_sources,
    writes_counts,
    topic_tiles,
    topic_targets,
    topic_sources,
    topic_counts,
    owner_map,
    weights,
    bias_row,
    cotangent,
):
    width = features.shape[1]
    relations = (
        (cites_tiles, cites_targets, cites_sources, cites_counts),
        (writes_tiles, writes_targets, writes_sources, writes_counts),
        (topic_tiles, topic_targets, topic_sources, topic_counts),
    )
    keep, send = gather_sums(owner_map, relations, features)
    got = swap(send)
    quarters = [add(keep[4 * k:4 * k + 4], got[4 * k:4 * k + 4]) for k in range(4)]
    owner_map, *quarters = barrier((owner_map, *quarters))
    arrived = three_ways(quarters)
    plan = plan_spread(owner_map, relations)
    *plan, a0, a1, a2 = barrier((*plan, *arrived))
    line = [add(quarters[0][k], *[part[k] for part in (a0, a1, a2)]) for k in range(4)]
    parts = (line[0], *three_ways(line, True))

    rounded, terms0, terms1, terms2, terms3 = hidden_terms(parts, weights)
    turned = barrier((turn(terms2, 2), turn(terms1, 1), turn(terms3, 3)))
    hidden = terms0 + bias_row.astype(F32)[None, :]
    for part in turned:
        hidden = hidden + part.astype(F32)
    mixed_out, pullback = jax.vjp(functools.partial(jax.nn.gelu, approximate=True), hidden)
    grad_hidden = pullback(cotangent.astype(F32))[0].astype(BF16)
    two, one, three = barrier(
        (turn(grad_hidden, -2), turn(grad_hidden, -1), turn(grad_hidden, -3))
    )
    grads = [grad_hidden, one, two, three]

    own = form_messages(grads, weights)
    own, *grads = barrier((own, *grads))
    weight_keep, weight_send = weight_terms(grads, rounded)
    weight_got = swap(weight_send)
    two, three, one = barrier(three_starts((own,) * 4))
    quarters = [
        add(weight_keep[4 * k:4 * k + 4], weight_got[4 * k:4 * k + 4]) for k in range(1, 4)
    ]
    quarters = [add_blocks(weight_keep[:4], weight_got[:4]), *quarters]
    arrived = barrier(three_starts(quarters, True))
    whole = join((own, one, two, three))
    spread_out = three_starts((whole,) * 4, True)
    beside = swap(whole)
    line = [add(quarters[0][k], *[part[k] for part in arrived]) for k in range(4)]
    weight_parts = three_ways(line)
    weight_sum = line[0].astype(F32)
    for part in weight_parts:
        weight_sum = weight_sum + part.astype(F32)
    grad_weight = weight_sum.reshape(3 * width // TILE, 32, TILE).transpose(0, 2, 1)
    grad_weight = grad_weight.reshape(3, width, 32)
    *spread_out, beside, grad_weight = barrier((*spread_out, beside, grad_weight))
    siblings = [swap(piece) for piece in spread_out]
    early = spread_early(plan, relations, [whole, *spread_out, beside])
    grad_source = spread_late(plan, early, siblings)
    return (
        mixed_out.astype(BF16),
        grad_weight,
        grad_source.reshape(-1, width),
    )


def solution(mesh):
    in_specs = (
        P("src", "tgt"),
        P("src", None, None),
        P("src"),
        P("src"),
        P("src"),
        P("src", None, None),
        P("src"),
        P("src"),
        P("src"),
        P("src", None, None),
        P("src"),
        P("src"),
        P("src"),
        P(),
        P(None, "tgt", None),
        P("tgt"),
        P("src", "tgt"),
    )
    out_specs = (P("src", "tgt"), P(None, "tgt", "src"), P("src", "tgt"))

    return jax.shard_map(shards, mesh=mesh, in_specs=in_specs, out_specs=out_specs, check_vma=False)
```

```python
import functools

import jax
import jax.numpy as jnp
from jax import lax
from jax.experimental import pallas as pl
from jax.experimental.pallas import tpu as pltpu
from jax.sharding import PartitionSpec as P


TILE = 128
SIDE = 4
GROUP = 16
BATCH = 32
PAIRS = 16
BF16 = jnp.bfloat16
F32 = jnp.float32
MIB = 1024 * 1024
GATHER_LIMIT = 36 * MIB
SPREAD_LIMIT = 12 * MIB
barrier = lax.optimization_barrier


def spec(space):
    return pl.BlockSpec(memory_space=space)


ANY, SMEM, VMEM = pl.ANY, pltpu.SMEM, pltpu.VMEM


def here():
    s = lax.axis_index("src")
    return s >> 3, (s >> 1) & 3, s & 1


def place_of(slot, mine):
    c = slot & 1
    dx = ((slot >> 3) - mine[0]) & 3
    dz = ((slot >> 1) - mine[1]) & 3
    first = jnp.where(c == 0, dx, dz)
    second = jnp.where(c == 0, dz, dx)
    return first, second, c ^ mine[2]


def live_parts(counts):
    parts = [(count[0] + GROUP - 1) // GROUP for count in counts]
    return parts, [0, parts[0], parts[0] + parts[1], parts[0] + parts[1] + parts[2]]


def start_tiles(tiles, counts, buffer, sems):
    parts, begins = live_parts(counts)
    for number in range(3):
        def step(part, carry, number=number):
            at = begins[number] + part
            pltpu.make_async_copy(
                tiles[number].at[pl.ds(part * GROUP, GROUP)],
                buffer.at[pl.ds(at * GROUP, GROUP)],
                sems.at[at],
            ).start()
            return carry

        lax.fori_loop(0, parts[number], step, 0)
    return begins


def wait_tiles(tile, buffer, sems, waited, needed):
    def step(at, carry):
        pltpu.make_async_copy(
            tile.at[pl.ds(0, GROUP)], buffer.at[pl.ds(at * GROUP, GROUP)], sems.at[at]
        ).wait()
        return carry

    lax.fori_loop(waited, needed, step, 0)
    return jnp.maximum(waited, needed)


def clear(total, amount, begin=0):
    def step(block, carry):
        total[block] = jnp.zeros(total.shape[1:], F32)
        return carry

    lax.fori_loop(begin, amount, step, 0)


def gather_list(codes, amount, features, buffer, total, ready):
    def add_group(group, waited):
        waited = ready(waited, codes[jnp.minimum(group * BATCH + BATCH, amount) - 1] & 1023)
        marks = [codes[group * BATCH + lane] for lane in range(BATCH)]
        products = [
            jnp.dot(
                buffer[mark & 1023], features[(mark >> 10) & 15], preferred_element_type=F32
            )
            for mark in marks
        ]
        for mark, product in zip(marks, products):
            total[mark >> 14] += product
        return waited

    return lax.fori_loop(0, (amount + BATCH - 1) // BATCH, add_group, jnp.int32(0))


def emit_blocks(total, target):
    def emit(spot, carry):
        for number in range(3):
            target[spot, pl.ds(number * TILE, TILE), :] = total[spot * 3 + number].astype(BF16)
        return carry

    lax.fori_loop(0, 16, emit, 0)


def gather_send_kernel(
    owner_map,
    targets0, targets1, targets2, sources0, sources1, sources2, counts0, counts1, counts2,
    features, tiles0, tiles1, tiles2,
    send, keep_codes, keep_amount, buffer, held,
    total, table, send_codes, tile_sems, feature_sem,
):
    targets, sources = (targets0, targets1, targets2), (sources0, sources1, sources2)
    counts, tiles = (counts0, counts1, counts2), (tiles0, tiles1, tiles2)
    feature_copy = pltpu.make_async_copy(features, held, feature_sem)
    feature_copy.start()
    begins = start_tiles(tiles, counts, buffer, tile_sems)
    mine = here()

    def fill(slot, carry):
        first, second, away = place_of(slot, mine)
        table[owner_map[slot]] = (first * SIDE + second) * 3 + away * 128
        total[slot] = jnp.zeros(total.shape[1:], F32)
        return carry

    lax.fori_loop(0, 32, fill, 0)
    clear(total, 48, 32)

    sent, kept = jnp.int32(0), jnp.int32(0)
    for number in range(3):
        def sort(group, carry, number=number):
            sent, kept = carry
            for lane in range(GROUP):
                j = group * GROUP + lane
                spot = table[targets[number][j]]
                code = (
                    (begins[number] * GROUP + j)
                    + sources[number][j] * 1024
                    + ((spot & 127) + number) * 16384
                )
                send_codes[sent] = code
                keep_codes[kept] = code
                live = jnp.where(j < counts[number][0], 1, 0)
                away = live & (spot >> 7)
                sent, kept = sent + away, kept + (live - away)
            return sent, kept

        sent, kept = lax.fori_loop(
            0, (counts[number][0] + GROUP - 1) // GROUP, sort, (sent, kept)
        )
    for lane in range(BATCH):
        send_codes[sent + lane] = 48 * 16384
        keep_codes[kept + lane] = 48 * 16384
    keep_amount[0] = kept
    feature_copy.wait()

    def ready(waited, last):
        return wait_tiles(tiles[0], buffer, tile_sems, waited, (last >> 4) + 1)

    waited = gather_list(send_codes, sent, held, buffer, total, ready)
    wait_tiles(tiles[0], buffer, tile_sems, waited, begins[3])
    emit_blocks(total, send)


def gather_keep_kernel(codes, amount, buffer, held, keep, total):
    clear(total, 48)
    gather_list(codes, amount[0], held, buffer, total, lambda waited, last: waited)
    emit_blocks(total, keep)


def in_hbm(value):
    return pltpu.with_memory_space_constraint(value, pltpu.HBM)


def flat_args(owner_map, relations):
    return (
        in_hbm(owner_map),
        *[in_hbm(relation[1]) for relation in relations],
        *[in_hbm(relation[2]) for relation in relations],
        *[relation[3] for relation in relations],
    )


def tile_args(relations):
    return [in_hbm(relation[0]) for relation in relations]


def gather_sums(owner_map, relations, features):
    width = features.shape[-1]
    slots = sum(relation[0].shape[0] for relation in relations)
    blocks = jax.ShapeDtypeStruct((16, 3 * TILE, width), BF16)
    features = features.reshape(-1, TILE, width)
    total = pltpu.VMEM((49, TILE, width), F32)
    common = dict(
        compiler_params=pltpu.CompilerParams(vmem_limit_bytes=GATHER_LIMIT),
        cost_estimate=pl.CostEstimate(
            flops=2 * 10**9, bytes_accessed=12 * 10**6, transcendentals=0
        ),
    )
    send, codes, amount, buffer, held = pl.pallas_call(
        gather_send_kernel,
        out_shape=(
            blocks,
            jax.ShapeDtypeStruct((slots + BATCH,), jnp.int32),
            jax.ShapeDtypeStruct((1,), jnp.int32),
            jax.ShapeDtypeStruct((slots, TILE, TILE), BF16),
            jax.ShapeDtypeStruct(features.shape, BF16),
        ),
        in_specs=[spec(SMEM)] * 10 + [spec(ANY)] * 4,
        out_specs=(spec(VMEM), spec(SMEM), spec(SMEM), spec(VMEM), spec(VMEM)),
        scratch_shapes=[
            total,
            pltpu.SMEM((32,), jnp.int32),
            pltpu.SMEM((slots + BATCH,), jnp.int32),
            pltpu.SemaphoreType.DMA((slots // GROUP,)),
            pltpu.SemaphoreType.DMA(()),
        ],
        name="gather_send",
        **common,
    )(*flat_args(owner_map, relations), in_hbm(features), *tile_args(relations))
    keep = pl.pallas_call(
        gather_keep_kernel,
        out_shape=blocks,
        in_specs=[spec(SMEM)] * 2 + [spec(VMEM)] * 2,
        out_specs=spec(VMEM),
        scratch_shapes=[total],
        name="gather_keep",
        **common,
    )(codes, amount, buffer, held)
    return keep, send


EARLY = 20


def plan_kernel(
    owner_map,
    targets0, targets1, targets2, sources0, sources1, sources2, counts0, counts1, counts2,
    pair_a, pair_b, pair_spot, amounts,
    table, pending,
    *, room, blank,
):
    targets, sources = (targets0, targets1, targets2), (sources0, sources1, sources2)
    counts = (counts0, counts1, counts2)
    begins = live_parts(counts)[1]
    mine = here()

    def fill(slot, carry):
        first, second, away = place_of(slot, mine)
        place = away * 16 + second * SIDE + first
        late = jnp.where(place >= EARLY, 1, 0)
        table[owner_map[slot]] = (place - late * EARLY) * 3 + late * 128
        pending[slot] = -1
        return carry

    lax.fori_loop(0, 32, fill, 0)
    pending[32] = -1

    def put(found, late, a, b, spot, yes):
        at = jnp.where(late == 1, room + found[1], found[0])
        pair_a[at] = a
        pair_b[at] = b
        pair_spot[at] = spot
        return found[0] + yes * (1 - late), found[1] + yes * late

    found = (jnp.int32(0), jnp.int32(0))
    for number in range(3):
        def match(group, found, number=number):
            for lane in range(GROUP):
                j = group * GROUP + lane
                live = j < counts[number][0]
                place = table[targets[number][j]]
                late = place >> 7
                source = sources[number][j]
                code = begins[number] * GROUP + j + ((place & 127) + number) * 1024
                spot = jnp.where(live, late * 16 + source, 32)
                waiting = pending[spot]
                hit = live & (waiting >= 0)
                found = put(found, late, waiting, code, source, jnp.where(hit, 1, 0))
                pending[spot] = jnp.where(hit, -1, code)
            return found

        found = lax.fori_loop(0, (counts[number][0] + GROUP - 1) // GROUP, match, found)

    def flush(spot, found):
        waiting = pending[spot]
        yes = jnp.where(waiting >= 0, 1, 0)
        return put(found, spot >> 4, waiting, blank, spot & 15, yes)

    found = lax.fori_loop(0, 32, flush, found)
    for late in range(2):
        for lane in range(PAIRS):
            pair_a[late * room + found[late] + lane] = blank
            pair_b[late * room + found[late] + lane] = blank
            pair_spot[late * room + found[late] + lane] = 16
        amounts[late] = found[late]


def pair_room(slots):
    return slots // 2 + 32 + PAIRS


def plan_spread(owner_map, relations):
    slots = sum(relation[0].shape[0] for relation in relations)
    room = pair_room(slots)
    pairs = jax.ShapeDtypeStruct((2 * room,), jnp.int32)
    return pl.pallas_call(
        functools.partial(plan_kernel, room=room, blank=slots),
        out_shape=(pairs, pairs, pairs, jax.ShapeDtypeStruct((2,), jnp.int32)),
        in_specs=[spec(SMEM)] * 10,
        out_specs=tuple([spec(SMEM)] * 4),
        scratch_shapes=[pltpu.SMEM((32,), jnp.int32), pltpu.SMEM((33,), jnp.int32)],
        compiler_params=pltpu.CompilerParams(vmem_limit_bytes=MIB),
        cost_estimate=pl.CostEstimate(flops=10**9, bytes_accessed=10**6, transcendentals=0),
        name="plan_spread",
    )(*flat_args(owner_map, relations))


def spread_list(plan, offset, amount, messages, buffer, total, ready):
    pair_a, pair_b, pair_spot = plan

    def add_group(group, waited):
        at = offset + group * PAIRS
        waited = ready(waited, pair_b[at + PAIRS - 1] & 1023)
        products = []
        for lane in range(PAIRS):
            marks = (pair_a[at + lane], pair_b[at + lane])
            tile = jnp.concatenate([buffer[mark & 1023] for mark in marks], axis=0)
            block = jnp.concatenate([messages[mark >> 10] for mark in marks], axis=0)
            products.append(
                lax.dot_general(
                    tile, block, (((0,), (0,)), ((), ())), preferred_element_type=F32
                )
            )
        for lane in range(PAIRS):
            total[pair_spot[at + lane]] += products[lane]
        return waited

    return lax.fori_loop(0, (amount + PAIRS - 1) // PAIRS, add_group, jnp.int32(0))


def spread_early_kernel(
    pair_a, pair_b, pair_spot, amounts, counts0, counts1, counts2, tiles0, tiles1, tiles2,
    own0, own2, own3, own1, sib0,
    out, buffer, messages, total, tile_sems, piece_sem,
):
    tiles = (tiles0, tiles1, tiles2)
    copy = pltpu.make_async_copy(sib0, messages.at[pl.ds(48, 12)], piece_sem)
    copy.start()
    begins = start_tiles(tiles, (counts0, counts1, counts2), buffer, tile_sems)

    def place(block, carry):
        for piece, at in ((own0, 0), (own2, 8), (own3, 12), (own1, 4)):
            messages[at * 3 + block] = piece[block]
        return carry

    lax.fori_loop(0, 12, place, 0)
    buffer[buffer.shape[0] - 1] = jnp.zeros((TILE, TILE), BF16)
    clear(total, 16)
    copy.wait()

    def ready(waited, last):
        needed = jnp.minimum((last >> 4) + 1, begins[3])
        return wait_tiles(tiles0, buffer, tile_sems, waited, needed)

    waited = spread_list(
        (pair_a, pair_b, pair_spot), 0, amounts[0], messages, buffer, total, ready
    )
    wait_tiles(tiles0, buffer, tile_sems, waited, begins[3])

    def emit(block, carry):
        out[block] = total[block]
        return carry

    lax.fori_loop(0, 16, emit, 0)


def spread_late_kernel(
    pair_a, pair_b, pair_spot, amounts, buffer, before, sib2, sib3, sib1,
    out, messages, total,
):
    def place(block, carry):
        for piece, at in ((sib2, 4), (sib3, 8), (sib1, 0)):
            messages[at * 3 + block] = piece[block]
        return carry

    lax.fori_loop(0, 12, place, 0)

    def take(block, carry):
        total[block] = before[block]
        return carry

    lax.fori_loop(0, 16, take, 0)
    spread_list(
        (pair_a, pair_b, pair_spot),
        pair_a.shape[0] // 2,
        amounts[1],
        messages,
        buffer,
        total,
        lambda waited, last: waited,
    )

    def emit(block, carry):
        out[block] = total[block].astype(BF16)
        return carry

    lax.fori_loop(0, 16, emit, 0)


def spread_early(plan, relations, pieces):
    width = pieces[0].shape[-1]
    slots = sum(relation[0].shape[0] for relation in relations)
    whole, own2, own3, own1, beside = pieces
    return pl.pallas_call(
        spread_early_kernel,
        out_shape=(
            jax.ShapeDtypeStruct((16, TILE, width), F32),
            jax.ShapeDtypeStruct((slots + 1, TILE, TILE), BF16),
        ),
        in_specs=[spec(SMEM)] * 7
        + [spec(ANY)] * 3
        + [spec(VMEM)] * 4
        + [spec(ANY)],
        out_specs=(spec(VMEM), spec(VMEM)),
        scratch_shapes=[
            pltpu.VMEM((3 * EARLY, TILE, width), BF16),
            pltpu.VMEM((17, TILE, width), F32),
            pltpu.SemaphoreType.DMA((slots // GROUP,)),
            pltpu.SemaphoreType.DMA(()),
        ],
        compiler_params=pltpu.CompilerParams(vmem_limit_bytes=SPREAD_LIMIT),
        cost_estimate=pl.CostEstimate(
            flops=2 * 10**9, bytes_accessed=14 * 10**6, transcendentals=0
        ),
        name="spread_early",
    )(
        *plan,
        *[relation[3] for relation in relations],
        *tile_args(relations),
        whole, own2, own3, own1, in_hbm(beside),
    )


def spread_late(plan, early, pieces):
    before, buffer = early
    width = pieces[0].shape[-1]
    return pl.pallas_call(
        spread_late_kernel,
        out_shape=jax.ShapeDtypeStruct((16, TILE, width), BF16),
        in_specs=[spec(SMEM)] * 4 + [spec(VMEM)] * 5,
        out_specs=spec(VMEM),
        scratch_shapes=[
            pltpu.VMEM((3 * (32 - EARLY), TILE, width), BF16),
            pltpu.VMEM((17, TILE, width), F32),
        ],
        compiler_params=pltpu.CompilerParams(vmem_limit_bytes=SPREAD_LIMIT),
        cost_estimate=pl.CostEstimate(
            flops=10**9, bytes_accessed=4 * 10**6, transcendentals=0
        ),
        name="spread_late",
    )(*plan, buffer, before, *pieces)


def columns_at(step, width):
    column = (lax.axis_index("tgt") + step) % SIDE
    return pl.ds(pl.multiple_of(column * width, width), width)


def hidden_kernel(part0, part1, part2, part3, weights, rounded, terms0, terms1, terms2, terms3):
    width = part0.shape[1]
    whole = part0[...].astype(F32)
    for part in (part1, part2, part3):
        whole = whole + part[...].astype(F32)
    whole = whole.astype(BF16)
    rounded[...] = whole
    for step, terms in ((2, terms2), (1, terms1), (3, terms3), (0, terms0)):
        value = jnp.zeros(terms.shape, F32)
        for number in range(3):
            value += jnp.dot(
                whole[number * TILE:(number + 1) * TILE],
                weights[number, :, columns_at(step, width)],
                preferred_element_type=F32,
            )
        terms[...] = value.astype(terms.dtype)


def hidden_terms(parts, weights):
    width = parts[0].shape[1]
    return pl.pallas_call(
        hidden_kernel,
        out_shape=(
            jax.ShapeDtypeStruct((3 * TILE, width), BF16),
            jax.ShapeDtypeStruct((TILE, width), F32),
            jax.ShapeDtypeStruct((TILE, width), BF16),
            jax.ShapeDtypeStruct((TILE, width), BF16),
            jax.ShapeDtypeStruct((TILE, width), BF16),
        ),
        in_specs=[spec(VMEM)] * 5,
        out_specs=tuple([spec(VMEM)] * 5),
        compiler_params=pltpu.CompilerParams(vmem_limit_bytes=8 * MIB),
        name="hidden_terms",
    )(*parts, weights)


def message_kernel(grad0, grad1, grad2, grad3, weights, messages):
    width = grad0.shape[1]
    for number in range(3):
        value = jnp.zeros((TILE, width), F32)
        for step, grad in enumerate((grad0, grad1, grad2, grad3)):
            value += lax.dot_general(
                grad[...],
                weights[number, :, columns_at(step, width)],
                (((1,), (1,)), ((), ())),
                preferred_element_type=F32,
            )
        messages[number] = value.astype(BF16)


def form_messages(grads, weights):
    width = grads[0].shape[1]
    return pl.pallas_call(
        message_kernel,
        out_shape=jax.ShapeDtypeStruct((3, TILE, width), BF16),
        in_specs=[spec(VMEM)] * 5,
        out_specs=spec(VMEM),
        compiler_params=pltpu.CompilerParams(vmem_limit_bytes=8 * MIB),
        name="form_messages",
    )(*grads, weights)


def add_kernel(left, right, out):
    out[...] = (left[...].astype(F32) + right[...].astype(F32)).astype(BF16)


def add_blocks(left, right):
    return pl.pallas_call(
        add_kernel,
        out_shape=jax.ShapeDtypeStruct(left.shape, BF16),
        in_specs=[spec(VMEM)] * 2,
        out_specs=spec(VMEM),
        compiler_params=pltpu.CompilerParams(vmem_limit_bytes=8 * MIB),
        name="add_blocks",
    )(left, right)


def join_kernel(*refs):
    for number, ref in enumerate(refs[:-1]):
        refs[-1][pl.ds(number * ref.shape[0], ref.shape[0])] = ref[...]


def join(blocks):
    shape = (sum(block.shape[0] for block in blocks), *blocks[0].shape[1:])
    return pl.pallas_call(
        join_kernel,
        out_shape=jax.ShapeDtypeStruct(shape, BF16),
        in_specs=[spec(VMEM)] * len(blocks),
        out_specs=spec(VMEM),
        compiler_params=pltpu.CompilerParams(vmem_limit_bytes=8 * MIB),
        name="join_blocks",
    )(*blocks)


def weight_kernel(grad0, grad1, grad2, grad3, rounded, keep, send, staged, sems):
    mine = here()
    block0 = lax.axis_index("tgt")
    values = jnp.concatenate(
        [rounded[number * TILE:(number + 1) * TILE, :] for number in range(3)], axis=1
    )
    for step, grad in enumerate((grad0, grad1, grad2, grad3)):
        turned = grad[...].astype(F32).T.astype(BF16)
        block = (block0 + step) % SIDE
        for part in range(8):
            first, second, away = place_of(block * 8 + part, mine)
            spot = away * 16 + second * SIDE + first
            value = jnp.dot(
                turned[part * 32:(part + 1) * 32], values, preferred_element_type=F32
            ).astype(BF16)
            for column in range(values.shape[1] // TILE):
                staged[spot, pl.ds(column * 32, 32), :] = value[
                    :, column * TILE:(column + 1) * TILE
                ]
    copies = [
        pltpu.make_async_copy(staged.at[pl.ds(16, 16)], send, sems.at[0]),
        pltpu.make_async_copy(staged.at[pl.ds(0, 16)], keep, sems.at[1]),
    ]
    for copy in copies:
        copy.start()
    for copy in copies:
        copy.wait()


def weight_terms(grads, rounded):
    width = grads[0].shape[1]
    rows = 32 * 3 * width // TILE
    blocks = jax.ShapeDtypeStruct((16, rows, TILE), BF16)
    return pl.pallas_call(
        weight_kernel,
        out_shape=(blocks, blocks),
        in_specs=[spec(VMEM)] * 5,
        out_specs=(spec(ANY), spec(ANY)),
        scratch_shapes=[
            pltpu.VMEM((32, rows, TILE), BF16),
            pltpu.SemaphoreType.DMA((2,)),
        ],
        compiler_params=pltpu.CompilerParams(vmem_limit_bytes=8 * MIB),
        cost_estimate=pl.CostEstimate(flops=10**9, bytes_accessed=3 * 10**6, transcendentals=0),
        name="weight_terms",
    )(*grads, rounded)


def shift_pairs(step, second):
    pairs = []
    for s in range(32):
        x, z, c = s // 8, (s // 2) % 4, s % 2
        if (c == 0) != second:
            x = (x + step) % SIDE
        else:
            z = (z + step) % SIDE
        pairs.append((s, (x * SIDE + z) * 2 + c))
    return pairs


def shift(value, step, second=False):
    return lax.ppermute(value, "src", shift_pairs(step, second))


def swap(value):
    return lax.ppermute(value, "src", [(s, s ^ 1) for s in range(32)])


def add(*values):
    total = values[0].astype(F32)
    for value in values[1:]:
        total = total + value.astype(F32)
    return total.astype(BF16)


def three_starts(values, second=False):
    arrived = []
    for k in (2, 1, 3):
        arrived.append(shift(values[k], k if k < 3 else -1, second))
    return tuple(arrived)


def three_ways(values, second=False):
    return barrier(three_starts(values, second))


def turn(value, step):
    return lax.ppermute(value, "tgt", [(t, (t + step) % SIDE) for t in range(SIDE)])


def shards(
    features,
    cites_tiles,
    cites_targets,
    cites_sources,
    cites_counts,
    writes_tiles,
    writes_targets,
    writes_sources,
    writes_counts,
    topic_tiles,
    topic_targets,
    topic_sources,
    topic_counts,
    owner_map,
    weights,
    bias_row,
    cotangent,
):
    width = features.shape[1]
    relations = (
        (cites_tiles, cites_targets, cites_sources, cites_counts),
        (writes_tiles, writes_targets, writes_sources, writes_counts),
        (topic_tiles, topic_targets, topic_sources, topic_counts),
    )
    keep, send = gather_sums(owner_map, relations, features)
    got = swap(send)
    quarters = [add(keep[4 * k:4 * k + 4], got[4 * k:4 * k + 4]) for k in range(4)]
    owner_map, *quarters = barrier((owner_map, *quarters))
    arrived = three_ways(quarters)
    plan = plan_spread(owner_map, relations)
    *plan, a0, a1, a2 = barrier((*plan, *arrived))
    line = [add(quarters[0][k], *[part[k] for part in (a0, a1, a2)]) for k in range(4)]
    parts = (line[0], *three_ways(line, True))

    rounded, terms0, terms1, terms2, terms3 = hidden_terms(parts, weights)
    turned = barrier((turn(terms2, 2), turn(terms1, 1), turn(terms3, 3)))
    hidden = terms0 + bias_row.astype(F32)[None, :]
    for part in turned:
        hidden = hidden + part.astype(F32)
    mixed_out, pullback = jax.vjp(functools.partial(jax.nn.gelu, approximate=True), hidden)
    grad_hidden = pullback(cotangent.astype(F32))[0].astype(BF16)
    two, one, three = barrier(
        (turn(grad_hidden, -2), turn(grad_hidden, -1), turn(grad_hidden, -3))
    )
    grads = [grad_hidden, one, two, three]

    own = form_messages(grads, weights)
    own, *grads = barrier((own, *grads))
    weight_keep, weight_send = weight_terms(grads, rounded)
    weight_got = swap(weight_send)
    two, three, one = barrier(three_starts((own,) * 4))
    quarters = [
        add(weight_keep[4 * k:4 * k + 4], weight_got[4 * k:4 * k + 4]) for k in range(1, 4)
    ]
    quarters = [add_blocks(weight_keep[:4], weight_got[:4]), *quarters]
    arrived = barrier(three_starts(quarters, True))
    whole = join((own, one, two, three))
    spread_out = three_starts((whole,) * 4, True)
    beside = swap(whole)
    line = [add(quarters[0][k], *[part[k] for part in arrived]) for k in range(4)]
    weight_parts = three_ways(line)
    weight_sum = line[0].astype(F32)
    for part in weight_parts:
        weight_sum = weight_sum + part.astype(F32)
    grad_weight = weight_sum.reshape(3 * width // TILE, 32, TILE).transpose(0, 2, 1)
    grad_weight = grad_weight.reshape(3, width, 32)
    *spread_out, beside, grad_weight = barrier((*spread_out, beside, grad_weight))
    siblings = [swap(piece) for piece in spread_out]
    early = spread_early(plan, relations, [whole, *spread_out, beside])
    grad_source = spread_late(plan, early, siblings)
    return (
        mixed_out.astype(BF16),
        grad_weight,
        grad_source.reshape(-1, width),
    )


def solution(mesh):
    in_specs = (
        P("src", "tgt"),
        P("src", None, None),
        P("src"),
        P("src"),
        P("src"),
        P("src", None, None),
        P("src"),
        P("src"),
        P("src"),
        P("src", None, None),
        P("src"),
        P("src"),
        P("src"),
        P(),
        P(None, "tgt", None),
        P("tgt"),
        P("src", "tgt"),
    )
    out_specs = (P("src", "tgt"), P(None, "tgt", "src"), P("src", "tgt"))

    return jax.shard_map(shards, mesh=mesh, in_specs=in_specs, out_specs=out_specs, check_vma=False)
```
